32 devices in a mesh: ctx: 16 (over z, x, core), fsdp: 2 (over y).
Axes of the slice: x: 2, y: 2, z: 4, core: 2. Of those that a mesh axis runs over, the one named last changes fastest.
Arguments:
- hidden_in: bfloat16 [2, 2048, 1024], P('fsdp', 'ctx'), may hold values from -6 to 6
- out_grad: bfloat16 [2, 2048, 1024], P('fsdp', 'ctx'), may hold values from -6 to 6
- doc_lengths: int32 [2, 16], P('fsdp'), may hold values from 1 to 512, 2048 in all within a row
- block_order: int32 [2, 32], P('fsdp'), may hold values from 0 to 31, as said below
- routes: int32 [2, 2048, 8], P('fsdp', 'ctx'), may hold values from 0 to 15, all different within a row
- attn_norm: bfloat16 [1024], P(('ctx', 'fsdp')), may hold values from 0.5 to 1.5
- w_query: bfloat16 [1024, 1024], P(('ctx', 'fsdp')), may hold values from -0.625 to 0.625
- w_key: bfloat16 [1024, 512], P(('ctx', 'fsdp')), may hold values from -0.625 to 0.625
- w_value: bfloat16 [1024, 512], P(('ctx', 'fsdp')), may hold values from -0.1875 to 0.1875
- w_output: bfloat16 [1024, 1024], P(('ctx', 'fsdp')), may hold values from -3 to 3
- ffn_norm: bfloat16 [1024], P(('ctx', 'fsdp')), may hold values from 0.5 to 1.5
- w_router: bfloat16 [1024, 16], P(('ctx', 'fsdp')), may hold values from -0.09375 to 0.09375
- w_gate_up: bfloat16 [1024, 16384], P(('ctx', 'fsdp')), may hold values from -0.1875 to 0.1875
- w_down: bfloat16 [1024, 8192], P(('ctx', 'fsdp')), may hold values from -4 to 4
Outputs:
- hidden_out: bfloat16 [2, 2048, 1024], P('fsdp', 'ctx')
- grad_in: float32 [2, 2048, 1024], P('fsdp', 'ctx')
- grad_attn_norm: float32 [1024], P(('ctx', 'fsdp'))
- grad_query: float32 [1024, 1024], P(('ctx', 'fsdp'))
- grad_key: float32 [1024, 512], P(('ctx', 'fsdp'))
- grad_value: float32 [1024, 512], P(('ctx', 'fsdp'))
- grad_output: float32 [1024, 1024], P(('ctx', 'fsdp'))
- grad_ffn_norm: float32 [1024], P(('ctx', 'fsdp'))
- grad_router: float32 [1024, 16], P(('ctx', 'fsdp'))
- grad_gate_up: float32 [1024, 16384], P(('ctx', 'fsdp'))
- grad_down: float32 [1024, 8192], P(('ctx', 'fsdp'))
The draws below stay inside these ranges and needn't reach their ends.
Inputs may be any that keep to these rules, and one draw needn't show every extreme that they name: `block_order`: in each sequence, storage blocks 2 c and 2 c + 1 (those of ctx index c) hold the sequence blocks p and 31 - p, in either order; every sequence block is held once. `doc_lengths`: each row sums to 2048; the longest document has exactly 512 tokens. `routes`: each token names 8 different experts; every expert is named by some token.
All inputs are finite; a program needn't handle non-finite values.
Results may differ from the reference program's by a relative error of at most 0.017.
Values may be sent and summed in bfloat16 or wider, within the bound.
No kernel may reach another device: no remote copies, remote signals or barrier semaphores. Data moves between devices by JAX's collectives and lax.ppermute only.
A program may use at most 320 MiB of HBM per device.

```python
import math
import jax
import jax.numpy as jnp
import numpy as np
from jax import lax

D = 1024
H = 16
KVH = 8
HD = 64
F = 512
TOP = 8
E = 16
DOCS = 16
SEQ = 2048
SEQS = 2
BLOCKS = 32
BLOCK_LEN = 64


def draw_block_order(key, part):
    seq_keys = jax.random.split(key, SEQS)

    def one_sequence(seq_key):
        perm_key, flip_key = jax.random.split(seq_key)
        pair_ids = jax.random.permutation(perm_key, BLOCKS // 2)
        flipped = jax.random.randint(flip_key, (BLOCKS // 2,), 0, 2)
        first_block = jnp.where(flipped == 1, BLOCKS - 1 - pair_ids, pair_ids)
        return jnp.stack([first_block, BLOCKS - 1 - first_block], axis=1).reshape(BLOCKS)
    return jax.vmap(one_sequence)(seq_keys).astype(jnp.int32)


def block_levels(key, shape, cuts, low, top_value):
    gain, own = 1.0, jax.random.fold_in(key, 6)
    for dim, shards_of in cuts:
        steps = jnp.exp(jax.random.uniform(jax.random.fold_in(own, dim), (shards_of,), jnp.float32, low / len(cuts), top_value / len(cuts)))
        gain = gain * jnp.repeat(steps, shape[dim] // shards_of).reshape([-1 if axis == dim else 1 for axis in range(len(shape))])
    return gain


def different_ones(own_key, rows, number_of, top, lift):
    sequence = jax.random.permutation(jax.random.fold_in(own_key, 1), number_of)
    pull = sequence
    for power in range(3):
        pull = pull * pull // number_of
    pull = pull * lift // number_of
    tickets = jax.random.randint(jax.random.fold_in(own_key, 2), (rows, number_of), 0, 4096) + pull
    fixed_rows = jax.random.permutation(jax.random.fold_in(own_key, 3), rows)[jnp.arange(number_of) % rows]
    tickets = jnp.where(jnp.arange(rows)[:, None] == fixed_rows[None, :], 1 << 14, tickets)
    merit = tickets * number_of + jnp.arange(number_of)
    return lax.top_k(merit.astype(jnp.int32), top)[1].astype(jnp.int32)


def profile(count, total, bound, slope):
    weights = [(1 << 20) // math.isqrt(grade ** slope) + 1 for grade in range(2, count + 1)]
    spare, holding = total - bound - (count - 1), [1] * (count - 1)
    while spare > 0:
        candidates = [i for i in range(count - 1) if holding[i] < bound]
        mass, budget = sum([weights[i] for i in candidates]), spare
        for i in candidates:
            addition = min(bound - holding[i], max(1, budget * weights[i] // mass), spare)
            holding[i] = holding[i] + addition
            spare = spare - addition
    return np.array([bound] + holding)


def ragged_sizes(rng, amount, total, reach, lean):
    if amount == 2:
        one = jax.random.randint(rng, (), max(1, total - reach), min(reach, total - 1) + 1)
        return jnp.stack([one, total - one])
    sizes = jnp.asarray(profile(amount, total, reach, lean), jnp.int32)
    couples = (amount - 1) // 2
    giver, taker = sizes[1:1 + 2 * couples:2], sizes[2:2 + 2 * couples:2]
    room = jnp.minimum(giver - 1, reach - taker)
    passed = jax.random.randint(jax.random.fold_in(rng, 1), (couples,), 0, 1 << 20) % (room + 1)
    sizes = sizes.at[1:1 + 2 * couples:2].set(giver - passed).at[2:2 + 2 * couples:2].set(taker + passed)
    return sizes[jax.random.permutation(jax.random.fold_in(rng, 2), amount)]


def noise(own_key, dims, spread, most, pieces=(), held_as=jnp.bfloat16):
    drawn = spread * jax.random.normal(own_key, dims, jnp.float32)
    if pieces:
        drawn = drawn * block_levels(own_key, dims, pieces, -0.22, 0.18)
    return jnp.clip(drawn, -most, most).astype(held_as)


def setup_inputs(seed: int = 0) -> dict:
    key_list = jax.random.split(jax.random.key(seed), 15)
    return {
        "hidden_in": noise(key_list[0], (SEQS, SEQ, D), 1.0, 6.0, ((0, 2), (1, 16))),
        "out_grad": noise(key_list[1], (SEQS, SEQ, D), 1.0, 6.0, ((0, 2), (1, 16))),
        "doc_lengths": jax.vmap(lambda own: ragged_sizes(own, DOCS, SEQ, SEQ // 4, 2))(jax.random.split(key_list[2], SEQS)).reshape((SEQS, DOCS)).astype(jnp.int32),
        "block_order": draw_block_order(jax.random.fold_in(key_list[14], 71), 0),
        "routes": different_ones(key_list[4], SEQS * SEQ, E, TOP, 4096).reshape((SEQS, SEQ, TOP)),
        "attn_norm": jnp.clip(1.0 + 0.1 * jax.random.normal(key_list[5], (D,), jnp.float32), 0.5, 1.5).astype(jnp.bfloat16),
        "w_query": noise(key_list[6], (D, H * HD), (D // 12) ** -0.5, 0.625, ((0, 32),)),
        "w_key": noise(key_list[7], (D, KVH * HD), (D // 12) ** -0.5, 0.625, ((0, 32),)),
        "w_value": noise(key_list[8], (D, KVH * HD), D ** -0.5, 0.1875, ((0, 32),)),
        "w_output": noise(key_list[9], (H * HD, D), (HD // 16) ** -0.5, 3.0, ((0, 32),)),
        "ffn_norm": jnp.clip(1.0 + 0.1 * jax.random.normal(key_list[10], (D,), jnp.float32), 0.5, 1.5).astype(jnp.bfloat16),
        "w_router": noise(key_list[11], (D, E), (4 * D) ** -0.5, 0.09375, ((0, 32),)),
        "w_gate_up": noise(key_list[12], (D, E * 2 * F), D ** -0.5, 0.1875, ((0, 32),)),
        "w_down": noise(key_list[13], (D, E * F), 2 ** -0.5, 4.0, ((0, 32),)),
    }


@jax.custom_vjp
def low(v):
    return lax.optimization_barrier(v.astype(jnp.bfloat16)).astype(jnp.float32)

@jax.custom_vjp
def low_back(v):
    return v

def low_keep(v):
    return (low(v), None)

def low_pass(kept, grad):
    return (grad,)

def back_keep(v):
    return (v, None)

def back_low(kept, grad):
    return (low(grad),)
low.defvjp(low_keep, low_pass)
low_back.defvjp(back_keep, back_low)
EPSILON = 1e-06
SCORE_SCALE = 0.015625
RESIDUAL_SCALE = 0.22
THETA = 10000.0
NEGATIVE = -1e+30
HIGHEST = lax.Precision.HIGHEST

def rms_norm(values, gain_vec):
    return values * lax.rsqrt(lax.optimization_barrier(jnp.mean(values * values, axis=-1, keepdims=True)) + EPSILON) * gain_vec

def rotate(values, places):
    half_width = values.shape[-1] // 2
    frequency = THETA ** (-jnp.arange(half_width, dtype=jnp.float32) / half_width)
    angles = places.astype(jnp.float32)[:, None] * frequency[None, :]
    cosine = jnp.cos(angles)[:, None, :]
    sine = jnp.sin(angles)[:, None, :]
    first_half = values[..., :half_width]
    second_half = values[..., half_width:]
    return jnp.concatenate([first_half * cosine - second_half * sine, second_half * cosine + first_half * sine], axis=-1)

def attend_block(block_item, keys, values, places):
    query_blk, place_blk, start_blk = block_item
    raw_scores = jnp.einsum('qhgd,khd->hgqk', query_blk, keys, precision=HIGHEST)
    scores = low_back(raw_scores) * SCORE_SCALE
    visible = (places[None, :] <= place_blk[:, None]) & (places[None, :] >= start_blk[:, None])
    scores = jnp.where(visible[None, None], scores, NEGATIVE)
    row_top = lax.optimization_barrier(jnp.max(scores, axis=-1, keepdims=True))
    log_total = row_top + jnp.log(lax.optimization_barrier(jnp.sum(jnp.exp(scores - row_top), axis=-1, keepdims=True)))
    attn_weights = low(jnp.exp(scores - log_total))
    return jnp.einsum('hgqk,khd->qhgd', attn_weights, values, precision=HIGHEST)

def layer_forward(hidden, params, places, doc_start, route_ids):
    attn_norm, w_query, w_key, w_value, w_output, ffn_norm, w_router, w_gate_up, w_down = params
    seq_len = hidden.shape[0]
    groups = H // KVH
    normed = low(rms_norm(hidden, attn_norm))
    queries = low(rotate(low_back(jnp.dot(normed, w_query, precision=HIGHEST)).reshape(seq_len, H, HD), places))
    keys = low(rotate(low_back(jnp.dot(normed, w_key, precision=HIGHEST)).reshape(seq_len, KVH, HD), places))
    values = low(low_back(jnp.dot(normed, w_value, precision=HIGHEST))).reshape(seq_len, KVH, HD)
    query_len = min(512, seq_len)
    count_q = seq_len // query_len

    def attend(block_item):
        return attend_block(block_item, keys, values, places)
    attended = lax.map(jax.checkpoint(attend), (queries.reshape(count_q, query_len, KVH, groups, HD), places.reshape(count_q, query_len), doc_start.reshape(count_q, query_len)))
    attended = low_back(low(attended.reshape(seq_len, H * HD)))
    middle = hidden + RESIDUAL_SCALE * low_back(jnp.dot(attended, w_output, precision=HIGHEST))
    mixed_in = low(rms_norm(middle, ffn_norm))
    logits = low_back(jnp.dot(mixed_in, w_router, precision=HIGHEST))
    onehot = (route_ids[:, :, None] == jnp.arange(E, dtype=jnp.int32)[None, None, :]).astype(jnp.float32)
    chosen = jnp.einsum('tke,te->tk', onehot, logits, precision=HIGHEST)
    gate_probs = jax.nn.softmax(chosen, axis=-1)
    combine = jnp.einsum('tk,tke->te', gate_probs, onehot, precision=HIGHEST)
    gate_up3 = w_gate_up.reshape(D, E, 2 * F)
    down3 = w_down.reshape(D, E, F)

    def experts(block_item):
        mixed_blk, combine_blk = block_item
        gate_up_val = low_back(jnp.einsum('td,def->tef', mixed_blk, gate_up3, precision=HIGHEST))
        activation = low(jax.nn.silu(gate_up_val[..., :F]) * gate_up_val[..., F:])
        expert_out = low_back(jnp.einsum('tef,def->ted', activation, down3, precision=HIGHEST))
        return jnp.einsum('te,ted->td', combine_blk, expert_out, precision=HIGHEST)
    token_len = min(1024, seq_len)
    count_t = seq_len // token_len
    moe_out = lax.map(jax.checkpoint(experts), (mixed_in.reshape(count_t, token_len, D), combine.reshape(count_t, token_len, E))).reshape(seq_len, D)
    return middle + RESIDUAL_SCALE * moe_out

def reference(hidden_in, out_grad, doc_lengths, block_order, routes, attn_norm, w_query, w_key, w_value, w_output, ffn_norm, w_router, w_gate_up, w_down):
    params = tuple((weight_arr.astype(jnp.float32) for weight_arr in (attn_norm, w_query, w_key, w_value, w_output, ffn_norm, w_router, w_gate_up, w_down)))
    outputs = []
    input_grads = []
    param_grads = tuple((jnp.zeros(weight_arr.shape, jnp.float32) for weight_arr in params))
    for seq_id in range(SEQS):
        places = (block_order[seq_id][:, None] * BLOCK_LEN + jnp.arange(BLOCK_LEN, dtype=jnp.int32)[None, :]).reshape(SEQ).astype(jnp.int32)
        lengths = doc_lengths[seq_id]
        doc_first = (jnp.cumsum(lengths) - lengths).astype(jnp.int32)
        doc_start = lax.optimization_barrier(jnp.max(jnp.where(doc_first[None, :] <= places[:, None], doc_first[None, :], 0), axis=1)).astype(jnp.int32)
        route_ids = routes[seq_id]

        def forward(hidden, weights):
            return layer_forward(hidden, weights, places, doc_start, route_ids)
        result, pullback = jax.vjp(forward, hidden_in[seq_id].astype(jnp.float32), params)
        grad_hidden, grad_params = pullback(out_grad[seq_id].astype(jnp.float32))
        outputs.append(result.astype(jnp.bfloat16))
        input_grads.append(grad_hidden)
        param_grads = jax.tree.map(lambda total_g, new_g: total_g + new_g, param_grads, grad_params)
    return (jnp.stack(outputs), jnp.stack(input_grads), param_grads[0], param_grads[1], param_grads[2], param_grads[3], param_grads[4], param_grads[5], param_grads[6], param_grads[7], param_grads[8])
```

```python
import functools

import jax
import jax.numpy as jnp
import numpy as np
from jax import lax
from jax.experimental import pallas as pl
from jax.experimental.pallas import tpu as pltpu
from jax.sharding import PartitionSpec as P

D = 1024
H = 16
KVH = 8
HD = 64
F = 512
E = 16

EPSILON = 1e-06
SCORE_SCALE = 0.015625
RESIDUAL_SCALE = 0.22
THETA = 10000.0
NEGATIVE = -1e30
BOTH = ("ctx", "fsdp")
BF = jnp.bfloat16
F32 = jnp.float32
QUERY_BLOCK = 256


def dot(left, right, left_dim, right_dim):
    return lax.dot_general(
        left, right, (((left_dim,), (right_dim,)), ((), ())), preferred_element_type=F32
    )


def permute(values, pairs):
    return lax.ppermute(values, "ctx", pairs)


def shift_z(step):
    return [(i, ((i // 4 + step) % 4) * 4 + i % 4) for i in range(16)]


SWAP_X = [(i, i ^ 2) for i in range(16)]
SWAP_CORE = [(i, i ^ 1) for i in range(16)]


def after(value, *others):
    return lax.optimization_barrier((value, *others))[0] if others else lax.optimization_barrier(value)


def block_order_of(count):
    index = jnp.arange(count, dtype=jnp.int32)
    if lax.axis_size("ctx") != 16:
        return index
    place = lax.axis_index("ctx")
    z_of = (place // 4 - (index % 8) // 2 + 4) % 4
    x_of = ((place // 2) % 2 + index % 2) % 2
    return z_of * 4 + x_of * 2 + (place % 2 + index // 8) % 2


class RingSum:
    def __init__(self, mine, arrived):
        self.mine, self.arrived = mine, arrived
        self.count = mine.shape[0] // 8
        self.cross_out = jnp.concatenate([self.chip(k, 1) for k in (2, 1, 3)], 0).astype(BF)

    def chip(self, k, dx):
        rows = slice((2 * k + dx) * self.count, (2 * k + dx + 1) * self.count)
        return self.mine[rows].astype(F32) + self.arrived[rows].astype(F32)

    def cross(self):
        got = permute(self.cross_out, SWAP_X)
        self.sends = []
        for j, k in enumerate((2, 1, 3)):
            term = got[j * self.count : (j + 1) * self.count].astype(F32)
            self.sends.append((self.chip(k, 0) + term).astype(BF))

    def end(self, *others):
        self.own = permute(self.chip(0, 1).astype(BF), SWAP_X)
        total = self.chip(0, 0) + self.own.astype(F32)
        for send, k in zip(self.sends, (2, 1, 3)):
            term = permute(send, shift_z(4 - k))
            if k == 2 and others:
                term = after(term, *others)
            total = total + term.astype(F32)
        return total


def join_kernel(places, *refs):
    pieces, out_ref, sems = refs[:14], refs[14], refs[15]
    count = out_ref.shape[1]
    copies = []
    for side in range(2):
        own, far, one, pair, two, far_two, three = pieces[7 * side : 7 * side + 7]
        lower, upper = pair.at[:count], pair.at[count:]
        for j, piece in enumerate((own, far, one, lower, two, far_two, three, upper)):
            block = 8 * side + j
            copies.append(
                pltpu.make_async_copy(piece, out_ref.at[places[block]], sems.at[block])
            )
    for copy in copies:
        copy.start()
    for copy in copies:
        copy.wait()


class Gather:
    def __init__(self, rows):
        self.count = rows.shape[0]
        self.own = rows
        self.one = permute(rows, shift_z(1))
        self.three = permute(rows, shift_z(3))
        self.far = permute(rows, SWAP_X)
        self.two = permute(rows, shift_z(2))

    def cross(self, *others):
        if others:
            self.one, self.three = after((self.one, self.three), *others)
        self.pair = permute(jnp.concatenate([self.one, self.three], 0), SWAP_X)

    def last(self, *others):
        if others:
            self.two = after(self.two, *others)
        self.far_two = permute(self.two, SWAP_X)

    def join(self, places, name, *others):
        if others:
            self.far, self.far_two = after((self.far, self.far_two), *others)
        mine = (self.own, self.far, self.one, self.pair, self.two, self.far_two, self.three)
        other = tuple(permute(piece, SWAP_CORE) for piece in mine)
        shape = (16, *self.own.shape)
        return pl.pallas_call(
            join_kernel,
            out_shape=jax.ShapeDtypeStruct(shape, BF),
            grid_spec=pltpu.PrefetchScalarGridSpec(
                num_scalar_prefetch=1,
                grid=(1,),
                in_specs=[fixed(piece.shape) for piece in (*mine, *other)],
                out_specs=pl.BlockSpec(memory_space=pl.ANY),
                scratch_shapes=[pltpu.SemaphoreType.DMA((16,))],
            ),
            compiler_params=params(),
            cost_estimate=cost(1, 4 * self.own.size * 16),
            name=name,
        )(places, *mine, *other)


def tables_of(total):
    half_width = HD // 2
    frequency = (THETA ** (-np.arange(half_width) / half_width)).astype(np.float32)
    angles = np.arange(total, dtype=np.float32)[:, None] * frequency[None, :]
    cosine = np.cos(angles.astype(np.float64)).astype(np.float32)
    sine = np.sin(angles.astype(np.float64)).astype(np.float32)
    return jnp.asarray(np.tile(cosine, (1, 4))), jnp.asarray(np.tile(sine, (1, 4)))


def window_of(step, band):
    start = jnp.maximum(step * QUERY_BLOCK - band, 0)
    return pl.multiple_of(start, QUERY_BLOCK), pl.multiple_of(step * QUERY_BLOCK, QUERY_BLOCK)


def masked_scores(queries, keys_win, first_key, first_query, firsts):
    raw = dot(queries, keys_win, 1, 1) * SCORE_SCALE
    key_place = first_key + lax.broadcasted_iota(jnp.int32, raw.shape, 1)
    query_place = first_query + lax.broadcasted_iota(jnp.int32, raw.shape, 0)
    column = first_query + lax.broadcasted_iota(jnp.int32, (raw.shape[0], 1), 0)
    start = jnp.zeros_like(column)
    for j in range(1, firsts.shape[0]):
        start = jnp.where(firsts[j] <= column, jnp.maximum(start, firsts[j]), start)
    visible = (key_place <= query_place) & (key_place >= start)
    return jnp.where(visible, raw, NEGATIVE)


def lanes_of(values):
    return lax.broadcasted_iota(jnp.int32, values.shape, 1)


def fixed(shape, at=None):
    place = (0,) * len(shape) if at is None else at
    return pl.BlockSpec(shape, lambda *_: place, pipeline_mode=pl.Buffered(1))


def params(mib=56):
    return pltpu.CompilerParams(vmem_limit_bytes=mib * 2**20)


def cost(flops, bytes_accessed, transcendentals=0, weight=20):
    return pl.CostEstimate(
        flops=weight * flops,
        bytes_accessed=weight * bytes_accessed,
        transcendentals=transcendentals,
    )


def column_of(row_ref):
    return jnp.broadcast_to(row_ref[:1, :], (128, row_ref.shape[1])).T


def pack_kernel(copies, wq_ref, wk_ref, wv_ref, wr_ref, norm_ref, small_ref):
    rows = wq_ref.shape[0]
    rest = jnp.concatenate(
        [wr_ref[...], norm_ref[...], jnp.zeros((rows, HD - E - 2), BF)], axis=1
    )
    for place in range(E * copies):
        head = place // copies
        pair = head // (H // KVH)
        query = wq_ref[:, head * HD : (head + 1) * HD]
        key = wk_ref[:, pair * HD : (pair + 1) * HD]
        value = wv_ref[:, pair * HD : (pair + 1) * HD]
        small_ref[place] = jnp.concatenate([query, key, value, rest], axis=1)


def pack_small(copies, *weights):
    shape = (E * copies, weights[0].shape[0], 256)
    return pl.pallas_call(
        functools.partial(pack_kernel, copies),
        out_shape=jax.ShapeDtypeStruct(shape, BF),
        grid=(1,),
        in_specs=[fixed(weight.shape) for weight in weights],
        out_specs=fixed(shape),
        compiler_params=params(),
        cost_estimate=cost(1, 2**20),
        name="pack_small",
    )(*weights)


def split_kernel(small_ref, ext_ref, head_ref, router_ref, one_ref, two_ref):
    small = small_ref[...]
    wq, wk, wv = (small[:, j * HD : (j + 1) * HD] for j in range(3))
    turn = HD // 2
    zero = jnp.zeros_like(wv)
    rest = small[:, 3 * HD :]
    ext_ref[:, :128] = small[:, :128]
    ext_ref[:, 128:256] = jnp.concatenate(
        [-wq[:, turn:], wq[:, :turn], -wk[:, turn:], wk[:, :turn]], 1
    )
    value = jnp.concatenate([wv, zero], 1)
    ext_ref[:, 256:] = value
    head_ref[:, :128] = small[:, :128]
    head_ref[:, 128:] = value
    rest = jnp.concatenate([rest, zero], 1).astype(F32)
    router_ref[...] = jnp.where(lanes_of(rest) < E, rest, 0.0).astype(BF)
    turned = rest.T
    one_ref[...] = turned[E : E + 1, :]
    two_ref[...] = turned[E + 1 : E + 2, :]


def split_small(small):
    shapes = ((D, 384), (D, 256), (D, 128), (1, D), (1, D))
    types = (BF, BF, BF, F32, F32)
    return pl.pallas_call(
        split_kernel,
        out_shape=tuple(jax.ShapeDtypeStruct(s, t) for s, t in zip(shapes, types)),
        grid=(1,),
        in_specs=[fixed(small.shape)],
        out_specs=tuple(fixed(s) for s in shapes),
        compiler_params=params(),
        cost_estimate=cost(1, 3 * 2**20),
        name="split_weights",
    )(small)


def project(x_blk, w_ref, gain_ref, cosine, sine):
    x_f = x_blk.astype(F32)
    factor = lax.rsqrt(jnp.mean(x_f * x_f, axis=1, keepdims=True) + EPSILON)
    normed = (x_f * factor * gain_ref[...]).astype(BF)
    out = dot(normed, w_ref[...], 1, 0)
    both = out[:, :128] * cosine + out[:, 128:256] * sine
    swapped = pltpu.roll(both, 64, 1)
    low = lanes_of(both) < HD
    zero = jnp.zeros_like(both)
    return jnp.concatenate(
        [
            jnp.where(low, both, zero).astype(BF),
            jnp.where(low, swapped, zero).astype(BF),
            jnp.where(low, zero, swapped).astype(BF),
            out[:, 256:].astype(BF),
        ],
        axis=1,
    )


def spot_of(ids, block, block_len):
    return pl.ds(pl.multiple_of(ids[block] * block_len, block_len), block_len)


def head_kernel(
    block_len, band, ids, spots, firsts,
    x_ref, w_ref, gain_ref, cos_ref, sin_ref, all_ref, log_ref, att_ref, a_store,
):
    step = pl.program_id(0)
    total = all_ref.shape[0]
    blocks = QUERY_BLOCK // block_len

    places = [spot_of(ids, 4 * step + j, block_len) for j in range(4)]
    cosine = jnp.concatenate([cos_ref[spot, :] for spot in places], 0)
    sine = jnp.concatenate([sin_ref[spot, :] for spot in places], 0)
    made = project(x_ref[...], w_ref, gain_ref, cosine, sine)
    for j in range(4):
        all_ref[places[j], :] = made[j * block_len : (j + 1) * block_len]

    @pl.when(step == pl.num_programs(0) - 1)
    def _():
        window = band + QUERY_BLOCK

        def step_fn(index, carry):
            first_key, first_query = window_of(index, band)
            rows = pl.ds(first_query, QUERY_BLOCK)
            cols = pl.ds(first_key, window)
            scores = masked_scores(
                all_ref[rows, :128], all_ref[cols, 128:256], first_key, first_query, firsts
            )
            top = jnp.max(scores, axis=1, keepdims=True)
            weight = jnp.exp(scores - top)
            mass = jnp.sum(weight, axis=1, keepdims=True)
            log_ref[rows, :] = top + jnp.log(mass)
            weight = (weight * (1.0 / mass)).astype(BF)
            result = dot(weight, all_ref[cols, 384:], 1, 0)
            for j in range(blocks):
                spot = spot_of(spots, index * blocks + j, block_len)
                a_store[spot, :] = result[j * block_len : (j + 1) * block_len]
            return carry

        lax.fori_loop(0, total // QUERY_BLOCK, step_fn, 0)
        for j in range(total // QUERY_BLOCK):
            part = a_store[j * QUERY_BLOCK : (j + 1) * QUERY_BLOCK, :]
            att_ref[:, j * QUERY_BLOCK : (j + 1) * QUERY_BLOCK] = part.T[:HD].astype(BF)


def head_forward(hidden, w_ext, gain, tables, ids, spots, firsts, count, band):
    total = tables[0].shape[0]
    work = total * (band + QUERY_BLOCK)
    return pl.pallas_call(
        functools.partial(head_kernel, count // 2, band),
        out_shape=(
            jax.ShapeDtypeStruct((total, 512), BF),
            jax.ShapeDtypeStruct((total, 1), F32),
            jax.ShapeDtypeStruct((HD, total), BF),
        ),
        grid_spec=pltpu.PrefetchScalarGridSpec(
            num_scalar_prefetch=3,
            grid=(total // count // 2,),
            in_specs=[
                pl.BlockSpec((2 * count, D), lambda i, *_: (i, 0)),
                fixed((D, 384)), fixed((1, D)), fixed((total, 128)), fixed((total, 128)),
            ],
            out_specs=(fixed((total, 512)), fixed((total, 1)), fixed((HD, total))),
            scratch_shapes=[pltpu.VMEM((total, 128), F32)],
        ),
        compiler_params=params(),
        cost_estimate=cost(total * D * 384 + 4 * work * 128, 2 * total * D, work),
        name="head_forward",
    )(ids, spots, firsts, hidden, w_ext, gain, *tables)


def order_heads(heads, wo_ref, wo_rel):
    per = wo_ref.shape[1]
    many = HD // per
    for j in range(H):
        for m in range(many):
            wo_rel[j * HD + m * per : j * HD + (m + 1) * per, :] = wo_ref[heads[j] * many + m]


def front_kernel(
    tok_count, where, att_ref, x_ref, wo_ref, wgu_ref, gain_ref, mixed_ref, gates_ref, factor_ref,
    mid_ref, scr,
):
    step = pl.program_id(0)
    tile = x_ref.shape[0]
    moved = dot(att_ref[...].reshape(D, tile), wo_ref[...].reshape(D, D), 0, 0)
    middle = x_ref[...].astype(F32) + RESIDUAL_SCALE * moved
    scr[...] = middle

    @pl.when(step == where[2] * tok_count // tile)
    def _():
        own = pl.multiple_of(where[2] * tok_count % tile, tok_count)
        mid_ref[...] = scr[pl.ds(own, tok_count), :]

    factor = lax.rsqrt(jnp.mean(middle * middle, axis=1, keepdims=True) + EPSILON)
    factor_ref[...] = jnp.broadcast_to(factor, factor_ref.shape)
    mixed = (middle * factor * gain_ref[...]).astype(BF)
    mixed_ref[...] = mixed
    gates_ref[...] = dot(mixed, wgu_ref[...], 1, 0)


def expert_front(att, hidden, wo, wgu, gain, where, count):
    total = hidden.shape[0]
    wide = wgu.shape[1]
    tile = 4 * count

    def rows(width):
        return pl.BlockSpec((tile, width), lambda i, *_: (i, 0))

    return pl.pallas_call(
        functools.partial(front_kernel, count),
        out_shape=(
            jax.ShapeDtypeStruct((total, D), BF),
            jax.ShapeDtypeStruct((total, wide), F32),
            jax.ShapeDtypeStruct((total, 128), F32),
            jax.ShapeDtypeStruct((count, D), F32),
        ),
        grid_spec=pltpu.PrefetchScalarGridSpec(
            num_scalar_prefetch=1,
            grid=(total // tile,),
            in_specs=[
                pl.BlockSpec((H, HD, tile), lambda i, *_: (0, 0, i)),
                rows(D), fixed(wo.shape), fixed((D, wide)), fixed((1, D)),
            ],
            out_specs=(rows(D), rows(wide), rows(128), fixed((count, D))),
            scratch_shapes=[pltpu.VMEM((tile, D), F32)],
        ),
        compiler_params=params(),
        cost_estimate=cost(2 * total * D * (D + wide), 14 * total * D),
        name="expert_front",
    )(where, att, hidden, wo, wgu, gain)


def back_kernel(
    part, heads, where, mixed_ref, gates_ref, factor_ref, g_ref, wo_ref, wgu_ref, wd_ref, wr_ref,
    gain_ref, gb_ref, act_ref, v_ref, coef_ref, pa_ref, pb_ref, norm_ref, wo_rel,
):
    step = pl.program_id(0)
    own_expert = where[0]
    half = D // 2

    @pl.when(step == 0)
    def _():
        order_heads(heads, wo_ref, wo_rel)
        norm_ref[...] = jnp.zeros_like(norm_ref)

    mixed = mixed_ref[...]
    grads = g_ref[...].reshape(mixed.shape[0], D + 128)
    logits = dot(mixed, wr_ref[...], 1, 0)
    mask = grads[:, D:].astype(F32)
    logits = jnp.where(mask > 0.0, logits, NEGATIVE)
    odds = jnp.where(mask > 0.0, jnp.exp(logits - jnp.max(logits, axis=1, keepdims=True)), 0.0)
    combine = odds / jnp.sum(odds, axis=1, keepdims=True)
    mark = (lanes_of(combine) == own_expert).astype(F32)
    own_gate = jnp.sum(combine * mark, axis=1, keepdims=True)
    grad_top = grads[:, :D]
    pulled = RESIDUAL_SCALE * dot(grad_top, wd_ref[...], 1, 0)
    gate, up = gates_ref[:, :part], gates_ref[:, part:]
    sigma = 1.0 / (1.0 + jnp.exp(-gate))
    silu = gate * sigma
    activation = silu * up
    grad_act = own_gate * pulled
    act_ref[...] = (RESIDUAL_SCALE * own_gate * activation).astype(BF)
    gb_ref[:, :part] = (grad_act * up * sigma * (1.0 + gate * (1.0 - sigma))).astype(BF)
    gb_ref[:, part:] = (grad_act * silu).astype(BF)
    grad_combine = jnp.sum(activation * pulled, axis=1, keepdims=True)
    coef = (grad_combine * own_gate * (mark - combine)).astype(BF)
    coef_ref[...] = coef
    grad_mixed = dot(gb_ref[...], wgu_ref[...], 1, 1) + dot(coef, wr_ref[...], 1, 1)
    gain = gain_ref[...]
    scaled = mixed.astype(F32) * (1.0 / gain)
    norm_ref[...] += jnp.broadcast_to(
        jnp.sum(grad_mixed * scaled, axis=0, keepdims=True), norm_ref.shape
    )
    inner = grad_mixed * gain
    factor = factor_ref[:, :1]
    grad_mid = factor * (inner - scaled * jnp.mean(inner * scaled, axis=1, keepdims=True))
    grad_mid = grad_mid.astype(BF)
    v_ref[...] = grad_mid
    out_grads = dot(wo_rel[...], grad_mid, 1, 1)
    if part == F:
        top = out_grads[:HD] + dot(wo_rel[:HD, :], grad_top, 1, 1)
        pa_ref[:HD, :] = (RESIDUAL_SCALE * top).astype(BF)
        pa_ref[HD:, :] = (RESIDUAL_SCALE * out_grads[HD:half]).astype(BF)
    else:
        pa_ref[...] = (RESIDUAL_SCALE * out_grads[:half]).astype(BF)
    pb_ref[...] = (RESIDUAL_SCALE * out_grads[half:]).astype(BF)


def expert_back(
    mixed, gates, factor, top, wo, wgu, wd, wr, gain, heads, where, count
):
    total = mixed.shape[0]
    part = wd.shape[1]
    tile = 2 * count

    def rows(width):
        return pl.BlockSpec((tile, width), lambda i, *_: (i, 0))

    def cols(height):
        return pl.BlockSpec((height, tile), lambda i, *_: (0, i))

    def out(width):
        return jax.ShapeDtypeStruct((total, width), BF)

    half = jax.ShapeDtypeStruct((D // 2, total), BF)
    return pl.pallas_call(
        functools.partial(back_kernel, part),
        out_shape=(
            out(2 * part), out(part), out(D), out(128), half, half,
            jax.ShapeDtypeStruct((8, D), F32),
        ),
        grid_spec=pltpu.PrefetchScalarGridSpec(
            num_scalar_prefetch=2,
            grid=(total // tile,),
            in_specs=[
                rows(D), rows(2 * part), rows(128),
                pl.BlockSpec((2, count, D + 128), lambda i, *_: (i, 0, 0)),
                fixed(wo.shape), fixed((D, 2 * part)), fixed((D, part)), fixed((D, 128)),
                fixed((1, D)),
            ],
            out_specs=(
                rows(2 * part), rows(part), rows(D), rows(128), cols(D // 2), cols(D // 2),
                fixed((8, D)),
            ),
            scratch_shapes=[pltpu.VMEM((D, D), BF)],
        ),
        compiler_params=params(),
        cost_estimate=cost(2 * total * D * (D + 3 * part), 14 * total * D, total * part),
        name="expert_back",
    )(heads, where, mixed, gates, factor, top, wo, wgu, wd, wr, gain)


def up_kernel(mixed_ref, gb_ref, coef_ref, norm_ref, out_ref, acc):
    step = pl.program_id(0)
    wide = gb_ref.shape[1]
    terms = ((0, wide, gb_ref[...]), (wide, wide + 128, coef_ref[...]))

    @pl.when(step == 0)
    def _():
        for low, high, right in terms:
            acc[:, low:high] = dot(mixed_ref[...], right, 0, 0)

    @pl.when(step > 0)
    def _():
        for low, high, right in terms:
            acc[:, low:high] += dot(mixed_ref[...], right, 0, 0)

    @pl.when(step == pl.num_programs(0) - 1)
    def _():
        out_ref[:, :wide] = acc[:, :wide].astype(BF)
        last = acc[:, wide:]
        out_ref[:, wide:] = jnp.where(lanes_of(last) == E, column_of(norm_ref), last).astype(BF)


def up_weights(mixed, gb, coef, norm):
    total, wide = gb.shape
    tile = 512

    def rows(size):
        return pl.BlockSpec((tile, size), lambda i: (i, 0))

    return pl.pallas_call(
        up_kernel,
        out_shape=jax.ShapeDtypeStruct((D, wide + 128), BF),
        grid=(total // tile,),
        in_specs=[rows(D), rows(wide), rows(128), fixed((8, D))],
        out_specs=fixed((D, wide + 128)),
        scratch_shapes=[pltpu.VMEM((D, wide + 128), F32)],
        compiler_params=params(),
        cost_estimate=cost(2 * total * D * wide, 4 * total * D),
        name="up_weights",
    )(mixed, gb, coef, norm)


def down_kernel(g_ref, act_ref, out_ref, acc):
    step = pl.program_id(0)
    grads = g_ref[...].reshape(-1, D)

    @pl.when(step == 0)
    def _():
        acc[...] = dot(grads, act_ref[...], 0, 0)

    @pl.when(step > 0)
    def _():
        acc[...] += dot(grads, act_ref[...], 0, 0)

    @pl.when(step == pl.num_programs(0) - 1)
    def _():
        out_ref[...] = acc[...].astype(BF)


def down_weights(both, act, count):
    total, part = act.shape
    return pl.pallas_call(
        down_kernel,
        out_shape=jax.ShapeDtypeStruct((D, part), BF),
        grid=(total // (4 * count),),
        in_specs=[
            pl.BlockSpec((4, count, D), lambda i: (i, 0, 0)),
            pl.BlockSpec((4 * count, part), lambda i: (i, 0)),
        ],
        out_specs=fixed((D, part)),
        scratch_shapes=[pltpu.VMEM((D, part), F32)],
        compiler_params=params(),
        cost_estimate=cost(2 * total * D * part, 3 * total * D),
        name="down_weights",
    )(both, act)


def moe_kernel(act_ref, wd_ref, out_ref):
    out_ref[...] = dot(act_ref[...], wd_ref[...], 1, 1).astype(BF).reshape(out_ref.shape)


def moe_out(act, wd, count, rows):
    total, part = act.shape
    many = 4
    return pl.pallas_call(
        moe_kernel,
        out_shape=jax.ShapeDtypeStruct((total // count, count + 2 * rows, D), BF),
        grid=(total // count // many,),
        in_specs=[pl.BlockSpec((many * count, part), lambda i: (i, 0)), fixed((D, part))],
        out_specs=pl.BlockSpec((many, count, D), lambda i: (i, 0, 0)),
        compiler_params=params(),
        cost_estimate=cost(2 * total * D * part, 3 * total * D),
        name="moe_out",
    )(act, wd)


def output_kernel(where, att_ref, v_ref, g_ref, moe_ref, out_ref, acc):
    step = pl.program_id(0)
    tile = v_ref.shape[0]

    @pl.when(step == 0)
    def _():
        acc[...] = jnp.zeros_like(acc)

    acc[...] += dot(att_ref[...].reshape(D, tile), v_ref[...], 1, 0)
    picked = att_ref[where[0]]
    place = step * tile + lanes_of(picked)
    picked = jnp.where(place // where[3] == where[1], picked, jnp.zeros_like(picked))
    target = pl.ds(pl.multiple_of(where[0] * HD, HD), HD)
    acc[target, :] += dot(picked, g_ref[...].reshape(tile, D), 1, 0)

    @pl.when(step == pl.num_programs(0) - 1)
    def _():
        out_ref[...] = (RESIDUAL_SCALE * acc[...]).astype(BF).reshape(out_ref.shape)


def output_weights(att, grad_mid, top, moe, where, count, rows):
    total = grad_mid.shape[0]
    tile = 4 * count
    per = 2 * rows
    return pl.pallas_call(
        output_kernel,
        out_shape=jax.ShapeDtypeStruct(moe.shape, BF),
        grid_spec=pltpu.PrefetchScalarGridSpec(
            num_scalar_prefetch=1,
            grid=(total // tile,),
            in_specs=[
                pl.BlockSpec((H, HD, tile), lambda i, *_: (0, 0, i)),
                pl.BlockSpec((tile, D), lambda i, *_: (i, 0)),
                pl.BlockSpec((4, count, D), lambda i, *_: (i, 0, 0)),
                pl.BlockSpec(memory_space=pl.ANY),
            ],
            out_specs=fixed((moe.shape[0], per, D), (0, count // per, 0)),
            scratch_shapes=[pltpu.VMEM((D, D), F32)],
        ),
        input_output_aliases={4: 0},
        compiler_params=params(),
        cost_estimate=cost(2 * total * D * D, 8 * total * D),
        name="output_weights",
    )(where, att, grad_mid, top, moe)


def attend_kernel(
    block_len, band, ids, spots, firsts, where, all_ref, up_ref, log_ref, cos_ref, sin_ref,
    own_ref, up_sort, acc_qk, acc_v,
):
    total = all_ref.shape[0]
    blocks = QUERY_BLOCK // block_len
    window = band + QUERY_BLOCK
    acc_qk[...] = jnp.zeros_like(acc_qk)
    acc_v[...] = jnp.zeros_like(acc_v)
    for j in range(total // QUERY_BLOCK):
        piece = up_ref[:, j * QUERY_BLOCK : (j + 1) * QUERY_BLOCK]
        piece = jnp.concatenate([piece, jnp.zeros_like(piece)], 0).T.astype(BF)
        for m in range(blocks):
            spot = spot_of(ids, j * blocks + m, block_len)
            up_sort[spot, :] = piece[m * block_len : (m + 1) * block_len]

    def step_fn(index, carry):
        first_key, first_query = window_of(index, band)
        rows = pl.ds(first_query, QUERY_BLOCK)
        cols = pl.ds(first_key, window)
        keys_win, upstream = all_ref[cols, 128:256], up_sort[rows, :]
        scores = masked_scores(all_ref[rows, :128], keys_win, first_key, first_query, firsts)
        weight = jnp.exp(scores - log_ref[rows, :])
        grad_weight = dot(upstream, all_ref[cols, 384:], 1, 1)
        delta = jnp.sum(weight * grad_weight, axis=1, keepdims=True)
        grad_raw = (SCORE_SCALE * weight * (grad_weight - delta)).astype(BF)
        acc_qk[rows, :] += dot(grad_raw, keys_win, 1, 0)
        acc_qk[cols, :] += dot(grad_raw, all_ref[rows, 256:384], 0, 0)
        acc_v[cols, :] += dot(weight.astype(BF), upstream, 0, 0)
        return carry

    lax.fori_loop(0, total // QUERY_BLOCK, step_fn, 0)

    def turn(index, carry):
        first = pl.multiple_of(index * QUERY_BLOCK, QUERY_BLOCK)
        rows = pl.ds(first, QUERY_BLOCK)
        both = acc_qk[rows, :]
        low = lanes_of(both) % HD < HD // 2
        swapped = jnp.where(low, pltpu.roll(both, 96, 1), -pltpu.roll(both, 32, 1))
        turned = (both * cos_ref[rows, :] + swapped * sin_ref[rows, :]).astype(BF)
        made = jnp.concatenate([turned, acc_v[rows, :].astype(BF)], 1)
        for j in range(blocks):
            block = spots[index * blocks + j]
            first = pl.multiple_of(block * block_len, block_len)
            piece = made[j * block_len : (j + 1) * block_len]
            keep = first // where[3] == where[1]
            own_ref[pl.ds(first, block_len), :] = jnp.where(keep, piece, jnp.zeros_like(piece))
        return carry

    lax.fori_loop(0, total // QUERY_BLOCK, turn, 0)


def attend_backward(heads_all, upstream, logs, tables, ids, spots, firsts, where, count, band):
    total = heads_all.shape[0]
    work = total * (band + QUERY_BLOCK)
    return pl.pallas_call(
        functools.partial(attend_kernel, count // 2, band),
        out_shape=jax.ShapeDtypeStruct((total, 256), BF),
        grid_spec=pltpu.PrefetchScalarGridSpec(
            num_scalar_prefetch=4,
            grid=(1,),
            in_specs=[
                fixed((total, 512)), fixed((HD, total)), fixed((total, 1)), fixed((total, 128)),
                fixed((total, 128)),
            ],
            out_specs=fixed((total, 256)),
            scratch_shapes=[
                pltpu.VMEM((total, 128), BF),
                pltpu.VMEM((total, 128), F32),
                pltpu.VMEM((total, 128), F32),
            ],
        ),
        compiler_params=params(60),
        cost_estimate=cost(10 * work * 128, 2 * total * 1024, work),
        name="attend_backward",
    )(ids, spots, firsts, where, heads_all, upstream, logs, *tables)


def pull_kernel(
    last, order, g_ref, h_ref, w_ref, gain_ref, x_ref, y_ref, gm_ref, hm_ref, w_in_ref, n_in_ref,
    out_ref, w_out_ref, n_out_ref, acc_w,
):
    step = pl.program_id(0)

    @pl.when(step == 0)
    def _():
        acc_w[...] = w_in_ref[...]
        n_out_ref[...] = n_in_ref[...]

    grads = jnp.concatenate([g_ref[...], h_ref[...]], 0)
    grad_mid = jnp.concatenate([gm_ref[...], hm_ref[...]], 0).astype(F32)
    grad_normed = dot(grads, w_ref[...], 1, 1)
    x_f = jnp.concatenate([x_ref[...], y_ref[...]], 0).astype(F32)
    factor = lax.rsqrt(jnp.mean(x_f * x_f, axis=1, keepdims=True) + EPSILON)
    scaled = x_f * factor
    normed = (scaled * gain_ref[...]).astype(BF)
    acc_w[...] += dot(normed, grads, 0, 0)
    n_out_ref[...] += jnp.broadcast_to(
        jnp.sum(grad_normed * scaled, axis=0, keepdims=True), n_out_ref.shape
    )
    inner = grad_normed * gain_ref[...]
    grad_x = factor * (inner - scaled * jnp.mean(inner * scaled, axis=1, keepdims=True))
    out_ref[...] = (grad_x + grad_mid).astype(BF)

    @pl.when(step == pl.num_programs(0) - 1)
    def _():
        if last:
            tail = acc_w[:, 128:]
            w_out_ref[:, :128] = acc_w[:, :128].astype(BF)
            w_out_ref[:, 128:] = jnp.where(
                lanes_of(tail) == HD, column_of(n_out_ref), tail
            ).astype(BF)
        else:
            w_out_ref[...] = acc_w[...]


def pull_heads(own_grads, w_head, gain, hidden, grad_mid, w_in, n_in, order, count, last):
    total = hidden.shape[0] // 2

    def at(width, j):
        return pl.BlockSpec((count, width), lambda i, order: (order[2 * i + j], 0))

    block = pl.BlockSpec((2 * count, D), lambda i, order: (i, 0))
    return pl.pallas_call(
        functools.partial(pull_kernel, last),
        out_shape=(
            jax.ShapeDtypeStruct((total, D), BF),
            jax.ShapeDtypeStruct((D, 256), BF if last else F32),
            jax.ShapeDtypeStruct((8, D), F32),
        ),
        grid_spec=pltpu.PrefetchScalarGridSpec(
            num_scalar_prefetch=1,
            grid=(total // count // 2,),
            in_specs=[
                at(256, 0), at(256, 1), fixed((D, 256)), fixed((1, D)), at(D, 0), at(D, 1), at(D, 0),
                at(D, 1),
                fixed((D, 256)), fixed((8, D)),
            ],
            out_specs=(block, fixed((D, 256)), fixed((8, D))),
            scratch_shapes=[pltpu.VMEM((D, 256), F32)],
        ),
        compiler_params=params(),
        cost_estimate=cost(4 * total * D * 256, 6 * total * D, weight=1),
        name="pull_last" if last else "pull_first",
    )(
        order, own_grads, own_grads, w_head, gain, hidden, hidden, grad_mid, grad_mid, w_in, n_in
    )


def finish_kernel(in_ref, q_ref, k_ref, v_ref, gain_ref):
    def piece(head):
        return in_ref[2 * head].astype(F32) + in_ref[2 * head + 1].astype(F32)

    total = jnp.zeros_like(piece(0))
    for quad in range(H // 4):
        heads = [piece(4 * quad + j) for j in range(4)]
        for j in range(2):
            first = (4 * quad + 2 * j) * HD
            q_ref[:, first : first + 128] = jnp.concatenate(
                [heads[2 * j][:, :HD], heads[2 * j + 1][:, :HD]], 1
            )
        pairs = [heads[0] + heads[1], heads[2] + heads[3]]
        total = total + pairs[0] + pairs[1]
        for ref, low in ((k_ref, HD), (v_ref, 2 * HD)):
            ref[:, quad * 128 : (quad + 1) * 128] = jnp.concatenate(
                [pair[:, low : low + HD] for pair in pairs], 1
            )
    gain_ref[...] = total[:, 128:]


def finish_heads(arrived):
    rows = arrived.shape[1]
    return pl.pallas_call(
        finish_kernel,
        out_shape=(
            jax.ShapeDtypeStruct((rows, D), F32),
            jax.ShapeDtypeStruct((rows, D // 2), F32),
            jax.ShapeDtypeStruct((rows, D // 2), F32),
            jax.ShapeDtypeStruct((rows, 128), F32),
        ),
        compiler_params=params(24),
        cost_estimate=cost(1, 2**20),
        name="finish_heads",
    )(arrived)


def finish_kernel_experts(in_ref, up_ref, down_ref, tail_ref):
    many = in_ref.shape[0]
    wide, narrow = up_ref.shape[1] // many, down_ref.shape[1] // many
    for j in range(many):
        up_ref[:, j * wide : (j + 1) * wide] = in_ref[j, :, :wide].astype(F32)
        down_ref[:, j * narrow : (j + 1) * narrow] = in_ref[j, :, wide + 128 :].astype(F32)

    @pl.when(pl.program_id(0) == 0)
    def _():
        tail_ref[...] = jnp.zeros_like(tail_ref)

    for j in range(many):
        tail_ref[...] += in_ref[j, :, wide : wide + 128].astype(F32)


def finish_experts(arrived):
    places, rows, width = arrived.shape
    part = (width - 128) // 3
    return pl.pallas_call(
        finish_kernel_experts,
        out_shape=(
            jax.ShapeDtypeStruct((rows, places * 2 * part), F32),
            jax.ShapeDtypeStruct((rows, places * part), F32),
            jax.ShapeDtypeStruct((rows, 128), F32),
        ),
        grid=(places // 4,),
        in_specs=[pl.BlockSpec((4, rows, width), lambda i: (i, 0, 0))],
        out_specs=(
            pl.BlockSpec((rows, 8 * part), lambda i: (0, i)),
            pl.BlockSpec((rows, 4 * part), lambda i: (0, i)),
            fixed((rows, 128)),
        ),
        compiler_params=params(),
        cost_estimate=cost(1, 5 * 2**20),
        name="finish_experts",
    )(arrived)


def per_device(
    hidden_in,
    out_grad,
    doc_lengths,
    block_order,
    routes,
    attn_norm,
    w_query,
    w_key,
    w_value,
    w_output,
    ffn_norm,
    w_router,
    w_gate_up,
    w_down,
):
    ctx_count = lax.axis_size("ctx")
    ctx_place = lax.axis_index("ctx")
    fsdp_place = lax.axis_index("fsdp")
    copies = ctx_count // E
    own_expert, own_copy = ctx_place // copies, ctx_place % copies
    tok_count = hidden_in.shape[1]
    seq_len = tok_count * ctx_count
    block_len = tok_count // 2
    band = seq_len // 4
    rows = attn_norm.shape[0]
    part = F // copies
    groups = H // KVH
    share = seq_len // copies
    swap_y = [(0, 1), (1, 0)]
    alone = copies == 1

    def swap_fsdp(mine):
        return lax.ppermute(mine, "fsdp", swap_y)

    def both_rows(mine):
        theirs = swap_fsdp(mine)
        stacked = jnp.where(
            fsdp_place == 0, jnp.stack([mine, theirs], 1), jnp.stack([theirs, mine], 1)
        )
        return stacked.reshape(-1, mine.shape[-1])

    def exchange(split):
        return lax.all_to_all(split, "ctx", 0, 0, tiled=True)

    ids = block_order[0]
    block_ids = jnp.arange(ids.shape[0], dtype=jnp.int32)
    spots = jnp.sum(jnp.where(ids[None, :] == block_ids[:, None], block_ids[None, :], 0), axis=1)
    lengths = doc_lengths[0]
    doc_ids = jnp.arange(lengths.shape[0], dtype=jnp.int32)
    firsts = jnp.sum(
        jnp.where(doc_ids[None, :] < doc_ids[:, None], lengths[None, :], 0), axis=1
    )
    tables = tables_of(seq_len)
    order, heads = block_order_of(ctx_count), block_order_of(E)
    where = jnp.stack([own_expert, own_copy, ctx_place, jnp.int32(share)]).astype(jnp.int32)

    def by_expert(weight, pieces):
        split = weight.reshape(rows, E, pieces, copies, part)
        return split.transpose(1, 3, 0, 2, 4).reshape(ctx_count, rows, pieces * part)

    chosen_mask = jnp.any(
        routes[0][:, :, None] == jnp.arange(E, dtype=jnp.int32)[None, None, :], axis=1
    ).astype(BF)
    grads_own = jnp.concatenate(
        [out_grad[0], chosen_mask, jnp.zeros((tok_count, 128 - E), BF)], axis=1
    )
    experts = jnp.concatenate([by_expert(w_gate_up, 2), by_expert(w_down, 1)], axis=2)
    norms = jnp.stack([attn_norm, ffn_norm], 1)
    if alone:
        small_here = exchange(pack_small(copies, w_query, w_key, w_value, w_router, norms))
        w_ext, w_head, router_full, gain_one, gain_two = split_small(both_rows(small_here))
        near = Gather(hidden_in[0])
        near.cross()
        near.last(small_here)
        experts_here = exchange(after(experts, near.two))
        hidden_all = near.join(order, "join_hidden", w_ext).reshape(seq_len, D)
    else:
        small_here = exchange(pack_small(copies, w_query, w_key, w_value, w_router, norms))
        w_ext, w_head, router_full, gain_one, gain_two = split_small(both_rows(small_here))
        hidden_all = lax.all_gather(hidden_in[0], "ctx", axis=0, tiled=True)
        experts_here = exchange(experts)
    out_all = lax.all_gather(w_output, BOTH, axis=0, tiled=True).reshape(ctx_count, 2 * rows, D)
    top_all = lax.all_gather(grads_own[None], "ctx", axis=0, tiled=True)

    heads_all, logs, attended = head_forward(
        hidden_all, w_ext, gain_one, tables, ids, spots, firsts, tok_count, band
    )
    def half_rows(mine, theirs):
        stacked = jnp.where(
            fsdp_place == 0, jnp.stack([mine, theirs], 1), jnp.stack([theirs, mine], 1)
        )
        return stacked.reshape(D, mine.shape[-1])

    if alone:
        att = Gather(attended)
        experts_here = after(experts_here, attended)
    gu_here, dn_here = experts_here[:, :, : 2 * part], experts_here[:, :, 2 * part :]
    gu_there, dn_there = swap_fsdp(gu_here), swap_fsdp(dn_here)
    w_gu, w_dn = half_rows(gu_here, gu_there), half_rows(dn_here, dn_there)
    if alone:
        att.cross()
        att.last(experts_here)
        att_all = att.join(heads, "join_heads", w_gu)
    else:
        sent = lax.dynamic_slice_in_dim(attended, own_copy * share, share, 1)
        att_all = lax.all_gather(sent, "ctx", axis=0, tiled=True)
        att_all = att_all.reshape(H, copies, HD, share).transpose(0, 2, 1, 3)
        att_all = att_all.reshape(H, HD, seq_len)

    mixed, gates, factor, middle = expert_front(
        att_all, hidden_all, out_all, w_gu, gain_two, where, tok_count
    )
    grad_both, act, grad_mid, coef, pull_a, pull_b, norm_sum = expert_back(
        mixed, gates, factor, top_all, out_all, w_gu, w_dn, router_full, gain_two, heads, where,
        tok_count,
    )

    def given_rows(grads):
        by_owner = grads.reshape(ctx_count, 2, rows, grads.shape[1])
        return by_owner, lax.dynamic_index_in_dim(by_owner, 1 - fsdp_place, 1, keepdims=False)

    def to_owner(by_owner, theirs):
        kept = lax.dynamic_index_in_dim(by_owner, fsdp_place, 1, keepdims=False)
        return (kept.astype(F32) + theirs.astype(F32)).astype(BF)

    gu_owner, gu_given = given_rows(up_weights(mixed, grad_both, coef, norm_sum))
    gu_theirs = swap_fsdp(gu_given)
    act_late, act_last = act, act
    if alone:
        ring = RingSum(pull_a, permute(pull_b, SWAP_CORE))
        act_late = after(act, ring.cross_out, gu_given)
    moe = moe_out(act_late, w_dn, tok_count, rows)
    out_both = output_weights(
        att_all, grad_mid, top_all, moe, where, tok_count, rows
    )
    if alone:
        ring.cross()
        out_both = after(out_both, *ring.sends)
        act_last = after(act, *ring.sends)
    dn_owner, dn_given = given_rows(
        down_weights(top_all, act_last, tok_count)
    )
    dn_theirs = swap_fsdp(dn_given)
    if alone:
        upstream = ring.end(dn_given)
        gu_theirs, dn_theirs = after(gu_theirs, upstream), after(dn_theirs, upstream)
    else:
        joined = jnp.concatenate([pull_a, pull_b], 0)
        pulled = lax.psum_scatter(joined, "ctx", scatter_dimension=0, tiled=True)
        rings = [[i * copies + j for j in range(copies)] for i in range(E)]
        pulled = lax.all_gather(pulled, "ctx", axis=0, tiled=True, axis_index_groups=rings)
        own_out = lax.dynamic_slice_in_dim(out_all.reshape(D, D), own_expert * HD, HD, 0)
        top_rows = top_all[:, :, :D].reshape(seq_len, D)
        upstream = pulled.astype(F32) + RESIDUAL_SCALE * dot(own_out, top_rows, 1, 1)
    grads_all_expert = jnp.concatenate(
        [to_owner(gu_owner, gu_theirs), to_owner(dn_owner, dn_theirs)], 2
    )

    own_grads = attend_backward(
        heads_all, upstream, logs, tables, ids, spots, firsts, where, tok_count, band
    )
    own_grads = after(own_grads, grads_all_expert)
    experts_in = exchange(grads_all_expert)
    grad_b, head_sum, norm_head = pull_heads(
        own_grads, w_head, gain_one, hidden_all, grad_mid, jnp.zeros((D, 256), F32),
        jnp.zeros((8, D), F32), order[ctx_count // 2 :], tok_count, False,
    )
    grad_a, grad_heads, ignored = pull_heads(
        own_grads, w_head, gain_one, hidden_all, grad_mid, head_sum, norm_head,
        order[: ctx_count // 2], tok_count, True,
    )
    if alone:
        ring = RingSum(grad_a, permute(grad_b, SWAP_CORE))
        ring.cross()
        experts_in = after(experts_in, *ring.sends)
    else:
        joined = jnp.concatenate([grad_a, grad_b], 0)
        grad_own = lax.psum_scatter(joined, "ctx", scatter_dimension=0, tiled=True).astype(F32)
    def from_experts(block, pieces):
        block = block[:, :, : pieces * part].astype(F32)
        block = block.reshape(E, copies, rows, pieces, part).transpose(2, 0, 3, 1, 4)
        return block.reshape(rows, E * pieces * F)

    if alone:
        share_gate_up, share_down, tail = finish_experts(experts_in)
    else:
        gu_in = experts_in[:, :, : 2 * part + 128]
        dn_in = experts_in[:, :, 2 * part + 128 :]
        share_gate_up = from_experts(gu_in, 2)
        share_down = from_experts(dn_in, 1)
        tail = jnp.sum(gu_in[:, :, 2 * part :].astype(F32), axis=0)
    share_router = tail[:, :E]
    share_gain_two = tail[:, E]
    out_own = lax.psum_scatter(out_both, "ctx", scatter_dimension=0, tiled=False).astype(F32)
    hidden_out = (middle + out_own[:tok_count]).astype(BF)
    out_rows = out_own[tok_count:].reshape(2, rows, D)
    mine = lax.dynamic_index_in_dim(out_rows, fsdp_place, 0, keepdims=False)
    theirs = lax.dynamic_index_in_dim(out_rows, 1 - fsdp_place, 0, keepdims=False)
    share_output = mine + swap_fsdp(theirs)

    if alone:
        grad_own = ring.end(share_output, hidden_out, share_gate_up)
        grad_heads = after(grad_heads, ring.own)
    grad_in = out_grad[0].astype(F32) + grad_own
    tail_in = lax.all_to_all(
        grad_heads.reshape(2 * ctx_count, rows, 256), BOTH, 0, 0, tiled=True
    )
    if alone:
        share_query, share_key, share_value, gain_sum = finish_heads(tail_in)
        share_gain_one = gain_sum[:, HD]
    else:
        tail_in = tail_in.astype(F32).reshape(H, copies * 2, rows, 256)
        heads_in = jnp.sum(tail_in[..., : 3 * HD], axis=1)
        share_query = heads_in[:, :, :HD].transpose(1, 0, 2).reshape(rows, H * HD)
        pairs_in = heads_in[:, :, HD:].reshape(KVH, groups, rows, 2, HD).sum(1)
        share_key = pairs_in[:, :, 0].transpose(1, 0, 2).reshape(rows, KVH * HD)
        share_value = pairs_in[:, :, 1].transpose(1, 0, 2).reshape(rows, KVH * HD)
        share_gain_one = jnp.sum(tail_in[..., 3 * HD], axis=(0, 1))
    return (
        hidden_out[None],
        grad_in[None],
        share_gain_one,
        share_query,
        share_key,
        share_value,
        share_output,
        share_gain_two,
        share_router,
        share_gate_up,
        share_down,
    )


def solution(mesh):
    return jax.shard_map(
        per_device,
        mesh=mesh,
        in_specs=(
            P("fsdp", "ctx", None),
            P("fsdp", "ctx", None),
            P("fsdp", None),
            P("fsdp", None),
            P("fsdp", "ctx", None),
            P(BOTH),
            P(BOTH, None),
            P(BOTH, None),
            P(BOTH, None),
            P(BOTH, None),
            P(BOTH),
            P(BOTH, None),
            P(BOTH, None),
            P(BOTH, None),
        ),
        out_specs=(
            P("fsdp", "ctx", None),
            P("fsdp", "ctx", None),
            P(BOTH),
            P(BOTH, None),
            P(BOTH, None),
            P(BOTH, None),
            P(BOTH, None),
            P(BOTH),
            P(BOTH, None),
            P(BOTH, None),
            P(BOTH, None),
        ),
        check_vma=False,
    )
```

```python
import functools

import jax
import jax.numpy as jnp
import numpy as np
from jax import lax
from jax.experimental import pallas as pl
from jax.experimental.pallas import tpu as pltpu
from jax.sharding import PartitionSpec as P

D = 1024
H = 16
KVH = 8
HD = 64
F = 512
E = 16

EPSILON = 1e-06
SCORE_SCALE = 0.015625
RESIDUAL_SCALE = 0.22
THETA = 10000.0
NEGATIVE = -1e30
BOTH = ("ctx", "fsdp")
EXPERT_WEIGHT = 2
BF = jnp.bfloat16
F32 = jnp.float32
QUERY_BLOCK = 256


def dot(left, right, left_dim, right_dim):
    return lax.dot_general(
        left, right, (((left_dim,), (right_dim,)), ((), ())), preferred_element_type=F32
    )


def permute(values, pairs):
    return lax.ppermute(values, "ctx", pairs)


def shift_z(step):
    return [(i, ((i // 4 + step) % 4) * 4 + i % 4) for i in range(16)]


SWAP_X = [(i, i ^ 2) for i in range(16)]
SWAP_CORE = [(i, i ^ 1) for i in range(16)]


def after(value, *others):
    return lax.optimization_barrier((value, *others))[0] if others else lax.optimization_barrier(value)


def block_order_of(count):
    index = jnp.arange(count, dtype=jnp.int32)
    if lax.axis_size("ctx") != 16:
        return index
    place = lax.axis_index("ctx")
    z_of = (place // 4 - (index % 8) // 2 + 4) % 4
    x_of = ((place // 2) % 2 + index % 2) % 2
    return z_of * 4 + x_of * 2 + (place % 2 + index // 8) % 2


class RingSum:
    def __init__(self, mine, arrived):
        self.mine, self.arrived = mine, arrived
        self.count = mine.shape[0] // 8
        self.cross_out = jnp.concatenate([self.chip(k, 1) for k in (2, 1, 3)], 0).astype(BF)

    def chip(self, k, dx):
        rows = slice((2 * k + dx) * self.count, (2 * k + dx + 1) * self.count)
        return self.mine[rows].astype(F32) + self.arrived[rows].astype(F32)

    def cross(self):
        got = permute(self.cross_out, SWAP_X)
        self.sends = []
        for j, k in enumerate((2, 1, 3)):
            term = got[j * self.count : (j + 1) * self.count].astype(F32)
            self.sends.append((self.chip(k, 0) + term).astype(BF))

    def end(self, *others):
        self.own = permute(self.chip(0, 1).astype(BF), SWAP_X)
        total = self.chip(0, 0) + self.own.astype(F32)
        for send, k in zip(self.sends, (2, 1, 3)):
            term = permute(send, shift_z(4 - k))
            self.seen = term
            if k == 2 and others:
                term = after(term, *others)
            total = total + term.astype(F32)
        return total


def join_kernel(places, *refs):
    pieces, out_ref, sems = refs[:14], refs[14], refs[15]
    count = out_ref.shape[1]
    copies = []
    for side in range(2):
        own, far, one, pair, two, far_two, three = pieces[7 * side : 7 * side + 7]
        lower, upper = pair.at[:count], pair.at[count:]
        for j, piece in enumerate((own, far, one, lower, two, far_two, three, upper)):
            block = 8 * side + j
            copies.append(
                pltpu.make_async_copy(piece, out_ref.at[places[block]], sems.at[block])
            )
    for copy in copies:
        copy.start()
    for copy in copies:
        copy.wait()


def spread_ctx(blocks):
    _, rows, width = blocks.shape
    other = permute(blocks[8:], SWAP_CORE)
    chip = jnp.stack([blocks[:8], other], 1).reshape(4, 2, 2, rows, width)
    crossed = permute(chip[:, 1], SWAP_X)
    both = jnp.concatenate([chip[:, 0], crossed], 1)
    return (both[0], *(permute(both[k], shift_z(4 - k)) for k in range(1, 4)))


def sender_order_of():
    place = lax.axis_index("ctx")
    index = jnp.arange(16, dtype=jnp.int32)
    z_of = (place // 4 + index // 4) % 4
    x_of = ((place // 2) % 2 + (index // 2) % 2) % 2
    return z_of * 4 + x_of * 2 + (place % 2 + index % 2) % 2


class Gather:
    def __init__(self, rows):
        self.count = rows.shape[0]
        self.own = rows
        self.one = permute(rows, shift_z(1))
        self.three = permute(rows, shift_z(3))
        self.far = permute(rows, SWAP_X)
        self.two = permute(rows, shift_z(2))

    def cross(self, *others):
        if others:
            self.one, self.three = after((self.one, self.three), *others)
        self.pair = permute(jnp.concatenate([self.one, self.three], 0), SWAP_X)

    def last(self, *others):
        if others:
            self.two = after(self.two, *others)
        self.far_two = permute(self.two, SWAP_X)

    def join(self, places, name, *others):
        if others:
            self.far, self.far_two = after((self.far, self.far_two), *others)
        mine = (self.own, self.far, self.one, self.pair, self.two, self.far_two, self.three)
        other = tuple(permute(piece, SWAP_CORE) for piece in mine)
        shape = (16, *self.own.shape)
        return pl.pallas_call(
            join_kernel,
            out_shape=jax.ShapeDtypeStruct(shape, BF),
            grid_spec=pltpu.PrefetchScalarGridSpec(
                num_scalar_prefetch=1,
                grid=(1,),
                in_specs=[fixed(piece.shape) for piece in (*mine, *other)],
                out_specs=pl.BlockSpec(memory_space=pl.ANY),
                scratch_shapes=[pltpu.SemaphoreType.DMA((16,))],
            ),
            compiler_params=params(),
            cost_estimate=cost(1, 4 * self.own.size * 16),
            name=name,
        )(places, *mine, *other)


def tables_of(total):
    half_width = HD // 2
    frequency = (THETA ** (-np.arange(half_width) / half_width)).astype(np.float32)
    angles = np.arange(total, dtype=np.float32)[:, None] * frequency[None, :]
    cosine = np.cos(angles.astype(np.float64)).astype(np.float32)
    sine = np.sin(angles.astype(np.float64)).astype(np.float32)
    return jnp.asarray(np.tile(cosine, (1, 4))), jnp.asarray(np.tile(sine, (1, 4)))


def window_of(step, band):
    start = jnp.maximum(step * QUERY_BLOCK - band, 0)
    return pl.multiple_of(start, QUERY_BLOCK), pl.multiple_of(step * QUERY_BLOCK, QUERY_BLOCK)


def masked_scores(queries, keys_win, first_key, first_query, firsts):
    raw = dot(queries, keys_win, 1, 1) * SCORE_SCALE
    key_place = first_key + lax.broadcasted_iota(jnp.int32, raw.shape, 1)
    query_place = first_query + lax.broadcasted_iota(jnp.int32, raw.shape, 0)
    column = first_query + lax.broadcasted_iota(jnp.int32, (raw.shape[0], 1), 0)
    start = jnp.max(jnp.where(firsts <= column, firsts, 0), axis=1, keepdims=True)
    visible = (key_place <= query_place) & (key_place >= start)
    return jnp.where(visible, raw, NEGATIVE)


def lanes_of(values):
    return lax.broadcasted_iota(jnp.int32, values.shape, 1)


def fixed(shape, at=None):
    place = (0,) * len(shape) if at is None else at
    return pl.BlockSpec(shape, lambda *_: place, pipeline_mode=pl.Buffered(1))


def params(mib=56):
    return pltpu.CompilerParams(vmem_limit_bytes=mib * 2**20)


def cost(flops, bytes_accessed, transcendentals=0, weight=20):
    return pl.CostEstimate(
        flops=weight * flops,
        bytes_accessed=weight * bytes_accessed,
        transcendentals=transcendentals,
    )


def column_of(row_ref):
    return jnp.broadcast_to(row_ref[:1, :], (128, row_ref.shape[1])).T


def pack_kernel(copies, wq_ref, wk_ref, wv_ref, wr_ref, norm_ref, small_ref):
    rows = wq_ref.shape[0]
    rest = jnp.concatenate(
        [wr_ref[...], norm_ref[...], jnp.zeros((rows, HD - E - 2), BF)], axis=1
    )
    for place in range(E * copies):
        head = place // copies
        pair = head // (H // KVH)
        query = wq_ref[:, head * HD : (head + 1) * HD]
        key = wk_ref[:, pair * HD : (pair + 1) * HD]
        value = wv_ref[:, pair * HD : (pair + 1) * HD]
        small_ref[place] = jnp.concatenate([query, key, value, rest], axis=1)


def pack_small(copies, *weights):
    shape = (E * copies, weights[0].shape[0], 256)
    return pl.pallas_call(
        functools.partial(pack_kernel, copies),
        out_shape=jax.ShapeDtypeStruct(shape, BF),
        grid=(1,),
        in_specs=[fixed(weight.shape) for weight in weights],
        out_specs=fixed(shape),
        compiler_params=params(),
        cost_estimate=cost(1, 2**20),
        name="pack_small",
    )(*weights)


def split_kernel(small_ref, ext_ref, head_ref, router_ref, one_ref, two_ref):
    small = small_ref[...]
    wq, wk, wv = (small[:, j * HD : (j + 1) * HD] for j in range(3))
    turn = HD // 2
    zero = jnp.zeros_like(wv)
    rest = small[:, 3 * HD :]
    ext_ref[:, :128] = small[:, :128]
    ext_ref[:, 128:256] = jnp.concatenate(
        [-wq[:, turn:], wq[:, :turn], -wk[:, turn:], wk[:, :turn]], 1
    )
    value = jnp.concatenate([wv, zero], 1)
    ext_ref[:, 256:] = value
    head_ref[:, :128] = small[:, :128]
    head_ref[:, 128:] = value
    rest = jnp.concatenate([rest, zero], 1).astype(F32)
    router_ref[...] = jnp.where(lanes_of(rest) < E, rest, 0.0).astype(BF)
    turned = rest.T
    one_ref[...] = turned[E : E + 1, :]
    two_ref[...] = turned[E + 1 : E + 2, :]


def split_small(small):
    shapes = ((D, 384), (D, 256), (D, 128), (1, D), (1, D))
    types = (BF, BF, BF, F32, F32)
    return pl.pallas_call(
        split_kernel,
        out_shape=tuple(jax.ShapeDtypeStruct(s, t) for s, t in zip(shapes, types)),
        grid=(1,),
        in_specs=[fixed(small.shape)],
        out_specs=tuple(fixed(s) for s in shapes),
        compiler_params=params(),
        cost_estimate=cost(1, 3 * 2**20),
        name="split_weights",
    )(small)


def project(x_blk, w_ref, gain_ref, cosine, sine):
    x_f = x_blk.astype(F32)
    factor = lax.rsqrt(jnp.mean(x_f * x_f, axis=1, keepdims=True) + EPSILON)
    normed = (x_f * factor * gain_ref[...]).astype(BF)
    out = dot(normed, w_ref[...], 1, 0)
    both = out[:, :128] * cosine + out[:, 128:256] * sine
    swapped = pltpu.roll(both, 64, 1)
    low = lanes_of(both) < HD
    zero = jnp.zeros_like(both)
    return jnp.concatenate(
        [
            jnp.where(low, both, zero).astype(BF),
            jnp.where(low, swapped, zero).astype(BF),
            jnp.where(low, zero, swapped).astype(BF),
            out[:, 256:].astype(BF),
        ],
        axis=1,
    )


def spot_of(ids, block, block_len):
    return pl.ds(pl.multiple_of(ids[block] * block_len, block_len), block_len)


def head_kernel(
    block_len, band, ids, spots, firsts_ref,
    x_ref, w_ref, gain_ref, cos_ref, sin_ref, all_ref, log_ref, att_ref, a_store,
):
    step = pl.program_id(0)
    total = all_ref.shape[0]
    blocks = QUERY_BLOCK // block_len

    places = [spot_of(ids, 4 * step + j, block_len) for j in range(4)]
    cosine = jnp.concatenate([cos_ref[spot, :] for spot in places], 0)
    sine = jnp.concatenate([sin_ref[spot, :] for spot in places], 0)
    made = project(x_ref[...], w_ref, gain_ref, cosine, sine)
    for j in range(4):
        all_ref[places[j], :] = made[j * block_len : (j + 1) * block_len]

    @pl.when(step == pl.num_programs(0) - 1)
    def _():
        window = band + QUERY_BLOCK

        def step_fn(index, carry):
            first_key, first_query = window_of(index, band)
            rows = pl.ds(first_query, QUERY_BLOCK)
            cols = pl.ds(first_key, window)
            scores = masked_scores(
                all_ref[rows, :128], all_ref[cols, 128:256], first_key, first_query,
                firsts_ref[...],
            )
            top = jnp.max(scores, axis=1, keepdims=True)
            weight = jnp.exp(scores - top)
            mass = jnp.sum(weight, axis=1, keepdims=True)
            log_ref[rows, :] = top + jnp.log(mass)
            weight = (weight * (1.0 / mass)).astype(BF)
            result = dot(weight, all_ref[cols, 384:], 1, 0)
            for j in range(blocks):
                spot = spot_of(spots, index * blocks + j, block_len)
                a_store[spot, :] = result[j * block_len : (j + 1) * block_len]
            return carry

        lax.fori_loop(0, total // QUERY_BLOCK, step_fn, 0, unroll=total // QUERY_BLOCK <= 8)
        for j in range(total // QUERY_BLOCK):
            part = a_store[j * QUERY_BLOCK : (j + 1) * QUERY_BLOCK, :]
            att_ref[:, j * QUERY_BLOCK : (j + 1) * QUERY_BLOCK] = part.T[:HD].astype(BF)


def head_forward(hidden, w_ext, gain, tables, ids, spots, firsts, count, band):
    total = tables[0].shape[0]
    work = total * (band + QUERY_BLOCK)
    return pl.pallas_call(
        functools.partial(head_kernel, count // 2, band),
        out_shape=(
            jax.ShapeDtypeStruct((total, 512), BF),
            jax.ShapeDtypeStruct((total, 1), F32),
            jax.ShapeDtypeStruct((HD, total), BF),
        ),
        grid_spec=pltpu.PrefetchScalarGridSpec(
            num_scalar_prefetch=2,
            grid=(total // count // 2,),
            in_specs=[
                fixed((1, 128)),
                pl.BlockSpec((2 * count, D), lambda i, *_: (i, 0)),
                fixed((D, 384)), fixed((1, D)), fixed((total, 128)), fixed((total, 128)),
            ],
            out_specs=(fixed((total, 512)), fixed((total, 1)), fixed((HD, total))),
            scratch_shapes=[pltpu.VMEM((total, 128), F32)],
        ),
        compiler_params=params(),
        cost_estimate=cost(total * D * 384 + 4 * work * 128, 2 * total * D, work),
        name="head_forward",
    )(ids, spots, firsts, hidden, w_ext, gain, *tables)


def order_heads(heads, wo_ref, wo_rel):
    per = wo_ref.shape[1]
    many = HD // per
    for j in range(H):
        for m in range(many):
            wo_rel[j * HD + m * per : j * HD + (m + 1) * per, :] = wo_ref[heads[j] * many + m]


def back_kernel(
    part, tok_count, heads, where, att_ref, x_ref, g_ref, wo_ref, wgu_ref, wd_ref, wr_ref,
    gain_ref, act_ref, v_ref, pa_ref, pb_ref, grads_ref, mid_ref, wo_rel, gb_ref, norm_ref, acc, scr,
):
    step = pl.program_id(0)
    own_expert = where[0]
    half = D // 2

    @pl.when(step == 0)
    def _():
        order_heads(heads, wo_ref, wo_rel)
        norm_ref[...] = jnp.zeros_like(norm_ref)

    tile = x_ref.shape[0]
    moved = dot(att_ref[...].reshape(D, tile), wo_ref[...].reshape(D, D), 0, 0)
    middle = x_ref[...].astype(F32) + RESIDUAL_SCALE * moved
    scr[...] = middle

    @pl.when(step == where[2] * tok_count // tile)
    def _():
        own = pl.multiple_of(where[2] * tok_count % tile, tok_count)
        mid_ref[...] = scr[pl.ds(own, tok_count), :]

    gain = gain_ref[...]
    factor = lax.rsqrt(jnp.mean(middle * middle, axis=1, keepdims=True) + EPSILON)
    mixed = (middle * factor * gain).astype(BF)
    grads = g_ref[...].reshape(mixed.shape[0], D + 128)
    logits = dot(mixed, wr_ref[...], 1, 0)
    mask = grads[:, D:].astype(F32)
    logits = jnp.where(mask > 0.0, logits, NEGATIVE)
    odds = jnp.where(mask > 0.0, jnp.exp(logits - jnp.max(logits, axis=1, keepdims=True)), 0.0)
    combine = odds / jnp.sum(odds, axis=1, keepdims=True)
    mark = (lanes_of(combine) == own_expert).astype(F32)
    own_gate = jnp.sum(combine * mark, axis=1, keepdims=True)
    grad_top = grads[:, :D]
    pulled = RESIDUAL_SCALE * dot(grad_top, wd_ref[...], 1, 0)
    gates = dot(mixed, wgu_ref[...], 1, 0)
    gate, up = gates[:, :part], gates[:, part:]
    sigma = 1.0 / (1.0 + jnp.exp(-gate))
    silu = gate * sigma
    activation = silu * up
    grad_act = own_gate * pulled
    act = (RESIDUAL_SCALE * own_gate * activation).astype(BF)
    act_ref[...] = act
    gb_ref[:, :part] = (grad_act * up * sigma * (1.0 + gate * (1.0 - sigma))).astype(BF)
    gb_ref[:, part:] = (grad_act * silu).astype(BF)
    grad_combine = jnp.sum(activation * pulled, axis=1, keepdims=True)
    coef = (grad_combine * own_gate * (mark - combine)).astype(BF)
    terms = (
        (0, 2 * part, mixed, gb_ref[...]),
        (2 * part, 2 * part + 128, mixed, coef),
        (2 * part + 128, 3 * part + 128, grad_top, act),
    )

    @pl.when(step == 0)
    def _():
        for low, high, left, right in terms:
            acc[:, low:high] = dot(left, right, 0, 0)

    @pl.when(step > 0)
    def _():
        for low, high, left, right in terms:
            acc[:, low:high] += dot(left, right, 0, 0)

    grad_mixed = dot(gb_ref[...], wgu_ref[...], 1, 1) + dot(coef, wr_ref[...], 1, 1)
    scaled = scr[...] * factor
    norm_ref[...] += jnp.broadcast_to(
        jnp.sum(grad_mixed * scaled, axis=0, keepdims=True), norm_ref.shape
    )
    inner = grad_mixed * gain
    grad_mid = factor * (inner - scaled * jnp.mean(inner * scaled, axis=1, keepdims=True))
    grad_mid = grad_mid.astype(BF)
    v_ref[...] = grad_mid
    out_grads = dot(wo_rel[...], grad_mid, 1, 1)
    if part == F:
        top = out_grads[:HD] + dot(wo_rel[:HD, :], grad_top, 1, 1)
        pa_ref[:HD, :] = (RESIDUAL_SCALE * top).astype(BF)
        pa_ref[HD:, :] = (RESIDUAL_SCALE * out_grads[HD:half]).astype(BF)
    else:
        pa_ref[...] = (RESIDUAL_SCALE * out_grads[:half]).astype(BF)
    pb_ref[...] = (RESIDUAL_SCALE * out_grads[half:]).astype(BF)

    @pl.when(step == pl.num_programs(0) - 1)
    def _():
        middle = slice(2 * part, 2 * part + 128)
        last = acc[:, middle]
        grads_ref[:, : 2 * part] = acc[:, : 2 * part].astype(BF)
        grads_ref[:, middle] = jnp.where(lanes_of(last) == E, column_of(norm_ref), last).astype(BF)
        grads_ref[:, 2 * part + 128 :] = acc[:, 2 * part + 128 :].astype(BF)


def expert_main(att, hidden, top, wo, wgu, wd, wr, gain, heads, where, count):
    total = hidden.shape[0]
    part = wd.shape[1]
    tile = 2 * count
    width = 3 * part + 128

    def rows(size):
        return pl.BlockSpec((tile, size), lambda i, *_: (i, 0))

    def cols(height):
        return pl.BlockSpec((height, tile), lambda i, *_: (0, i))

    def out(size):
        return jax.ShapeDtypeStruct((total, size), BF)

    half = jax.ShapeDtypeStruct((D // 2, total), BF)
    return pl.pallas_call(
        functools.partial(back_kernel, part, count),
        out_shape=(
            out(part), out(D), half, half, jax.ShapeDtypeStruct((D, width), BF),
            jax.ShapeDtypeStruct((count, D), F32),
        ),
        grid_spec=pltpu.PrefetchScalarGridSpec(
            num_scalar_prefetch=2,
            grid=(total // tile,),
            in_specs=[
                pl.BlockSpec((H, HD, tile), lambda i, *_: (0, 0, i)),
                rows(D),
                pl.BlockSpec((2, count, D + 128), lambda i, *_: (i, 0, 0)),
                fixed(wo.shape), fixed((D, 2 * part)), fixed((D, part)), fixed((D, 128)),
                fixed((1, D)),
            ],
            out_specs=(
                rows(part), rows(D), cols(D // 2), cols(D // 2), fixed((D, width)),
                fixed((count, D)),
            ),
            scratch_shapes=[
                pltpu.VMEM((D, D), BF),
                pltpu.VMEM((tile, 2 * part), BF),
                pltpu.VMEM((8, D), F32),
                pltpu.VMEM((D, width), F32),
                pltpu.VMEM((tile, D), F32),
            ],
        ),
        compiler_params=params(),
        cost_estimate=cost(
            2 * total * D * (2 * D + 8 * part), 12 * total * D, total * part, weight=EXPERT_WEIGHT
        ),
        name="expert_main",
    )(heads, where, att, hidden, top, wo, wgu, wd, wr, gain)


def moe_kernel(act_ref, wd_ref, out_ref):
    out_ref[...] = dot(act_ref[...], wd_ref[...], 1, 1).astype(BF).reshape(out_ref.shape)


def moe_out(act, wd, count, rows):
    total, part = act.shape
    many = 4
    return pl.pallas_call(
        moe_kernel,
        out_shape=jax.ShapeDtypeStruct((total // count, count + 2 * rows, D), BF),
        grid=(total // count // many,),
        in_specs=[pl.BlockSpec((many * count, part), lambda i: (i, 0)), fixed((D, part))],
        out_specs=pl.BlockSpec((many, count, D), lambda i: (i, 0, 0)),
        compiler_params=params(),
        cost_estimate=cost(2 * total * D * part, 3 * total * D),
        name="moe_out",
    )(act, wd)


def output_kernel(where, att_ref, v_ref, g_ref, moe_ref, out_ref, acc):
    step = pl.program_id(0)
    tile = v_ref.shape[0]

    @pl.when(step == 0)
    def _():
        acc[...] = jnp.zeros_like(acc)

    acc[...] += dot(att_ref[...].reshape(D, tile), v_ref[...], 1, 0)
    picked = att_ref[where[0]]
    place = step * tile + lanes_of(picked)
    picked = jnp.where(place // where[3] == where[1], picked, jnp.zeros_like(picked))
    target = pl.ds(pl.multiple_of(where[0] * HD, HD), HD)
    acc[target, :] += dot(picked, g_ref[...].reshape(tile, D), 1, 0)

    @pl.when(step == pl.num_programs(0) - 1)
    def _():
        out_ref[...] = (RESIDUAL_SCALE * acc[...]).astype(BF).reshape(out_ref.shape)


def output_weights(att, grad_mid, top, moe, where, count, rows):
    total = grad_mid.shape[0]
    tile = 4 * count
    per = 2 * rows
    return pl.pallas_call(
        output_kernel,
        out_shape=jax.ShapeDtypeStruct(moe.shape, BF),
        grid_spec=pltpu.PrefetchScalarGridSpec(
            num_scalar_prefetch=1,
            grid=(total // tile,),
            in_specs=[
                pl.BlockSpec((H, HD, tile), lambda i, *_: (0, 0, i)),
                pl.BlockSpec((tile, D), lambda i, *_: (i, 0)),
                pl.BlockSpec((4, count, D), lambda i, *_: (i, 0, 0)),
                pl.BlockSpec(memory_space=pl.ANY),
            ],
            out_specs=fixed((moe.shape[0], per, D), (0, count // per, 0)),
            scratch_shapes=[pltpu.VMEM((D, D), F32)],
        ),
        input_output_aliases={4: 0},
        compiler_params=params(),
        cost_estimate=cost(2 * total * D * D, 8 * total * D),
        name="output_weights",
    )(where, att, grad_mid, top, moe)


def attend_kernel(
    block_len, band, ids, spots, where, firsts_ref, all_ref, up_ref, log_ref, cos_ref, sin_ref,
    own_ref, up_sort, acc_qk, acc_v,
):
    total = all_ref.shape[0]
    blocks = QUERY_BLOCK // block_len
    window = band + QUERY_BLOCK
    acc_qk[...] = jnp.zeros_like(acc_qk)
    acc_v[...] = jnp.zeros_like(acc_v)
    for j in range(total // QUERY_BLOCK):
        piece = up_ref[:, j * QUERY_BLOCK : (j + 1) * QUERY_BLOCK]
        piece = jnp.concatenate([piece, jnp.zeros_like(piece)], 0).T.astype(BF)
        for m in range(blocks):
            spot = spot_of(ids, j * blocks + m, block_len)
            up_sort[spot, :] = piece[m * block_len : (m + 1) * block_len]

    def step_fn(index, carry):
        first_key, first_query = window_of(index, band)
        rows = pl.ds(first_query, QUERY_BLOCK)
        cols = pl.ds(first_key, window)
        keys_win, upstream = all_ref[cols, 128:256], up_sort[rows, :]
        scores = masked_scores(
            all_ref[rows, :128], keys_win, first_key, first_query, firsts_ref[...]
        )
        weight = jnp.exp(scores - log_ref[rows, :])
        grad_weight = dot(upstream, all_ref[cols, 384:], 1, 1)
        delta = jnp.sum(weight * grad_weight, axis=1, keepdims=True)
        grad_raw = (SCORE_SCALE * weight * (grad_weight - delta)).astype(BF)
        acc_qk[rows, :] += dot(grad_raw, keys_win, 1, 0)
        acc_qk[cols, :] += dot(grad_raw, all_ref[rows, 256:384], 0, 0)
        acc_v[cols, :] += dot(weight.astype(BF), upstream, 0, 0)
        return carry

    short = total // QUERY_BLOCK <= 8
    lax.fori_loop(0, total // QUERY_BLOCK, step_fn, 0, unroll=short)

    def turn(index, carry):
        first = pl.multiple_of(index * QUERY_BLOCK, QUERY_BLOCK)
        rows = pl.ds(first, QUERY_BLOCK)
        both = acc_qk[rows, :]
        low = lanes_of(both) % HD < HD // 2
        swapped = jnp.where(low, pltpu.roll(both, 96, 1), -pltpu.roll(both, 32, 1))
        turned = (both * cos_ref[rows, :] + swapped * sin_ref[rows, :]).astype(BF)
        made = jnp.concatenate([turned, acc_v[rows, :].astype(BF)], 1)
        for j in range(blocks):
            block = spots[index * blocks + j]
            first = pl.multiple_of(block * block_len, block_len)
            piece = made[j * block_len : (j + 1) * block_len]
            keep = first // where[3] == where[1]
            own_ref[pl.ds(first, block_len), :] = jnp.where(keep, piece, jnp.zeros_like(piece))
        return carry

    lax.fori_loop(0, total // QUERY_BLOCK, turn, 0, unroll=short)


def attend_backward(heads_all, upstream, logs, tables, ids, spots, firsts, where, count, band):
    total = heads_all.shape[0]
    work = total * (band + QUERY_BLOCK)
    return pl.pallas_call(
        functools.partial(attend_kernel, count // 2, band),
        out_shape=jax.ShapeDtypeStruct((total, 256), BF),
        grid_spec=pltpu.PrefetchScalarGridSpec(
            num_scalar_prefetch=3,
            grid=(1,),
            in_specs=[
                fixed((1, 128)),
                fixed((total, 512)), fixed((HD, total)), fixed((total, 1)), fixed((total, 128)),
                fixed((total, 128)),
            ],
            out_specs=fixed((total, 256)),
            scratch_shapes=[
                pltpu.VMEM((total, 128), BF),
                pltpu.VMEM((total, 128), F32),
                pltpu.VMEM((total, 128), F32),
            ],
        ),
        compiler_params=params(60),
        cost_estimate=cost(10 * work * 128, 2 * total * 1024, work),
        name="attend_backward",
    )(ids, spots, where, firsts, heads_all, upstream, logs, *tables)


def pull_kernel(
    last, order, every, g_ref, h_ref, w_ref, gain_ref, x_ref, y_ref, gm_ref, hm_ref, *refs
):
    out_ref, w_out_ref, n_out_ref, acc_w = refs[-4:]
    step = pl.program_id(0)

    @pl.when(step == 0)
    def _():
        if last:
            acc_w[...] = refs[0][...]
            n_out_ref[...] = refs[1][...]
        else:
            acc_w[...] = jnp.zeros_like(acc_w)
            n_out_ref[...] = jnp.zeros_like(n_out_ref)

    grads = jnp.concatenate([g_ref[...], h_ref[...]], 0)
    grad_mid = jnp.concatenate([gm_ref[...], hm_ref[...]], 0).astype(F32)
    grad_normed = dot(grads, w_ref[...], 1, 1)
    x_f = jnp.concatenate([x_ref[...], y_ref[...]], 0).astype(F32)
    factor = lax.rsqrt(jnp.mean(x_f * x_f, axis=1, keepdims=True) + EPSILON)
    scaled = x_f * factor
    normed = (scaled * gain_ref[...]).astype(BF)
    acc_w[...] += dot(normed, grads, 0, 0)
    n_out_ref[...] += jnp.broadcast_to(
        jnp.sum(grad_normed * scaled, axis=0, keepdims=True), n_out_ref.shape
    )
    inner = grad_normed * gain_ref[...]
    grad_x = factor * (inner - scaled * jnp.mean(inner * scaled, axis=1, keepdims=True))
    out_ref[...] = (grad_x + grad_mid).astype(BF)

    @pl.when(step == pl.num_programs(0) - 1)
    def _():
        if last:
            tail = acc_w[:, 128:]
            acc_w[:, 128:] = jnp.where(lanes_of(tail) == HD, column_of(n_out_ref), tail)
            places = every.shape[0]
            size = acc_w.shape[0] // places
            for j in range(places):
                first = pl.multiple_of(every[j] * size, size)
                w_out_ref[j * size : (j + 1) * size, :] = acc_w[pl.ds(first, size), :].astype(BF)
        else:
            w_out_ref[...] = acc_w[...]


def pull_heads(
    own_grads, w_head, gain, hidden, grad_mid, before, order, every, count
):
    last = len(before) > 0
    total = hidden.shape[0] // 2

    def at(width, j):
        return pl.BlockSpec((count, width), lambda i, order, _: (order[2 * i + j], 0))

    block = pl.BlockSpec((2 * count, D), lambda i, *_: (i, 0))
    return pl.pallas_call(
        functools.partial(pull_kernel, last),
        out_shape=(
            jax.ShapeDtypeStruct((total, D), BF),
            jax.ShapeDtypeStruct((D, 256), BF if last else F32),
            jax.ShapeDtypeStruct((8, D), F32),
        ),
        grid_spec=pltpu.PrefetchScalarGridSpec(
            num_scalar_prefetch=2,
            grid=(total // count // 2,),
            in_specs=[
                at(256, 0), at(256, 1), fixed((D, 256)), fixed((1, D)), at(D, 0), at(D, 1), at(D, 0),
                at(D, 1),
                *(fixed(item.shape) for item in before),
            ],
            out_specs=(block, fixed((D, 256)), fixed((8, D))),
            scratch_shapes=[pltpu.VMEM((D, 256), F32)],
        ),
        compiler_params=params(),
        cost_estimate=cost(4 * total * D * 256, 6 * total * D, weight=1),
        name="pull_last" if last else "pull_first",
    )(
        order, every, own_grads, own_grads, w_head, gain, hidden, hidden, grad_mid, grad_mid,
        *before,
    )


def finish_kernel(places, *refs):
    q_ref, k_ref, v_ref, gain_ref, scr = refs[4:]
    for j in range(16):
        scr[places[j]] = refs[j // 4][j % 4].astype(F32)
    total = jnp.zeros_like(scr[0])
    for quad in range(H // 4):
        heads = [scr[4 * quad + j] for j in range(4)]
        for j in range(2):
            first = (4 * quad + 2 * j) * HD
            q_ref[:, first : first + 128] = jnp.concatenate(
                [heads[2 * j][:, :HD], heads[2 * j + 1][:, :HD]], 1
            )
        pairs = [heads[0] + heads[1], heads[2] + heads[3]]
        total = total + pairs[0] + pairs[1]
        for ref, low in ((k_ref, HD), (v_ref, 2 * HD)):
            ref[:, quad * 128 : (quad + 1) * 128] = jnp.concatenate(
                [pair[:, low : low + HD] for pair in pairs], 1
            )
    gain_ref[...] = total[:, 128:]


def finish_heads(places, pieces):
    rows = pieces[0].shape[1]
    shapes = ((rows, D), (rows, D // 2), (rows, D // 2), (rows, 128))
    return pl.pallas_call(
        finish_kernel,
        out_shape=tuple(jax.ShapeDtypeStruct(shape, F32) for shape in shapes),
        grid_spec=pltpu.PrefetchScalarGridSpec(
            num_scalar_prefetch=1,
            grid=(1,),
            in_specs=[fixed(piece.shape) for piece in pieces],
            out_specs=tuple(fixed(shape) for shape in shapes),
            scratch_shapes=[pltpu.VMEM((16, rows, 256), F32)],
        ),
        compiler_params=params(),
        cost_estimate=cost(1, 2**20),
        name="finish_heads",
    )(places, *pieces)


def finish_kernel_experts(in_ref, up_ref, down_ref, tail_ref):
    many = in_ref.shape[0]
    wide, narrow = up_ref.shape[1] // many, down_ref.shape[1] // many
    for j in range(many):
        up_ref[:, j * wide : (j + 1) * wide] = in_ref[j, :, :wide].astype(F32)
        down_ref[:, j * narrow : (j + 1) * narrow] = in_ref[j, :, wide + 128 :].astype(F32)

    @pl.when(pl.program_id(0) == 0)
    def _():
        tail_ref[...] = jnp.zeros_like(tail_ref)

    for j in range(many):
        tail_ref[...] += in_ref[j, :, wide : wide + 128].astype(F32)


def finish_experts(arrived):
    places, rows, width = arrived.shape
    part = (width - 128) // 3
    return pl.pallas_call(
        finish_kernel_experts,
        out_shape=(
            jax.ShapeDtypeStruct((rows, places * 2 * part), F32),
            jax.ShapeDtypeStruct((rows, places * part), F32),
            jax.ShapeDtypeStruct((rows, 128), F32),
        ),
        grid=(places // 4,),
        in_specs=[pl.BlockSpec((4, rows, width), lambda i: (i, 0, 0))],
        out_specs=(
            pl.BlockSpec((rows, 8 * part), lambda i: (0, i)),
            pl.BlockSpec((rows, 4 * part), lambda i: (0, i)),
            fixed((rows, 128)),
        ),
        compiler_params=params(),
        cost_estimate=cost(1, 5 * 2**20),
        name="finish_experts",
    )(arrived)


def per_device(
    hidden_in,
    out_grad,
    doc_lengths,
    block_order,
    routes,
    attn_norm,
    w_query,
    w_key,
    w_value,
    w_output,
    ffn_norm,
    w_router,
    w_gate_up,
    w_down,
):
    ctx_count = lax.axis_size("ctx")
    ctx_place = lax.axis_index("ctx")
    fsdp_place = lax.axis_index("fsdp")
    copies = ctx_count // E
    own_expert, own_copy = ctx_place // copies, ctx_place % copies
    tok_count = hidden_in.shape[1]
    seq_len = tok_count * ctx_count
    block_len = tok_count // 2
    band = seq_len // 4
    rows = attn_norm.shape[0]
    part = F // copies
    groups = H // KVH
    share = seq_len // copies
    swap_y = [(0, 1), (1, 0)]
    alone = copies == 1

    def swap_fsdp(mine):
        return lax.ppermute(mine, "fsdp", swap_y)

    def both_rows(mine):
        theirs = swap_fsdp(mine)
        stacked = jnp.where(
            fsdp_place == 0, jnp.stack([mine, theirs], 1), jnp.stack([theirs, mine], 1)
        )
        return stacked.reshape(-1, mine.shape[-1])

    def exchange(split):
        return lax.all_to_all(split, "ctx", 0, 0, tiled=True)

    ids = block_order[0]
    block_ids = jnp.arange(ids.shape[0], dtype=jnp.int32)
    spots = jnp.sum(jnp.where(ids[None, :] == block_ids[:, None], block_ids[None, :], 0), axis=1)
    lengths = doc_lengths[0]
    doc_ids = jnp.arange(lengths.shape[0], dtype=jnp.int32)
    firsts = jnp.sum(
        jnp.where(doc_ids[None, :] < doc_ids[:, None], lengths[None, :], 0), axis=1
    )
    firsts = jnp.pad(firsts[None], ((0, 0), (0, 128 - lengths.shape[0])))
    tables = tables_of(seq_len)
    order, heads = block_order_of(ctx_count), block_order_of(E)
    where = jnp.stack([own_expert, own_copy, ctx_place, jnp.int32(share)]).astype(jnp.int32)

    def by_expert(weight, pieces):
        split = weight.reshape(rows, E, pieces, copies, part)
        return split.transpose(1, 3, 0, 2, 4).reshape(ctx_count, rows, pieces * part)

    chosen_mask = jnp.any(
        routes[0][:, :, None] == jnp.arange(E, dtype=jnp.int32)[None, None, :], axis=1
    ).astype(BF)
    grads_own = jnp.concatenate(
        [out_grad[0], chosen_mask, jnp.zeros((tok_count, 128 - E), BF)], axis=1
    )
    experts = jnp.concatenate([by_expert(w_gate_up, 2), by_expert(w_down, 1)], axis=2)
    norms = jnp.stack([attn_norm, ffn_norm], 1)
    if alone:
        small_here = exchange(pack_small(copies, w_query, w_key, w_value, w_router, norms))
        w_ext, w_head, router_full, gain_one, gain_two = split_small(both_rows(small_here))
        near = Gather(hidden_in[0])
        near.cross()
        near.last(small_here)
        experts_here = exchange(after(experts, near.two))
        hidden_all = near.join(order, "join_hidden", w_ext).reshape(seq_len, D)
    else:
        small_here = exchange(pack_small(copies, w_query, w_key, w_value, w_router, norms))
        w_ext, w_head, router_full, gain_one, gain_two = split_small(both_rows(small_here))
        hidden_all = lax.all_gather(hidden_in[0], "ctx", axis=0, tiled=True)
        experts_here = exchange(experts)
    out_all = lax.all_gather(w_output, BOTH, axis=0, tiled=True).reshape(ctx_count, 2 * rows, D)
    top_all = lax.all_gather(grads_own[None], "ctx", axis=0, tiled=True)

    heads_all, logs, attended = head_forward(
        hidden_all, w_ext, gain_one, tables, ids, spots, firsts, tok_count, band
    )
    def half_rows(mine, theirs):
        stacked = jnp.where(
            fsdp_place == 0, jnp.stack([mine, theirs], 1), jnp.stack([theirs, mine], 1)
        )
        return stacked.reshape(D, mine.shape[-1])

    if alone:
        att = Gather(attended)
        experts_here = after(experts_here, att.one, att.three)
    gu_here, dn_here = experts_here[:, :, : 2 * part], experts_here[:, :, 2 * part :]
    gu_there, dn_there = swap_fsdp(gu_here), swap_fsdp(dn_here)
    w_gu, w_dn = half_rows(gu_here, gu_there), half_rows(dn_here, dn_there)
    if alone:
        att.cross()
        att.last(experts_here)
        att_all = att.join(heads, "join_heads", w_gu)
    else:
        sent = lax.dynamic_slice_in_dim(attended, own_copy * share, share, 1)
        att_all = lax.all_gather(sent, "ctx", axis=0, tiled=True)
        att_all = att_all.reshape(H, copies, HD, share).transpose(0, 2, 1, 3)
        att_all = att_all.reshape(H, HD, seq_len)

    act, grad_mid, pull_a, pull_b, grads_expert, middle = expert_main(
        att_all, hidden_all, top_all, out_all, w_gu, w_dn, router_full, gain_two, heads, where,
        tok_count,
    )

    def given_rows(grads):
        by_owner = grads.reshape(ctx_count, 2, rows, grads.shape[1])
        return by_owner, lax.dynamic_index_in_dim(by_owner, 1 - fsdp_place, 1, keepdims=False)

    def to_owner(by_owner, theirs):
        kept = lax.dynamic_index_in_dim(by_owner, fsdp_place, 1, keepdims=False)
        return (kept.astype(F32) + theirs.astype(F32)).astype(BF)

    owner, given = given_rows(grads_expert)
    theirs = swap_fsdp(given)
    mid_late = grad_mid
    if alone:
        ring = RingSum(pull_a, permute(pull_b, SWAP_CORE))
        mid_late = after(grad_mid, ring.cross_out)
    moe = moe_out(act, w_dn, tok_count, rows)
    out_both = output_weights(
        att_all, mid_late, top_all, moe, where, tok_count, rows
    )
    if alone:
        ring.cross()
        out_both = after(out_both, *ring.sends)
    if alone:
        upstream = ring.end()
    else:
        joined = jnp.concatenate([pull_a, pull_b], 0)
        pulled = lax.psum_scatter(joined, "ctx", scatter_dimension=0, tiled=True)
        rings = [[i * copies + j for j in range(copies)] for i in range(E)]
        pulled = lax.all_gather(pulled, "ctx", axis=0, tiled=True, axis_index_groups=rings)
        own_out = lax.dynamic_slice_in_dim(out_all.reshape(D, D), own_expert * HD, HD, 0)
        top_rows = top_all[:, :, :D].reshape(seq_len, D)
        upstream = pulled.astype(F32) + RESIDUAL_SCALE * dot(own_out, top_rows, 1, 1)
    if alone:
        theirs = after(theirs, upstream)
    grads_all_expert = to_owner(owner, theirs)

    own_grads = attend_backward(
        heads_all, upstream, logs, tables, ids, spots, firsts, where, tok_count, band
    )
    experts_in = exchange(grads_all_expert)
    grad_b, *sums = pull_heads(
        own_grads, w_head, gain_one, hidden_all, grad_mid, (), order[ctx_count // 2 :], order,
        tok_count,
    )
    grad_a, grad_heads, ignored = pull_heads(
        own_grads, w_head, gain_one, hidden_all, grad_mid, sums, order[: ctx_count // 2], order,
        tok_count,
    )
    if alone:
        by_owner = grad_heads.reshape(ctx_count, 2, rows, 256)
        kept = lax.dynamic_index_in_dim(by_owner, fsdp_place, 1, keepdims=False)
        given = lax.dynamic_index_in_dim(by_owner, 1 - fsdp_place, 1, keepdims=False)
        theirs = swap_fsdp(given)
        ring = RingSum(grad_a, permute(grad_b, SWAP_CORE))
        ring.cross()
        theirs = after(theirs, *ring.sends)
        tail_sum = (kept.astype(F32) + theirs.astype(F32)).astype(BF)
        experts_in = after(experts_in, *ring.sends)
    else:
        joined = jnp.concatenate([grad_a, grad_b], 0)
        grad_own = lax.psum_scatter(joined, "ctx", scatter_dimension=0, tiled=True).astype(F32)
    def from_experts(block, pieces):
        block = block[:, :, : pieces * part].astype(F32)
        block = block.reshape(E, copies, rows, pieces, part).transpose(2, 0, 3, 1, 4)
        return block.reshape(rows, E * pieces * F)

    if alone:
        share_gate_up, share_down, tail = finish_experts(experts_in)
    else:
        gu_in = experts_in[:, :, : 2 * part + 128]
        dn_in = experts_in[:, :, 2 * part + 128 :]
        share_gate_up = from_experts(gu_in, 2)
        share_down = from_experts(dn_in, 1)
        tail = jnp.sum(gu_in[:, :, 2 * part :].astype(F32), axis=0)
    share_router = tail[:, :E]
    share_gain_two = tail[:, E]
    out_own = lax.psum_scatter(out_both, "ctx", scatter_dimension=0, tiled=False).astype(F32)
    hidden_out = (middle + out_own[:tok_count]).astype(BF)
    out_rows = out_own[tok_count:].reshape(2, rows, D)
    mine = lax.dynamic_index_in_dim(out_rows, fsdp_place, 0, keepdims=False)
    theirs = lax.dynamic_index_in_dim(out_rows, 1 - fsdp_place, 0, keepdims=False)
    share_output = mine + swap_fsdp(theirs)

    if alone:
        grad_own = ring.end(share_output, hidden_out, share_gate_up)
    grad_in = out_grad[0].astype(F32) + grad_own
    if alone:
        pieces = spread_ctx(tail_sum)
        share_query, share_key, share_value, gain_sum = finish_heads(sender_order_of(), pieces)
        share_gain_one = gain_sum[:, HD]
    else:
        tail_in = lax.all_to_all(
            grad_heads.reshape(2 * ctx_count, rows, 256), BOTH, 0, 0, tiled=True
        )
        tail_in = tail_in.astype(F32).reshape(H, copies * 2, rows, 256)
        heads_in = jnp.sum(tail_in[..., : 3 * HD], axis=1)
        share_query = heads_in[:, :, :HD].transpose(1, 0, 2).reshape(rows, H * HD)
        pairs_in = heads_in[:, :, HD:].reshape(KVH, groups, rows, 2, HD).sum(1)
        share_key = pairs_in[:, :, 0].transpose(1, 0, 2).reshape(rows, KVH * HD)
        share_value = pairs_in[:, :, 1].transpose(1, 0, 2).reshape(rows, KVH * HD)
        share_gain_one = jnp.sum(tail_in[..., 3 * HD], axis=(0, 1))
    return (
        hidden_out[None],
        grad_in[None],
        share_gain_one,
        share_query,
        share_key,
        share_value,
        share_output,
        share_gain_two,
        share_router,
        share_gate_up,
        share_down,
    )


def solution(mesh):
    return jax.shard_map(
        per_device,
        mesh=mesh,
        in_specs=(
            P("fsdp", "ctx", None),
            P("fsdp", "ctx", None),
            P("fsdp", None),
            P("fsdp", None),
            P("fsdp", "ctx", None),
            P(BOTH),
            P(BOTH, None),
            P(BOTH, None),
            P(BOTH, None),
            P(BOTH, None),
            P(BOTH),
            P(BOTH, None),
            P(BOTH, None),
            P(BOTH, None),
        ),
        out_specs=(
            P("fsdp", "ctx", None),
            P("fsdp", "ctx", None),
            P(BOTH),
            P(BOTH, None),
            P(BOTH, None),
            P(BOTH, None),
            P(BOTH, None),
            P(BOTH),
            P(BOTH, None),
            P(BOTH, None),
            P(BOTH, None),
        ),
        check_vma=False,
    )
```

```python
import functools

import jax
import jax.numpy as jnp
import numpy as np
from jax import lax
from jax.experimental import pallas as pl
from jax.experimental.pallas import tpu as pltpu
from jax.sharding import PartitionSpec as P

D = 1024
H = 16
KVH = 8
HD = 64
F = 512
E = 16

EPSILON = 1e-06
SCORE_SCALE = 0.015625
RESIDUAL_SCALE = 0.22
THETA = 10000.0
NEGATIVE = -1e30
BOTH = ("ctx", "fsdp")
EXPERT_WEIGHT = 2
BF = jnp.bfloat16
F32 = jnp.float32
QUERY_BLOCK = 256


def dot(left, right, left_dim, right_dim):
    return lax.dot_general(
        left, right, (((left_dim,), (right_dim,)), ((), ())), preferred_element_type=F32
    )


def permute(values, pairs):
    return lax.ppermute(values, "ctx", pairs)


def shift_z(step):
    return [(i, ((i // 4 + step) % 4) * 4 + i % 4) for i in range(16)]


SWAP_X = [(i, i ^ 2) for i in range(16)]
SWAP_CORE = [(i, i ^ 1) for i in range(16)]


def after(value, *others):
    return lax.optimization_barrier((value, *others))[0] if others else lax.optimization_barrier(value)


def block_order_of(count):
    index = jnp.arange(count, dtype=jnp.int32)
    if lax.axis_size("ctx") != 16:
        return index
    place = lax.axis_index("ctx")
    z_of = (place // 4 - (index % 8) // 2 + 4) % 4
    x_of = ((place // 2) % 2 + index % 2) % 2
    return z_of * 4 + x_of * 2 + (place % 2 + index // 8) % 2


class RingSum:
    def __init__(self, mine, arrived):
        self.mine, self.arrived = mine, arrived
        self.count = mine.shape[0] // 8
        self.cross_out = jnp.concatenate([self.chip(k, 1) for k in (2, 1, 3)], 0).astype(BF)

    def chip(self, k, dx):
        rows = slice((2 * k + dx) * self.count, (2 * k + dx + 1) * self.count)
        return self.mine[rows].astype(F32) + self.arrived[rows].astype(F32)

    def cross(self):
        got = permute(self.cross_out, SWAP_X)
        self.sends = []
        for j, k in enumerate((2, 1, 3)):
            term = got[j * self.count : (j + 1) * self.count].astype(F32)
            self.sends.append((self.chip(k, 0) + term).astype(BF))

    def end(self, *others):
        self.own = permute(self.chip(0, 1).astype(BF), SWAP_X)
        total = self.chip(0, 0) + self.own.astype(F32)
        for send, k in zip(self.sends, (2, 1, 3)):
            term = permute(send, shift_z(4 - k))
            self.seen = term
            if k == 2 and others:
                term = after(term, *others)
            total = total + term.astype(F32)
        return total


def join_kernel(places, *refs):
    pieces, out_ref, sems = refs[:14], refs[14], refs[15]
    count = out_ref.shape[1]
    copies = []
    for side in range(2):
        own, far, one, pair, two, far_two, three = pieces[7 * side : 7 * side + 7]
        lower, upper = pair.at[:count], pair.at[count:]
        for j, piece in enumerate((own, far, one, lower, two, far_two, three, upper)):
            block = 8 * side + j
            copies.append(
                pltpu.make_async_copy(piece, out_ref.at[places[block]], sems.at[block])
            )
    for copy in copies:
        copy.start()
    for copy in copies:
        copy.wait()


def spread_ctx(blocks):
    _, rows, width = blocks.shape
    other = permute(blocks[8:], SWAP_CORE)
    chip = jnp.stack([blocks[:8], other], 1).reshape(4, 2, 2, rows, width)
    crossed = permute(chip[:, 1], SWAP_X)
    both = jnp.concatenate([chip[:, 0], crossed], 1)
    return (both[0], *(permute(both[k], shift_z(4 - k)) for k in range(1, 4)))


def sender_order_of():
    place = lax.axis_index("ctx")
    index = jnp.arange(16, dtype=jnp.int32)
    z_of = (place // 4 + index // 4) % 4
    x_of = ((place // 2) % 2 + (index // 2) % 2) % 2
    return z_of * 4 + x_of * 2 + (place % 2 + index % 2) % 2


class Gather:
    def __init__(self, rows):
        self.count = rows.shape[0]
        self.own = rows
        self.one = permute(rows, shift_z(1))
        self.three = permute(rows, shift_z(3))
        self.far = permute(rows, SWAP_X)
        self.two = permute(rows, shift_z(2))

    def cross(self, *others):
        if others:
            self.one, self.three = after((self.one, self.three), *others)
        self.pair = permute(jnp.concatenate([self.one, self.three], 0), SWAP_X)

    def last(self, *others):
        if others:
            self.two = after(self.two, *others)
        self.far_two = permute(self.two, SWAP_X)

    def join(self, places, name, *others):
        if others:
            self.far, self.far_two = after((self.far, self.far_two), *others)
        mine = (self.own, self.far, self.one, self.pair, self.two, self.far_two, self.three)
        other = tuple(permute(piece, SWAP_CORE) for piece in mine)
        shape = (16, *self.own.shape)
        return pl.pallas_call(
            join_kernel,
            out_shape=jax.ShapeDtypeStruct(shape, BF),
            grid_spec=pltpu.PrefetchScalarGridSpec(
                num_scalar_prefetch=1,
                grid=(1,),
                in_specs=[fixed(piece.shape) for piece in (*mine, *other)],
                out_specs=pl.BlockSpec(memory_space=pl.ANY),
                scratch_shapes=[pltpu.SemaphoreType.DMA((16,))],
            ),
            compiler_params=params(),
            cost_estimate=cost(1, 4 * self.own.size * 16),
            name=name,
        )(places, *mine, *other)


def tables_of(total):
    half_width = HD // 2
    frequency = (THETA ** (-np.arange(half_width) / half_width)).astype(np.float32)
    angles = np.arange(total, dtype=np.float32)[:, None] * frequency[None, :]
    cosine = np.cos(angles.astype(np.float64)).astype(np.float32)
    sine = np.sin(angles.astype(np.float64)).astype(np.float32)
    return jnp.asarray(np.tile(cosine, (1, 4))), jnp.asarray(np.tile(sine, (1, 4)))


def window_of(step, band):
    start = jnp.maximum(step * QUERY_BLOCK - band, 0)
    return pl.multiple_of(start, QUERY_BLOCK), pl.multiple_of(step * QUERY_BLOCK, QUERY_BLOCK)


def masked_scores(queries, keys_win, first_key, first_query, firsts):
    raw = dot(queries, keys_win, 1, 1) * SCORE_SCALE
    key_place = first_key + lax.broadcasted_iota(jnp.int32, raw.shape, 1)
    query_place = first_query + lax.broadcasted_iota(jnp.int32, raw.shape, 0)
    column = first_query + lax.broadcasted_iota(jnp.int32, (raw.shape[0], 1), 0)
    start = jnp.zeros_like(column)
    for j in range(1, firsts.shape[0]):
        start = jnp.where(firsts[j] <= column, jnp.maximum(start, firsts[j]), start)
    visible = (key_place <= query_place) & (key_place >= start)
    return jnp.where(visible, raw, NEGATIVE)


def lanes_of(values):
    return lax.broadcasted_iota(jnp.int32, values.shape, 1)


def fixed(shape, at=None):
    place = (0,) * len(shape) if at is None else at
    return pl.BlockSpec(shape, lambda *_: place, pipeline_mode=pl.Buffered(1))


def params(mib=56):
    return pltpu.CompilerParams(vmem_limit_bytes=mib * 2**20)


def cost(flops, bytes_accessed, transcendentals=0, weight=20):
    return pl.CostEstimate(
        flops=weight * flops,
        bytes_accessed=weight * bytes_accessed,
        transcendentals=transcendentals,
    )


def column_of(row_ref):
    return jnp.broadcast_to(row_ref[:1, :], (128, row_ref.shape[1])).T


def pack_kernel(copies, wq_ref, wk_ref, wv_ref, wr_ref, norm_ref, small_ref):
    rows = wq_ref.shape[0]
    rest = jnp.concatenate(
        [wr_ref[...], norm_ref[...], jnp.zeros((rows, HD - E - 2), BF)], axis=1
    )
    for place in range(E * copies):
        head = place // copies
        pair = head // (H // KVH)
        query = wq_ref[:, head * HD : (head + 1) * HD]
        key = wk_ref[:, pair * HD : (pair + 1) * HD]
        value = wv_ref[:, pair * HD : (pair + 1) * HD]
        small_ref[place] = jnp.concatenate([query, key, value, rest], axis=1)


def pack_small(copies, *weights):
    shape = (E * copies, weights[0].shape[0], 256)
    return pl.pallas_call(
        functools.partial(pack_kernel, copies),
        out_shape=jax.ShapeDtypeStruct(shape, BF),
        grid=(1,),
        in_specs=[fixed(weight.shape) for weight in weights],
        out_specs=fixed(shape),
        compiler_params=params(),
        cost_estimate=cost(1, 2**20),
        name="pack_small",
    )(*weights)


def split_kernel(small_ref, ext_ref, head_ref, router_ref, one_ref, two_ref):
    small = small_ref[...]
    wq, wk, wv = (small[:, j * HD : (j + 1) * HD] for j in range(3))
    turn = HD // 2
    zero = jnp.zeros_like(wv)
    rest = small[:, 3 * HD :]
    ext_ref[:, :128] = small[:, :128]
    ext_ref[:, 128:256] = jnp.concatenate(
        [-wq[:, turn:], wq[:, :turn], -wk[:, turn:], wk[:, :turn]], 1
    )
    value = jnp.concatenate([wv, zero], 1)
    ext_ref[:, 256:] = value
    head_ref[:, :128] = small[:, :128]
    head_ref[:, 128:] = value
    rest = jnp.concatenate([rest, zero], 1).astype(F32)
    router_ref[...] = jnp.where(lanes_of(rest) < E, rest, 0.0).astype(BF)
    turned = rest.T
    one_ref[...] = turned[E : E + 1, :]
    two_ref[...] = turned[E + 1 : E + 2, :]


def split_small(small):
    shapes = ((D, 384), (D, 256), (D, 128), (1, D), (1, D))
    types = (BF, BF, BF, F32, F32)
    return pl.pallas_call(
        split_kernel,
        out_shape=tuple(jax.ShapeDtypeStruct(s, t) for s, t in zip(shapes, types)),
        grid=(1,),
        in_specs=[fixed(small.shape)],
        out_specs=tuple(fixed(s) for s in shapes),
        compiler_params=params(),
        cost_estimate=cost(1, 3 * 2**20),
        name="split_weights",
    )(small)


def project(x_blk, w_ref, gain_ref, cosine, sine):
    x_f = x_blk.astype(F32)
    factor = lax.rsqrt(jnp.mean(x_f * x_f, axis=1, keepdims=True) + EPSILON)
    normed = (x_f * factor * gain_ref[...]).astype(BF)
    out = dot(normed, w_ref[...], 1, 0)
    both = out[:, :128] * cosine + out[:, 128:256] * sine
    swapped = pltpu.roll(both, 64, 1)
    low = lanes_of(both) < HD
    zero = jnp.zeros_like(both)
    return jnp.concatenate(
        [
            jnp.where(low, both, zero).astype(BF),
            jnp.where(low, swapped, zero).astype(BF),
            jnp.where(low, zero, swapped).astype(BF),
            out[:, 256:].astype(BF),
        ],
        axis=1,
    )


def spot_of(ids, block, block_len):
    return pl.ds(pl.multiple_of(ids[block] * block_len, block_len), block_len)


def head_kernel(
    block_len, band, ids, spots, firsts,
    x_ref, w_ref, gain_ref, cos_ref, sin_ref, all_ref, log_ref, att_ref, a_store,
):
    step = pl.program_id(0)
    total = all_ref.shape[0]
    blocks = QUERY_BLOCK // block_len

    places = [spot_of(ids, 4 * step + j, block_len) for j in range(4)]
    cosine = jnp.concatenate([cos_ref[spot, :] for spot in places], 0)
    sine = jnp.concatenate([sin_ref[spot, :] for spot in places], 0)
    made = project(x_ref[...], w_ref, gain_ref, cosine, sine)
    for j in range(4):
        all_ref[places[j], :] = made[j * block_len : (j + 1) * block_len]

    @pl.when(step == pl.num_programs(0) - 1)
    def _():
        window = band + QUERY_BLOCK

        def step_fn(index, carry):
            first_key, first_query = window_of(index, band)
            rows = pl.ds(first_query, QUERY_BLOCK)
            cols = pl.ds(first_key, window)
            scores = masked_scores(
                all_ref[rows, :128], all_ref[cols, 128:256], first_key, first_query, firsts
            )
            top = jnp.max(scores, axis=1, keepdims=True)
            weight = jnp.exp(scores - top)
            mass = jnp.sum(weight, axis=1, keepdims=True)
            log_ref[rows, :] = top + jnp.log(mass)
            weight = (weight * (1.0 / mass)).astype(BF)
            result = dot(weight, all_ref[cols, 384:], 1, 0)
            for j in range(blocks):
                spot = spot_of(spots, index * blocks + j, block_len)
                a_store[spot, :] = result[j * block_len : (j + 1) * block_len]
            return carry

        lax.fori_loop(0, total // QUERY_BLOCK, step_fn, 0)
        for j in range(total // QUERY_BLOCK):
            part = a_store[j * QUERY_BLOCK : (j + 1) * QUERY_BLOCK, :]
            att_ref[:, j * QUERY_BLOCK : (j + 1) * QUERY_BLOCK] = part.T[:HD].astype(BF)


def head_forward(hidden, w_ext, gain, tables, ids, spots, firsts, count, band):
    total = tables[0].shape[0]
    work = total * (band + QUERY_BLOCK)
    return pl.pallas_call(
        functools.partial(head_kernel, count // 2, band),
        out_shape=(
            jax.ShapeDtypeStruct((total, 512), BF),
            jax.ShapeDtypeStruct((total, 1), F32),
            jax.ShapeDtypeStruct((HD, total), BF),
        ),
        grid_spec=pltpu.PrefetchScalarGridSpec(
            num_scalar_prefetch=3,
            grid=(total // count // 2,),
            in_specs=[
                pl.BlockSpec((2 * count, D), lambda i, *_: (i, 0)),
                fixed((D, 384)), fixed((1, D)), fixed((total, 128)), fixed((total, 128)),
            ],
            out_specs=(fixed((total, 512)), fixed((total, 1)), fixed((HD, total))),
            scratch_shapes=[pltpu.VMEM((total, 128), F32)],
        ),
        compiler_params=params(),
        cost_estimate=cost(total * D * 384 + 4 * work * 128, 2 * total * D, work),
        name="head_forward",
    )(ids, spots, firsts, hidden, w_ext, gain, *tables)


def order_heads(heads, wo_ref, wo_rel):
    per = wo_ref.shape[1]
    many = HD // per
    for j in range(H):
        for m in range(many):
            wo_rel[j * HD + m * per : j * HD + (m + 1) * per, :] = wo_ref[heads[j] * many + m]


def back_kernel(
    part, tok_count, heads, where, att_ref, x_ref, g_ref, wo_ref, wgu_ref, wd_ref, wr_ref,
    gain_ref, act_ref, v_ref, pa_ref, pb_ref, grads_ref, mid_ref, wo_rel, gb_ref, norm_ref, acc, scr,
):
    step = pl.program_id(0)
    own_expert = where[0]
    half = D // 2

    @pl.when(step == 0)
    def _():
        order_heads(heads, wo_ref, wo_rel)
        norm_ref[...] = jnp.zeros_like(norm_ref)

    tile = x_ref.shape[0]
    moved = dot(att_ref[...].reshape(D, tile), wo_ref[...].reshape(D, D), 0, 0)
    middle = x_ref[...].astype(F32) + RESIDUAL_SCALE * moved
    scr[...] = middle

    @pl.when(step == where[2] * tok_count // tile)
    def _():
        own = pl.multiple_of(where[2] * tok_count % tile, tok_count)
        mid_ref[...] = scr[pl.ds(own, tok_count), :]

    gain = gain_ref[...]
    factor = lax.rsqrt(jnp.mean(middle * middle, axis=1, keepdims=True) + EPSILON)
    mixed = (middle * factor * gain).astype(BF)
    grads = g_ref[...].reshape(mixed.shape[0], D + 128)
    logits = dot(mixed, wr_ref[...], 1, 0)
    mask = grads[:, D:].astype(F32)
    logits = jnp.where(mask > 0.0, logits, NEGATIVE)
    odds = jnp.where(mask > 0.0, jnp.exp(logits - jnp.max(logits, axis=1, keepdims=True)), 0.0)
    combine = odds / jnp.sum(odds, axis=1, keepdims=True)
    mark = (lanes_of(combine) == own_expert).astype(F32)
    own_gate = jnp.sum(combine * mark, axis=1, keepdims=True)
    grad_top = grads[:, :D]
    pulled = RESIDUAL_SCALE * dot(grad_top, wd_ref[...], 1, 0)
    gates = dot(mixed, wgu_ref[...], 1, 0)
    gate, up = gates[:, :part], gates[:, part:]
    sigma = 1.0 / (1.0 + jnp.exp(-gate))
    silu = gate * sigma
    activation = silu * up
    grad_act = own_gate * pulled
    act = (RESIDUAL_SCALE * own_gate * activation).astype(BF)
    act_ref[...] = act
    gb_ref[:, :part] = (grad_act * up * sigma * (1.0 + gate * (1.0 - sigma))).astype(BF)
    gb_ref[:, part:] = (grad_act * silu).astype(BF)
    grad_combine = jnp.sum(activation * pulled, axis=1, keepdims=True)
    coef = (grad_combine * own_gate * (mark - combine)).astype(BF)
    terms = (
        (0, 2 * part, mixed, gb_ref[...]),
        (2 * part, 2 * part + 128, mixed, coef),
        (2 * part + 128, 3 * part + 128, grad_top, act),
    )

    @pl.when(step == 0)
    def _():
        for low, high, left, right in terms:
            acc[:, low:high] = dot(left, right, 0, 0)

    @pl.when(step > 0)
    def _():
        for low, high, left, right in terms:
            acc[:, low:high] += dot(left, right, 0, 0)

    grad_mixed = dot(gb_ref[...], wgu_ref[...], 1, 1) + dot(coef, wr_ref[...], 1, 1)
    scaled = scr[...] * factor
    norm_ref[...] += jnp.broadcast_to(
        jnp.sum(grad_mixed * scaled, axis=0, keepdims=True), norm_ref.shape
    )
    inner = grad_mixed * gain
    grad_mid = factor * (inner - scaled * jnp.mean(inner * scaled, axis=1, keepdims=True))
    grad_mid = grad_mid.astype(BF)
    v_ref[...] = grad_mid
    out_grads = dot(wo_rel[...], grad_mid, 1, 1)
    if part == F:
        top = out_grads[:HD] + dot(wo_rel[:HD, :], grad_top, 1, 1)
        pa_ref[:HD, :] = (RESIDUAL_SCALE * top).astype(BF)
        pa_ref[HD:, :] = (RESIDUAL_SCALE * out_grads[HD:half]).astype(BF)
    else:
        pa_ref[...] = (RESIDUAL_SCALE * out_grads[:half]).astype(BF)
    pb_ref[...] = (RESIDUAL_SCALE * out_grads[half:]).astype(BF)

    @pl.when(step == pl.num_programs(0) - 1)
    def _():
        middle = slice(2 * part, 2 * part + 128)
        last = acc[:, middle]
        grads_ref[:, : 2 * part] = acc[:, : 2 * part].astype(BF)
        grads_ref[:, middle] = jnp.where(lanes_of(last) == E, column_of(norm_ref), last).astype(BF)
        grads_ref[:, 2 * part + 128 :] = acc[:, 2 * part + 128 :].astype(BF)


def expert_main(att, hidden, top, wo, wgu, wd, wr, gain, heads, where, count):
    total = hidden.shape[0]
    part = wd.shape[1]
    tile = 2 * count
    width = 3 * part + 128

    def rows(size):
        return pl.BlockSpec((tile, size), lambda i, *_: (i, 0))

    def cols(height):
        return pl.BlockSpec((height, tile), lambda i, *_: (0, i))

    def out(size):
        return jax.ShapeDtypeStruct((total, size), BF)

    half = jax.ShapeDtypeStruct((D // 2, total), BF)
    return pl.pallas_call(
        functools.partial(back_kernel, part, count),
        out_shape=(
            out(part), out(D), half, half, jax.ShapeDtypeStruct((D, width), BF),
            jax.ShapeDtypeStruct((count, D), F32),
        ),
        grid_spec=pltpu.PrefetchScalarGridSpec(
            num_scalar_prefetch=2,
            grid=(total // tile,),
            in_specs=[
                pl.BlockSpec((H, HD, tile), lambda i, *_: (0, 0, i)),
                rows(D),
                pl.BlockSpec((2, count, D + 128), lambda i, *_: (i, 0, 0)),
                fixed(wo.shape), fixed((D, 2 * part)), fixed((D, part)), fixed((D, 128)),
                fixed((1, D)),
            ],
            out_specs=(
                rows(part), rows(D), cols(D // 2), cols(D // 2), fixed((D, width)),
                fixed((count, D)),
            ),
            scratch_shapes=[
                pltpu.VMEM((D, D), BF),
                pltpu.VMEM((tile, 2 * part), BF),
                pltpu.VMEM((8, D), F32),
                pltpu.VMEM((D, width), F32),
                pltpu.VMEM((tile, D), F32),
            ],
        ),
        compiler_params=params(),
        cost_estimate=cost(
            2 * total * D * (2 * D + 8 * part), 12 * total * D, total * part, weight=EXPERT_WEIGHT
        ),
        name="expert_main",
    )(heads, where, att, hidden, top, wo, wgu, wd, wr, gain)


def moe_kernel(act_ref, wd_ref, out_ref):
    out_ref[...] = dot(act_ref[...], wd_ref[...], 1, 1).astype(BF).reshape(out_ref.shape)


def moe_out(act, wd, count, rows):
    total, part = act.shape
    many = 4
    return pl.pallas_call(
        moe_kernel,
        out_shape=jax.ShapeDtypeStruct((total // count, count + 2 * rows, D), BF),
        grid=(total // count // many,),
        in_specs=[pl.BlockSpec((many * count, part), lambda i: (i, 0)), fixed((D, part))],
        out_specs=pl.BlockSpec((many, count, D), lambda i: (i, 0, 0)),
        compiler_params=params(),
        cost_estimate=cost(2 * total * D * part, 3 * total * D),
        name="moe_out",
    )(act, wd)


def output_kernel(where, att_ref, v_ref, g_ref, moe_ref, out_ref, acc):
    step = pl.program_id(0)
    tile = v_ref.shape[0]

    @pl.when(step == 0)
    def _():
        acc[...] = jnp.zeros_like(acc)

    acc[...] += dot(att_ref[...].reshape(D, tile), v_ref[...], 1, 0)
    picked = att_ref[where[0]]
    place = step * tile + lanes_of(picked)
    picked = jnp.where(place // where[3] == where[1], picked, jnp.zeros_like(picked))
    target = pl.ds(pl.multiple_of(where[0] * HD, HD), HD)
    acc[target, :] += dot(picked, g_ref[...].reshape(tile, D), 1, 0)

    @pl.when(step == pl.num_programs(0) - 1)
    def _():
        out_ref[...] = (RESIDUAL_SCALE * acc[...]).astype(BF).reshape(out_ref.shape)


def output_weights(att, grad_mid, top, moe, where, count, rows):
    total = grad_mid.shape[0]
    tile = 4 * count
    per = 2 * rows
    return pl.pallas_call(
        output_kernel,
        out_shape=jax.ShapeDtypeStruct(moe.shape, BF),
        grid_spec=pltpu.PrefetchScalarGridSpec(
            num_scalar_prefetch=1,
            grid=(total // tile,),
            in_specs=[
                pl.BlockSpec((H, HD, tile), lambda i, *_: (0, 0, i)),
                pl.BlockSpec((tile, D), lambda i, *_: (i, 0)),
                pl.BlockSpec((4, count, D), lambda i, *_: (i, 0, 0)),
                pl.BlockSpec(memory_space=pl.ANY),
            ],
            out_specs=fixed((moe.shape[0], per, D), (0, count // per, 0)),
            scratch_shapes=[pltpu.VMEM((D, D), F32)],
        ),
        input_output_aliases={4: 0},
        compiler_params=params(),
        cost_estimate=cost(2 * total * D * D, 8 * total * D),
        name="output_weights",
    )(where, att, grad_mid, top, moe)


def attend_kernel(
    block_len, band, ids, spots, firsts, where, all_ref, up_ref, log_ref, cos_ref, sin_ref,
    own_ref, up_sort, acc_qk, acc_v,
):
    total = all_ref.shape[0]
    blocks = QUERY_BLOCK // block_len
    window = band + QUERY_BLOCK
    acc_qk[...] = jnp.zeros_like(acc_qk)
    acc_v[...] = jnp.zeros_like(acc_v)
    for j in range(total // QUERY_BLOCK):
        piece = up_ref[:, j * QUERY_BLOCK : (j + 1) * QUERY_BLOCK]
        piece = jnp.concatenate([piece, jnp.zeros_like(piece)], 0).T.astype(BF)
        for m in range(blocks):
            spot = spot_of(ids, j * blocks + m, block_len)
            up_sort[spot, :] = piece[m * block_len : (m + 1) * block_len]

    def step_fn(index, carry):
        first_key, first_query = window_of(index, band)
        rows = pl.ds(first_query, QUERY_BLOCK)
        cols = pl.ds(first_key, window)
        keys_win, upstream = all_ref[cols, 128:256], up_sort[rows, :]
        scores = masked_scores(all_ref[rows, :128], keys_win, first_key, first_query, firsts)
        weight = jnp.exp(scores - log_ref[rows, :])
        grad_weight = dot(upstream, all_ref[cols, 384:], 1, 1)
        delta = jnp.sum(weight * grad_weight, axis=1, keepdims=True)
        grad_raw = (SCORE_SCALE * weight * (grad_weight - delta)).astype(BF)
        acc_qk[rows, :] += dot(grad_raw, keys_win, 1, 0)
        acc_qk[cols, :] += dot(grad_raw, all_ref[rows, 256:384], 0, 0)
        acc_v[cols, :] += dot(weight.astype(BF), upstream, 0, 0)
        return carry

    lax.fori_loop(0, total // QUERY_BLOCK, step_fn, 0)

    def turn(index, carry):
        first = pl.multiple_of(index * QUERY_BLOCK, QUERY_BLOCK)
        rows = pl.ds(first, QUERY_BLOCK)
        both = acc_qk[rows, :]
        low = lanes_of(both) % HD < HD // 2
        swapped = jnp.where(low, pltpu.roll(both, 96, 1), -pltpu.roll(both, 32, 1))
        turned = (both * cos_ref[rows, :] + swapped * sin_ref[rows, :]).astype(BF)
        made = jnp.concatenate([turned, acc_v[rows, :].astype(BF)], 1)
        for j in range(blocks):
            block = spots[index * blocks + j]
            first = pl.multiple_of(block * block_len, block_len)
            piece = made[j * block_len : (j + 1) * block_len]
            keep = first // where[3] == where[1]
            own_ref[pl.ds(first, block_len), :] = jnp.where(keep, piece, jnp.zeros_like(piece))
        return carry

    lax.fori_loop(0, total // QUERY_BLOCK, turn, 0)


def attend_backward(heads_all, upstream, logs, tables, ids, spots, firsts, where, count, band):
    total = heads_all.shape[0]
    work = total * (band + QUERY_BLOCK)
    return pl.pallas_call(
        functools.partial(attend_kernel, count // 2, band),
        out_shape=jax.ShapeDtypeStruct((total, 256), BF),
        grid_spec=pltpu.PrefetchScalarGridSpec(
            num_scalar_prefetch=4,
            grid=(1,),
            in_specs=[
                fixed((total, 512)), fixed((HD, total)), fixed((total, 1)), fixed((total, 128)),
                fixed((total, 128)),
            ],
            out_specs=fixed((total, 256)),
            scratch_shapes=[
                pltpu.VMEM((total, 128), BF),
                pltpu.VMEM((total, 128), F32),
                pltpu.VMEM((total, 128), F32),
            ],
        ),
        compiler_params=params(60),
        cost_estimate=cost(10 * work * 128, 2 * total * 1024, work),
        name="attend_backward",
    )(ids, spots, firsts, where, heads_all, upstream, logs, *tables)


def pull_kernel(
    last, order, every, g_ref, h_ref, w_ref, gain_ref, x_ref, y_ref, gm_ref, hm_ref, w_in_ref, n_in_ref,
    out_ref, w_out_ref, n_out_ref, acc_w,
):
    step = pl.program_id(0)

    @pl.when(step == 0)
    def _():
        acc_w[...] = w_in_ref[...]
        n_out_ref[...] = n_in_ref[...]

    grads = jnp.concatenate([g_ref[...], h_ref[...]], 0)
    grad_mid = jnp.concatenate([gm_ref[...], hm_ref[...]], 0).astype(F32)
    grad_normed = dot(grads, w_ref[...], 1, 1)
    x_f = jnp.concatenate([x_ref[...], y_ref[...]], 0).astype(F32)
    factor = lax.rsqrt(jnp.mean(x_f * x_f, axis=1, keepdims=True) + EPSILON)
    scaled = x_f * factor
    normed = (scaled * gain_ref[...]).astype(BF)
    acc_w[...] += dot(normed, grads, 0, 0)
    n_out_ref[...] += jnp.broadcast_to(
        jnp.sum(grad_normed * scaled, axis=0, keepdims=True), n_out_ref.shape
    )
    inner = grad_normed * gain_ref[...]
    grad_x = factor * (inner - scaled * jnp.mean(inner * scaled, axis=1, keepdims=True))
    out_ref[...] = (grad_x + grad_mid).astype(BF)

    @pl.when(step == pl.num_programs(0) - 1)
    def _():
        if last:
            tail = acc_w[:, 128:]
            acc_w[:, 128:] = jnp.where(lanes_of(tail) == HD, column_of(n_out_ref), tail)
            places = every.shape[0]
            size = acc_w.shape[0] // places
            for j in range(places):
                first = pl.multiple_of(every[j] * size, size)
                w_out_ref[j * size : (j + 1) * size, :] = acc_w[pl.ds(first, size), :].astype(BF)
        else:
            w_out_ref[...] = acc_w[...]


def pull_heads(
    own_grads, w_head, gain, hidden, grad_mid, w_in, n_in, order, every, count, last
):
    total = hidden.shape[0] // 2

    def at(width, j):
        return pl.BlockSpec((count, width), lambda i, order, _: (order[2 * i + j], 0))

    block = pl.BlockSpec((2 * count, D), lambda i, *_: (i, 0))
    return pl.pallas_call(
        functools.partial(pull_kernel, last),
        out_shape=(
            jax.ShapeDtypeStruct((total, D), BF),
            jax.ShapeDtypeStruct((D, 256), BF if last else F32),
            jax.ShapeDtypeStruct((8, D), F32),
        ),
        grid_spec=pltpu.PrefetchScalarGridSpec(
            num_scalar_prefetch=2,
            grid=(total // count // 2,),
            in_specs=[
                at(256, 0), at(256, 1), fixed((D, 256)), fixed((1, D)), at(D, 0), at(D, 1), at(D, 0),
                at(D, 1),
                fixed((D, 256)), fixed((8, D)),
            ],
            out_specs=(block, fixed((D, 256)), fixed((8, D))),
            scratch_shapes=[pltpu.VMEM((D, 256), F32)],
        ),
        compiler_params=params(),
        cost_estimate=cost(4 * total * D * 256, 6 * total * D, weight=1),
        name="pull_last" if last else "pull_first",
    )(
        order, every, own_grads, own_grads, w_head, gain, hidden, hidden, grad_mid, grad_mid, w_in, n_in
    )


def finish_kernel(places, *refs):
    q_ref, k_ref, v_ref, gain_ref, scr = refs[4:]
    for j in range(16):
        scr[places[j]] = refs[j // 4][j % 4].astype(F32)
    total = jnp.zeros_like(scr[0])
    for quad in range(H // 4):
        heads = [scr[4 * quad + j] for j in range(4)]
        for j in range(2):
            first = (4 * quad + 2 * j) * HD
            q_ref[:, first : first + 128] = jnp.concatenate(
                [heads[2 * j][:, :HD], heads[2 * j + 1][:, :HD]], 1
            )
        pairs = [heads[0] + heads[1], heads[2] + heads[3]]
        total = total + pairs[0] + pairs[1]
        for ref, low in ((k_ref, HD), (v_ref, 2 * HD)):
            ref[:, quad * 128 : (quad + 1) * 128] = jnp.concatenate(
                [pair[:, low : low + HD] for pair in pairs], 1
            )
    gain_ref[...] = total[:, 128:]


def finish_heads(places, pieces):
    rows = pieces[0].shape[1]
    shapes = ((rows, D), (rows, D // 2), (rows, D // 2), (rows, 128))
    return pl.pallas_call(
        finish_kernel,
        out_shape=tuple(jax.ShapeDtypeStruct(shape, F32) for shape in shapes),
        grid_spec=pltpu.PrefetchScalarGridSpec(
            num_scalar_prefetch=1,
            grid=(1,),
            in_specs=[fixed(piece.shape) for piece in pieces],
            out_specs=tuple(fixed(shape) for shape in shapes),
            scratch_shapes=[pltpu.VMEM((16, rows, 256), F32)],
        ),
        compiler_params=params(),
        cost_estimate=cost(1, 2**20),
        name="finish_heads",
    )(places, *pieces)


def finish_kernel_experts(in_ref, up_ref, down_ref, tail_ref):
    many = in_ref.shape[0]
    wide, narrow = up_ref.shape[1] // many, down_ref.shape[1] // many
    for j in range(many):
        up_ref[:, j * wide : (j + 1) * wide] = in_ref[j, :, :wide].astype(F32)
        down_ref[:, j * narrow : (j + 1) * narrow] = in_ref[j, :, wide + 128 :].astype(F32)

    @pl.when(pl.program_id(0) == 0)
    def _():
        tail_ref[...] = jnp.zeros_like(tail_ref)

    for j in range(many):
        tail_ref[...] += in_ref[j, :, wide : wide + 128].astype(F32)


def finish_experts(arrived):
    places, rows, width = arrived.shape
    part = (width - 128) // 3
    return pl.pallas_call(
        finish_kernel_experts,
        out_shape=(
            jax.ShapeDtypeStruct((rows, places * 2 * part), F32),
            jax.ShapeDtypeStruct((rows, places * part), F32),
            jax.ShapeDtypeStruct((rows, 128), F32),
        ),
        grid=(places // 4,),
        in_specs=[pl.BlockSpec((4, rows, width), lambda i: (i, 0, 0))],
        out_specs=(
            pl.BlockSpec((rows, 8 * part), lambda i: (0, i)),
            pl.BlockSpec((rows, 4 * part), lambda i: (0, i)),
            fixed((rows, 128)),
        ),
        compiler_params=params(),
        cost_estimate=cost(1, 5 * 2**20),
        name="finish_experts",
    )(arrived)


def per_device(
    hidden_in,
    out_grad,
    doc_lengths,
    block_order,
    routes,
    attn_norm,
    w_query,
    w_key,
    w_value,
    w_output,
    ffn_norm,
    w_router,
    w_gate_up,
    w_down,
):
    ctx_count = lax.axis_size("ctx")
    ctx_place = lax.axis_index("ctx")
    fsdp_place = lax.axis_index("fsdp")
    copies = ctx_count // E
    own_expert, own_copy = ctx_place // copies, ctx_place % copies
    tok_count = hidden_in.shape[1]
    seq_len = tok_count * ctx_count
    block_len = tok_count // 2
    band = seq_len // 4
    rows = attn_norm.shape[0]
    part = F // copies
    groups = H // KVH
    share = seq_len // copies
    swap_y = [(0, 1), (1, 0)]
    alone = copies == 1

    def swap_fsdp(mine):
        return lax.ppermute(mine, "fsdp", swap_y)

    def both_rows(mine):
        theirs = swap_fsdp(mine)
        stacked = jnp.where(
            fsdp_place == 0, jnp.stack([mine, theirs], 1), jnp.stack([theirs, mine], 1)
        )
        return stacked.reshape(-1, mine.shape[-1])

    def exchange(split):
        return lax.all_to_all(split, "ctx", 0, 0, tiled=True)

    ids = block_order[0]
    block_ids = jnp.arange(ids.shape[0], dtype=jnp.int32)
    spots = jnp.sum(jnp.where(ids[None, :] == block_ids[:, None], block_ids[None, :], 0), axis=1)
    lengths = doc_lengths[0]
    doc_ids = jnp.arange(lengths.shape[0], dtype=jnp.int32)
    firsts = jnp.sum(
        jnp.where(doc_ids[None, :] < doc_ids[:, None], lengths[None, :], 0), axis=1
    )
    tables = tables_of(seq_len)
    order, heads = block_order_of(ctx_count), block_order_of(E)
    where = jnp.stack([own_expert, own_copy, ctx_place, jnp.int32(share)]).astype(jnp.int32)

    def by_expert(weight, pieces):
        split = weight.reshape(rows, E, pieces, copies, part)
        return split.transpose(1, 3, 0, 2, 4).reshape(ctx_count, rows, pieces * part)

    chosen_mask = jnp.any(
        routes[0][:, :, None] == jnp.arange(E, dtype=jnp.int32)[None, None, :], axis=1
    ).astype(BF)
    grads_own = jnp.concatenate(
        [out_grad[0], chosen_mask, jnp.zeros((tok_count, 128 - E), BF)], axis=1
    )
    experts = jnp.concatenate([by_expert(w_gate_up, 2), by_expert(w_down, 1)], axis=2)
    norms = jnp.stack([attn_norm, ffn_norm], 1)
    if alone:
        small_here = exchange(pack_small(copies, w_query, w_key, w_value, w_router, norms))
        w_ext, w_head, router_full, gain_one, gain_two = split_small(both_rows(small_here))
        near = Gather(hidden_in[0])
        near.cross()
        near.last(small_here)
        experts_here = exchange(after(experts, near.two))
        hidden_all = near.join(order, "join_hidden", w_ext).reshape(seq_len, D)
    else:
        small_here = exchange(pack_small(copies, w_query, w_key, w_value, w_router, norms))
        w_ext, w_head, router_full, gain_one, gain_two = split_small(both_rows(small_here))
        hidden_all = lax.all_gather(hidden_in[0], "ctx", axis=0, tiled=True)
        experts_here = exchange(experts)
    out_all = lax.all_gather(w_output, BOTH, axis=0, tiled=True).reshape(ctx_count, 2 * rows, D)
    top_all = lax.all_gather(grads_own[None], "ctx", axis=0, tiled=True)

    heads_all, logs, attended = head_forward(
        hidden_all, w_ext, gain_one, tables, ids, spots, firsts, tok_count, band
    )
    def half_rows(mine, theirs):
        stacked = jnp.where(
            fsdp_place == 0, jnp.stack([mine, theirs], 1), jnp.stack([theirs, mine], 1)
        )
        return stacked.reshape(D, mine.shape[-1])

    if alone:
        att = Gather(attended)
        experts_here = after(experts_here, att.one, att.three)
    gu_here, dn_here = experts_here[:, :, : 2 * part], experts_here[:, :, 2 * part :]
    gu_there, dn_there = swap_fsdp(gu_here), swap_fsdp(dn_here)
    w_gu, w_dn = half_rows(gu_here, gu_there), half_rows(dn_here, dn_there)
    if alone:
        att.cross()
        att.last(experts_here)
        att_all = att.join(heads, "join_heads", w_gu)
    else:
        sent = lax.dynamic_slice_in_dim(attended, own_copy * share, share, 1)
        att_all = lax.all_gather(sent, "ctx", axis=0, tiled=True)
        att_all = att_all.reshape(H, copies, HD, share).transpose(0, 2, 1, 3)
        att_all = att_all.reshape(H, HD, seq_len)

    act, grad_mid, pull_a, pull_b, grads_expert, middle = expert_main(
        att_all, hidden_all, top_all, out_all, w_gu, w_dn, router_full, gain_two, heads, where,
        tok_count,
    )

    def given_rows(grads):
        by_owner = grads.reshape(ctx_count, 2, rows, grads.shape[1])
        return by_owner, lax.dynamic_index_in_dim(by_owner, 1 - fsdp_place, 1, keepdims=False)

    def to_owner(by_owner, theirs):
        kept = lax.dynamic_index_in_dim(by_owner, fsdp_place, 1, keepdims=False)
        return (kept.astype(F32) + theirs.astype(F32)).astype(BF)

    owner, given = given_rows(grads_expert)
    theirs = swap_fsdp(given)
    mid_late = grad_mid
    if alone:
        ring = RingSum(pull_a, permute(pull_b, SWAP_CORE))
        mid_late = after(grad_mid, ring.cross_out)
    moe = moe_out(act, w_dn, tok_count, rows)
    out_both = output_weights(
        att_all, mid_late, top_all, moe, where, tok_count, rows
    )
    if alone:
        ring.cross()
        out_both = after(out_both, *ring.sends)
    if alone:
        upstream = ring.end(theirs)
    else:
        joined = jnp.concatenate([pull_a, pull_b], 0)
        pulled = lax.psum_scatter(joined, "ctx", scatter_dimension=0, tiled=True)
        rings = [[i * copies + j for j in range(copies)] for i in range(E)]
        pulled = lax.all_gather(pulled, "ctx", axis=0, tiled=True, axis_index_groups=rings)
        own_out = lax.dynamic_slice_in_dim(out_all.reshape(D, D), own_expert * HD, HD, 0)
        top_rows = top_all[:, :, :D].reshape(seq_len, D)
        upstream = pulled.astype(F32) + RESIDUAL_SCALE * dot(own_out, top_rows, 1, 1)
    if alone:
        theirs = after(theirs, upstream)
    grads_all_expert = to_owner(owner, theirs)

    own_grads = attend_backward(
        heads_all, upstream, logs, tables, ids, spots, firsts, where, tok_count, band
    )
    experts_in = exchange(grads_all_expert)
    grad_b, head_sum, norm_head = pull_heads(
        own_grads, w_head, gain_one, hidden_all, grad_mid, jnp.zeros((D, 256), F32),
        jnp.zeros((8, D), F32), order[ctx_count // 2 :], order, tok_count, False,
    )
    grad_a, grad_heads, ignored = pull_heads(
        own_grads, w_head, gain_one, hidden_all, grad_mid, head_sum, norm_head,
        order[: ctx_count // 2], order, tok_count, True,
    )
    if alone:
        by_owner = grad_heads.reshape(ctx_count, 2, rows, 256)
        kept = lax.dynamic_index_in_dim(by_owner, fsdp_place, 1, keepdims=False)
        given = lax.dynamic_index_in_dim(by_owner, 1 - fsdp_place, 1, keepdims=False)
        theirs = swap_fsdp(given)
        ring = RingSum(grad_a, permute(grad_b, SWAP_CORE))
        ring.cross()
        theirs = after(theirs, *ring.sends)
        tail_sum = (kept.astype(F32) + theirs.astype(F32)).astype(BF)
        experts_in = after(experts_in, *ring.sends)
    else:
        joined = jnp.concatenate([grad_a, grad_b], 0)
        grad_own = lax.psum_scatter(joined, "ctx", scatter_dimension=0, tiled=True).astype(F32)
    def from_experts(block, pieces):
        block = block[:, :, : pieces * part].astype(F32)
        block = block.reshape(E, copies, rows, pieces, part).transpose(2, 0, 3, 1, 4)
        return block.reshape(rows, E * pieces * F)

    if alone:
        share_gate_up, share_down, tail = finish_experts(experts_in)
    else:
        gu_in = experts_in[:, :, : 2 * part + 128]
        dn_in = experts_in[:, :, 2 * part + 128 :]
        share_gate_up = from_experts(gu_in, 2)
        share_down = from_experts(dn_in, 1)
        tail = jnp.sum(gu_in[:, :, 2 * part :].astype(F32), axis=0)
    share_router = tail[:, :E]
    share_gain_two = tail[:, E]
    out_own = lax.psum_scatter(out_both, "ctx", scatter_dimension=0, tiled=False).astype(F32)
    hidden_out = (middle + out_own[:tok_count]).astype(BF)
    out_rows = out_own[tok_count:].reshape(2, rows, D)
    mine = lax.dynamic_index_in_dim(out_rows, fsdp_place, 0, keepdims=False)
    theirs = lax.dynamic_index_in_dim(out_rows, 1 - fsdp_place, 0, keepdims=False)
    share_output = mine + swap_fsdp(theirs)

    if alone:
        grad_own = ring.end(share_output, hidden_out, share_gate_up)
    grad_in = out_grad[0].astype(F32) + grad_own
    if alone:
        pieces = spread_ctx(tail_sum)
        share_query, share_key, share_value, gain_sum = finish_heads(sender_order_of(), pieces)
        share_gain_one = gain_sum[:, HD]
    else:
        tail_in = lax.all_to_all(
            grad_heads.reshape(2 * ctx_count, rows, 256), BOTH, 0, 0, tiled=True
        )
        tail_in = tail_in.astype(F32).reshape(H, copies * 2, rows, 256)
        heads_in = jnp.sum(tail_in[..., : 3 * HD], axis=1)
        share_query = heads_in[:, :, :HD].transpose(1, 0, 2).reshape(rows, H * HD)
        pairs_in = heads_in[:, :, HD:].reshape(KVH, groups, rows, 2, HD).sum(1)
        share_key = pairs_in[:, :, 0].transpose(1, 0, 2).reshape(rows, KVH * HD)
        share_value = pairs_in[:, :, 1].transpose(1, 0, 2).reshape(rows, KVH * HD)
        share_gain_one = jnp.sum(tail_in[..., 3 * HD], axis=(0, 1))
    return (
        hidden_out[None],
        grad_in[None],
        share_gain_one,
        share_query,
        share_key,
        share_value,
        share_output,
        share_gain_two,
        share_router,
        share_gate_up,
        share_down,
    )


def solution(mesh):
    return jax.shard_map(
        per_device,
        mesh=mesh,
        in_specs=(
            P("fsdp", "ctx", None),
            P("fsdp", "ctx", None),
            P("fsdp", None),
            P("fsdp", None),
            P("fsdp", "ctx", None),
            P(BOTH),
            P(BOTH, None),
            P(BOTH, None),
            P(BOTH, None),
            P(BOTH, None),
            P(BOTH),
            P(BOTH, None),
            P(BOTH, None),
            P(BOTH, None),
        ),
        out_specs=(
            P("fsdp", "ctx", None),
            P("fsdp", "ctx", None),
            P(BOTH),
            P(BOTH, None),
            P(BOTH, None),
            P(BOTH, None),
            P(BOTH, None),
            P(BOTH),
            P(BOTH, None),
            P(BOTH, None),
            P(BOTH, None),
        ),
        check_vma=False,
    )
```

```python
import functools

import jax
import jax.numpy as jnp
import numpy as np
from jax import lax
from jax.experimental import pallas as pl
from jax.experimental.pallas import tpu as pltpu
from jax.sharding import PartitionSpec as P

D = 1024
H = 16
KVH = 8
HD = 64
F = 512
E = 16

EPSILON = 1e-06
SCORE_SCALE = 0.015625
RESIDUAL_SCALE = 0.22
THETA = 10000.0
NEGATIVE = -1e30
BOTH = ("ctx", "fsdp")
EXPERT_WEIGHT = 2
BF = jnp.bfloat16
F32 = jnp.float32
QUERY_BLOCK = 256


def dot(left, right, left_dim, right_dim):
    return lax.dot_general(
        left, right, (((left_dim,), (right_dim,)), ((), ())), preferred_element_type=F32
    )


def permute(values, pairs):
    return lax.ppermute(values, "ctx", pairs)


def shift_z(step):
    return [(i, ((i // 4 + step) % 4) * 4 + i % 4) for i in range(16)]


SWAP_X = [(i, i ^ 2) for i in range(16)]
SWAP_CORE = [(i, i ^ 1) for i in range(16)]


def after(value, *others):
    return lax.optimization_barrier((value, *others))[0] if others else lax.optimization_barrier(value)


def block_order_of(count):
    index = jnp.arange(count, dtype=jnp.int32)
    if lax.axis_size("ctx") != 16:
        return index
    place = lax.axis_index("ctx")
    z_of = (place // 4 - (index % 8) // 2 + 4) % 4
    x_of = ((place // 2) % 2 + index % 2) % 2
    return z_of * 4 + x_of * 2 + (place % 2 + index // 8) % 2


class RingSum:
    def __init__(self, mine, arrived):
        self.mine, self.arrived = mine, arrived
        self.count = mine.shape[0] // 8
        self.cross_out = jnp.concatenate([self.chip(k, 1) for k in (2, 1, 3)], 0).astype(BF)

    def chip(self, k, dx):
        rows = slice((2 * k + dx) * self.count, (2 * k + dx + 1) * self.count)
        return self.mine[rows].astype(F32) + self.arrived[rows].astype(F32)

    def cross(self):
        got = permute(self.cross_out, SWAP_X)
        self.sends = []
        for j, k in enumerate((2, 1, 3)):
            term = got[j * self.count : (j + 1) * self.count].astype(F32)
            self.sends.append((self.chip(k, 0) + term).astype(BF))

    def end(self, *others):
        self.own = permute(self.chip(0, 1).astype(BF), SWAP_X)
        total = self.chip(0, 0) + self.own.astype(F32)
        for send, k in zip(self.sends, (2, 1, 3)):
            term = permute(send, shift_z(4 - k))
            self.seen = term
            if k == 2 and others:
                term = after(term, *others)
            total = total + term.astype(F32)
        return total


def join_kernel(places, *refs):
    pieces, out_ref, sems = refs[:14], refs[14], refs[15]
    count = out_ref.shape[1]
    copies = []
    for side in range(2):
        own, far, one, pair, two, far_two, three = pieces[7 * side : 7 * side + 7]
        lower, upper = pair.at[:count], pair.at[count:]
        for j, piece in enumerate((own, far, one, lower, two, far_two, three, upper)):
            block = 8 * side + j
            copies.append(
                pltpu.make_async_copy(piece, out_ref.at[places[block]], sems.at[block])
            )
    for copy in copies:
        copy.start()
    for copy in copies:
        copy.wait()


def spread_ctx(blocks):
    _, rows, width = blocks.shape
    other = permute(blocks[8:], SWAP_CORE)
    chip = jnp.stack([blocks[:8], other], 1).reshape(4, 2, 2, rows, width)
    crossed = permute(chip[:, 1], SWAP_X)
    both = jnp.concatenate([chip[:, 0], crossed], 1)
    return (both[0], *(permute(both[k], shift_z(4 - k)) for k in range(1, 4)))


def sender_order_of():
    place = lax.axis_index("ctx")
    index = jnp.arange(16, dtype=jnp.int32)
    z_of = (place // 4 + index // 4) % 4
    x_of = ((place // 2) % 2 + (index // 2) % 2) % 2
    return z_of * 4 + x_of * 2 + (place % 2 + index % 2) % 2


class Gather:
    def __init__(self, rows):
        self.count = rows.shape[0]
        self.own = rows
        self.one = permute(rows, shift_z(1))
        self.three = permute(rows, shift_z(3))
        self.far = permute(rows, SWAP_X)
        self.two = permute(rows, shift_z(2))

    def cross(self, *others):
        if others:
            self.one, self.three = after((self.one, self.three), *others)
        self.pair = permute(jnp.concatenate([self.one, self.three], 0), SWAP_X)

    def last(self, *others):
        if others:
            self.two = after(self.two, *others)
        self.far_two = permute(self.two, SWAP_X)

    def join(self, places, name, *others):
        if others:
            self.far, self.far_two = after((self.far, self.far_two), *others)
        mine = (self.own, self.far, self.one, self.pair, self.two, self.far_two, self.three)
        other = tuple(permute(piece, SWAP_CORE) for piece in mine)
        shape = (16, *self.own.shape)
        return pl.pallas_call(
            join_kernel,
            out_shape=jax.ShapeDtypeStruct(shape, BF),
            grid_spec=pltpu.PrefetchScalarGridSpec(
                num_scalar_prefetch=1,
                grid=(1,),
                in_specs=[fixed(piece.shape) for piece in (*mine, *other)],
                out_specs=pl.BlockSpec(memory_space=pl.ANY),
                scratch_shapes=[pltpu.SemaphoreType.DMA((16,))],
            ),
            compiler_params=params(),
            cost_estimate=cost(1, 4 * self.own.size * 16),
            name=name,
        )(places, *mine, *other)


def tables_of(total):
    half_width = HD // 2
    frequency = (THETA ** (-np.arange(half_width) / half_width)).astype(np.float32)
    angles = np.arange(total, dtype=np.float32)[:, None] * frequency[None, :]
    cosine = np.cos(angles.astype(np.float64)).astype(np.float32)
    sine = np.sin(angles.astype(np.float64)).astype(np.float32)
    return jnp.asarray(np.tile(cosine, (1, 4))), jnp.asarray(np.tile(sine, (1, 4)))


def window_of(step, band):
    start = jnp.maximum(step * QUERY_BLOCK - band, 0)
    return pl.multiple_of(start, QUERY_BLOCK), pl.multiple_of(step * QUERY_BLOCK, QUERY_BLOCK)


def masked_scores(queries, keys_win, first_key, first_query, firsts):
    raw = dot(queries, keys_win, 1, 1) * SCORE_SCALE
    key_place = first_key + lax.broadcasted_iota(jnp.int32, raw.shape, 1)
    query_place = first_query + lax.broadcasted_iota(jnp.int32, raw.shape, 0)
    column = first_query + lax.broadcasted_iota(jnp.int32, (raw.shape[0], 1), 0)
    start = jnp.zeros_like(column)
    for j in range(1, firsts.shape[0]):
        start = jnp.where(firsts[j] <= column, jnp.maximum(start, firsts[j]), start)
    visible = (key_place <= query_place) & (key_place >= start)
    return jnp.where(visible, raw, NEGATIVE)


def lanes_of(values):
    return lax.broadcasted_iota(jnp.int32, values.shape, 1)


def fixed(shape, at=None):
    place = (0,) * len(shape) if at is None else at
    return pl.BlockSpec(shape, lambda *_: place, pipeline_mode=pl.Buffered(1))


def params(mib=56):
    return pltpu.CompilerParams(vmem_limit_bytes=mib * 2**20)


def cost(flops, bytes_accessed, transcendentals=0, weight=20):
    return pl.CostEstimate(
        flops=weight * flops,
        bytes_accessed=weight * bytes_accessed,
        transcendentals=transcendentals,
    )


def column_of(row_ref):
    return jnp.broadcast_to(row_ref[:1, :], (128, row_ref.shape[1])).T


def pack_kernel(copies, wq_ref, wk_ref, wv_ref, wr_ref, norm_ref, small_ref):
    rows = wq_ref.shape[0]
    rest = jnp.concatenate(
        [wr_ref[...], norm_ref[...], jnp.zeros((rows, HD - E - 2), BF)], axis=1
    )
    for place in range(E * copies):
        head = place // copies
        pair = head // (H // KVH)
        query = wq_ref[:, head * HD : (head + 1) * HD]
        key = wk_ref[:, pair * HD : (pair + 1) * HD]
        value = wv_ref[:, pair * HD : (pair + 1) * HD]
        small_ref[place] = jnp.concatenate([query, key, value, rest], axis=1)


def pack_small(copies, *weights):
    shape = (E * copies, weights[0].shape[0], 256)
    return pl.pallas_call(
        functools.partial(pack_kernel, copies),
        out_shape=jax.ShapeDtypeStruct(shape, BF),
        grid=(1,),
        in_specs=[fixed(weight.shape) for weight in weights],
        out_specs=fixed(shape),
        compiler_params=params(),
        cost_estimate=cost(1, 2**20),
        name="pack_small",
    )(*weights)


def split_kernel(small_ref, ext_ref, head_ref, router_ref, one_ref, two_ref):
    small = small_ref[...]
    wq, wk, wv = (small[:, j * HD : (j + 1) * HD] for j in range(3))
    turn = HD // 2
    zero = jnp.zeros_like(wv)
    rest = small[:, 3 * HD :]
    ext_ref[:, :128] = small[:, :128]
    ext_ref[:, 128:256] = jnp.concatenate(
        [-wq[:, turn:], wq[:, :turn], -wk[:, turn:], wk[:, :turn]], 1
    )
    value = jnp.concatenate([wv, zero], 1)
    ext_ref[:, 256:] = value
    head_ref[:, :128] = small[:, :128]
    head_ref[:, 128:] = value
    rest = jnp.concatenate([rest, zero], 1).astype(F32)
    router_ref[...] = jnp.where(lanes_of(rest) < E, rest, 0.0).astype(BF)
    turned = rest.T
    one_ref[...] = turned[E : E + 1, :]
    two_ref[...] = turned[E + 1 : E + 2, :]


def split_small(small):
    shapes = ((D, 384), (D, 256), (D, 128), (1, D), (1, D))
    types = (BF, BF, BF, F32, F32)
    return pl.pallas_call(
        split_kernel,
        out_shape=tuple(jax.ShapeDtypeStruct(s, t) for s, t in zip(shapes, types)),
        grid=(1,),
        in_specs=[fixed(small.shape)],
        out_specs=tuple(fixed(s) for s in shapes),
        compiler_params=params(),
        cost_estimate=cost(1, 3 * 2**20),
        name="split_weights",
    )(small)


def project(x_blk, w_ref, gain_ref, cosine, sine):
    x_f = x_blk.astype(F32)
    factor = lax.rsqrt(jnp.mean(x_f * x_f, axis=1, keepdims=True) + EPSILON)
    normed = (x_f * factor * gain_ref[...]).astype(BF)
    out = dot(normed, w_ref[...], 1, 0)
    both = out[:, :128] * cosine + out[:, 128:256] * sine
    swapped = pltpu.roll(both, 64, 1)
    low = lanes_of(both) < HD
    zero = jnp.zeros_like(both)
    return jnp.concatenate(
        [
            jnp.where(low, both, zero).astype(BF),
            jnp.where(low, swapped, zero).astype(BF),
            jnp.where(low, zero, swapped).astype(BF),
            out[:, 256:].astype(BF),
        ],
        axis=1,
    )


def spot_of(ids, block, block_len):
    return pl.ds(pl.multiple_of(ids[block] * block_len, block_len), block_len)


def head_kernel(
    block_len, band, ids, spots, firsts,
    x_ref, w_ref, gain_ref, cos_ref, sin_ref, all_ref, log_ref, att_ref, a_store,
):
    step = pl.program_id(0)
    total = all_ref.shape[0]
    blocks = QUERY_BLOCK // block_len

    places = [spot_of(ids, 4 * step + j, block_len) for j in range(4)]
    cosine = jnp.concatenate([cos_ref[spot, :] for spot in places], 0)
    sine = jnp.concatenate([sin_ref[spot, :] for spot in places], 0)
    made = project(x_ref[...], w_ref, gain_ref, cosine, sine)
    for j in range(4):
        all_ref[places[j], :] = made[j * block_len : (j + 1) * block_len]

    @pl.when(step == pl.num_programs(0) - 1)
    def _():
        window = band + QUERY_BLOCK

        def step_fn(index, carry):
            first_key, first_query = window_of(index, band)
            rows = pl.ds(first_query, QUERY_BLOCK)
            cols = pl.ds(first_key, window)
            scores = masked_scores(
                all_ref[rows, :128], all_ref[cols, 128:256], first_key, first_query, firsts
            )
            top = jnp.max(scores, axis=1, keepdims=True)
            weight = jnp.exp(scores - top)
            mass = jnp.sum(weight, axis=1, keepdims=True)
            log_ref[rows, :] = top + jnp.log(mass)
            weight = (weight * (1.0 / mass)).astype(BF)
            result = dot(weight, all_ref[cols, 384:], 1, 0)
            for j in range(blocks):
                spot = spot_of(spots, index * blocks + j, block_len)
                a_store[spot, :] = result[j * block_len : (j + 1) * block_len]
            return carry

        lax.fori_loop(0, total // QUERY_BLOCK, step_fn, 0, unroll=total // QUERY_BLOCK <= 8)
        for j in range(total // QUERY_BLOCK):
            part = a_store[j * QUERY_BLOCK : (j + 1) * QUERY_BLOCK, :]
            att_ref[:, j * QUERY_BLOCK : (j + 1) * QUERY_BLOCK] = part.T[:HD].astype(BF)


def head_forward(hidden, w_ext, gain, tables, ids, spots, firsts, count, band):
    total = tables[0].shape[0]
    work = total * (band + QUERY_BLOCK)
    return pl.pallas_call(
        functools.partial(head_kernel, count // 2, band),
        out_shape=(
            jax.ShapeDtypeStruct((total, 512), BF),
            jax.ShapeDtypeStruct((total, 1), F32),
            jax.ShapeDtypeStruct((HD, total), BF),
        ),
        grid_spec=pltpu.PrefetchScalarGridSpec(
            num_scalar_prefetch=3,
            grid=(total // count // 2,),
            in_specs=[
                pl.BlockSpec((2 * count, D), lambda i, *_: (i, 0)),
                fixed((D, 384)), fixed((1, D)), fixed((total, 128)), fixed((total, 128)),
            ],
            out_specs=(fixed((total, 512)), fixed((total, 1)), fixed((HD, total))),
            scratch_shapes=[pltpu.VMEM((total, 128), F32)],
        ),
        compiler_params=params(),
        cost_estimate=cost(total * D * 384 + 4 * work * 128, 2 * total * D, work),
        name="head_forward",
    )(ids, spots, firsts, hidden, w_ext, gain, *tables)


def order_heads(heads, wo_ref, wo_rel):
    per = wo_ref.shape[1]
    many = HD // per
    for j in range(H):
        for m in range(many):
            wo_rel[j * HD + m * per : j * HD + (m + 1) * per, :] = wo_ref[heads[j] * many + m]


def back_kernel(
    part, tok_count, heads, where, att_ref, x_ref, g_ref, wo_ref, wgu_ref, wd_ref, wr_ref,
    gain_ref, act_ref, v_ref, pa_ref, pb_ref, grads_ref, mid_ref, wo_rel, gb_ref, norm_ref, acc, scr,
):
    step = pl.program_id(0)
    own_expert = where[0]
    half = D // 2

    @pl.when(step == 0)
    def _():
        order_heads(heads, wo_ref, wo_rel)
        norm_ref[...] = jnp.zeros_like(norm_ref)

    tile = x_ref.shape[0]
    moved = dot(att_ref[...].reshape(D, tile), wo_ref[...].reshape(D, D), 0, 0)
    middle = x_ref[...].astype(F32) + RESIDUAL_SCALE * moved
    scr[...] = middle

    @pl.when(step == where[2] * tok_count // tile)
    def _():
        own = pl.multiple_of(where[2] * tok_count % tile, tok_count)
        mid_ref[...] = scr[pl.ds(own, tok_count), :]

    gain = gain_ref[...]
    factor = lax.rsqrt(jnp.mean(middle * middle, axis=1, keepdims=True) + EPSILON)
    mixed = (middle * factor * gain).astype(BF)
    grads = g_ref[...].reshape(mixed.shape[0], D + 128)
    logits = dot(mixed, wr_ref[...], 1, 0)
    mask = grads[:, D:].astype(F32)
    logits = jnp.where(mask > 0.0, logits, NEGATIVE)
    odds = jnp.where(mask > 0.0, jnp.exp(logits - jnp.max(logits, axis=1, keepdims=True)), 0.0)
    combine = odds / jnp.sum(odds, axis=1, keepdims=True)
    mark = (lanes_of(combine) == own_expert).astype(F32)
    own_gate = jnp.sum(combine * mark, axis=1, keepdims=True)
    grad_top = grads[:, :D]
    pulled = RESIDUAL_SCALE * dot(grad_top, wd_ref[...], 1, 0)
    gates = dot(mixed, wgu_ref[...], 1, 0)
    gate, up = gates[:, :part], gates[:, part:]
    sigma = 1.0 / (1.0 + jnp.exp(-gate))
    silu = gate * sigma
    activation = silu * up
    grad_act = own_gate * pulled
    act = (RESIDUAL_SCALE * own_gate * activation).astype(BF)
    act_ref[...] = act
    gb_ref[:, :part] = (grad_act * up * sigma * (1.0 + gate * (1.0 - sigma))).astype(BF)
    gb_ref[:, part:] = (grad_act * silu).astype(BF)
    grad_combine = jnp.sum(activation * pulled, axis=1, keepdims=True)
    coef = (grad_combine * own_gate * (mark - combine)).astype(BF)
    terms = (
        (0, 2 * part, mixed, gb_ref[...]),
        (2 * part, 2 * part + 128, mixed, coef),
        (2 * part + 128, 3 * part + 128, grad_top, act),
    )

    @pl.when(step == 0)
    def _():
        for low, high, left, right in terms:
            acc[:, low:high] = dot(left, right, 0, 0)

    @pl.when(step > 0)
    def _():
        for low, high, left, right in terms:
            acc[:, low:high] += dot(left, right, 0, 0)

    grad_mixed = dot(gb_ref[...], wgu_ref[...], 1, 1) + dot(coef, wr_ref[...], 1, 1)
    scaled = scr[...] * factor
    norm_ref[...] += jnp.broadcast_to(
        jnp.sum(grad_mixed * scaled, axis=0, keepdims=True), norm_ref.shape
    )
    inner = grad_mixed * gain
    grad_mid = factor * (inner - scaled * jnp.mean(inner * scaled, axis=1, keepdims=True))
    grad_mid = grad_mid.astype(BF)
    v_ref[...] = grad_mid
    out_grads = dot(wo_rel[...], grad_mid, 1, 1)
    if part == F:
        top = out_grads[:HD] + dot(wo_rel[:HD, :], grad_top, 1, 1)
        pa_ref[:HD, :] = (RESIDUAL_SCALE * top).astype(BF)
        pa_ref[HD:, :] = (RESIDUAL_SCALE * out_grads[HD:half]).astype(BF)
    else:
        pa_ref[...] = (RESIDUAL_SCALE * out_grads[:half]).astype(BF)
    pb_ref[...] = (RESIDUAL_SCALE * out_grads[half:]).astype(BF)

    @pl.when(step == pl.num_programs(0) - 1)
    def _():
        middle = slice(2 * part, 2 * part + 128)
        last = acc[:, middle]
        grads_ref[:, : 2 * part] = acc[:, : 2 * part].astype(BF)
        grads_ref[:, middle] = jnp.where(lanes_of(last) == E, column_of(norm_ref), last).astype(BF)
        grads_ref[:, 2 * part + 128 :] = acc[:, 2 * part + 128 :].astype(BF)


def expert_main(att, hidden, top, wo, wgu, wd, wr, gain, heads, where, count):
    total = hidden.shape[0]
    part = wd.shape[1]
    tile = 2 * count
    width = 3 * part + 128

    def rows(size):
        return pl.BlockSpec((tile, size), lambda i, *_: (i, 0))

    def cols(height):
        return pl.BlockSpec((height, tile), lambda i, *_: (0, i))

    def out(size):
        return jax.ShapeDtypeStruct((total, size), BF)

    half = jax.ShapeDtypeStruct((D // 2, total), BF)
    return pl.pallas_call(
        functools.partial(back_kernel, part, count),
        out_shape=(
            out(part), out(D), half, half, jax.ShapeDtypeStruct((D, width), BF),
            jax.ShapeDtypeStruct((count, D), F32),
        ),
        grid_spec=pltpu.PrefetchScalarGridSpec(
            num_scalar_prefetch=2,
            grid=(total // tile,),
            in_specs=[
                pl.BlockSpec((H, HD, tile), lambda i, *_: (0, 0, i)),
                rows(D),
                pl.BlockSpec((2, count, D + 128), lambda i, *_: (i, 0, 0)),
                fixed(wo.shape), fixed((D, 2 * part)), fixed((D, part)), fixed((D, 128)),
                fixed((1, D)),
            ],
            out_specs=(
                rows(part), rows(D), cols(D // 2), cols(D // 2), fixed((D, width)),
                fixed((count, D)),
            ),
            scratch_shapes=[
                pltpu.VMEM((D, D), BF),
                pltpu.VMEM((tile, 2 * part), BF),
                pltpu.VMEM((8, D), F32),
                pltpu.VMEM((D, width), F32),
                pltpu.VMEM((tile, D), F32),
            ],
        ),
        compiler_params=params(),
        cost_estimate=cost(
            2 * total * D * (2 * D + 8 * part), 12 * total * D, total * part, weight=EXPERT_WEIGHT
        ),
        name="expert_main",
    )(heads, where, att, hidden, top, wo, wgu, wd, wr, gain)


def moe_kernel(act_ref, wd_ref, out_ref):
    out_ref[...] = dot(act_ref[...], wd_ref[...], 1, 1).astype(BF).reshape(out_ref.shape)


def moe_out(act, wd, count, rows):
    total, part = act.shape
    many = 4
    return pl.pallas_call(
        moe_kernel,
        out_shape=jax.ShapeDtypeStruct((total // count, count + 2 * rows, D), BF),
        grid=(total // count // many,),
        in_specs=[pl.BlockSpec((many * count, part), lambda i: (i, 0)), fixed((D, part))],
        out_specs=pl.BlockSpec((many, count, D), lambda i: (i, 0, 0)),
        compiler_params=params(),
        cost_estimate=cost(2 * total * D * part, 3 * total * D),
        name="moe_out",
    )(act, wd)


def output_kernel(where, att_ref, v_ref, g_ref, moe_ref, out_ref, acc):
    step = pl.program_id(0)
    tile = v_ref.shape[0]

    @pl.when(step == 0)
    def _():
        acc[...] = jnp.zeros_like(acc)

    acc[...] += dot(att_ref[...].reshape(D, tile), v_ref[...], 1, 0)
    picked = att_ref[where[0]]
    place = step * tile + lanes_of(picked)
    picked = jnp.where(place // where[3] == where[1], picked, jnp.zeros_like(picked))
    target = pl.ds(pl.multiple_of(where[0] * HD, HD), HD)
    acc[target, :] += dot(picked, g_ref[...].reshape(tile, D), 1, 0)

    @pl.when(step == pl.num_programs(0) - 1)
    def _():
        out_ref[...] = (RESIDUAL_SCALE * acc[...]).astype(BF).reshape(out_ref.shape)


def output_weights(att, grad_mid, top, moe, where, count, rows):
    total = grad_mid.shape[0]
    tile = 4 * count
    per = 2 * rows
    return pl.pallas_call(
        output_kernel,
        out_shape=jax.ShapeDtypeStruct(moe.shape, BF),
        grid_spec=pltpu.PrefetchScalarGridSpec(
            num_scalar_prefetch=1,
            grid=(total // tile,),
            in_specs=[
                pl.BlockSpec((H, HD, tile), lambda i, *_: (0, 0, i)),
                pl.BlockSpec((tile, D), lambda i, *_: (i, 0)),
                pl.BlockSpec((4, count, D), lambda i, *_: (i, 0, 0)),
                pl.BlockSpec(memory_space=pl.ANY),
            ],
            out_specs=fixed((moe.shape[0], per, D), (0, count // per, 0)),
            scratch_shapes=[pltpu.VMEM((D, D), F32)],
        ),
        input_output_aliases={4: 0},
        compiler_params=params(),
        cost_estimate=cost(2 * total * D * D, 8 * total * D),
        name="output_weights",
    )(where, att, grad_mid, top, moe)


def attend_kernel(
    block_len, band, ids, spots, firsts, where, all_ref, up_ref, log_ref, cos_ref, sin_ref,
    own_ref, up_sort, acc_qk, acc_v,
):
    total = all_ref.shape[0]
    blocks = QUERY_BLOCK // block_len
    window = band + QUERY_BLOCK
    acc_qk[...] = jnp.zeros_like(acc_qk)
    acc_v[...] = jnp.zeros_like(acc_v)
    for j in range(total // QUERY_BLOCK):
        piece = up_ref[:, j * QUERY_BLOCK : (j + 1) * QUERY_BLOCK]
        piece = jnp.concatenate([piece, jnp.zeros_like(piece)], 0).T.astype(BF)
        for m in range(blocks):
            spot = spot_of(ids, j * blocks + m, block_len)
            up_sort[spot, :] = piece[m * block_len : (m + 1) * block_len]

    def step_fn(index, carry):
        first_key, first_query = window_of(index, band)
        rows = pl.ds(first_query, QUERY_BLOCK)
        cols = pl.ds(first_key, window)
        keys_win, upstream = all_ref[cols, 128:256], up_sort[rows, :]
        scores = masked_scores(all_ref[rows, :128], keys_win, first_key, first_query, firsts)
        weight = jnp.exp(scores - log_ref[rows, :])
        grad_weight = dot(upstream, all_ref[cols, 384:], 1, 1)
        delta = jnp.sum(weight * grad_weight, axis=1, keepdims=True)
        grad_raw = (SCORE_SCALE * weight * (grad_weight - delta)).astype(BF)
        acc_qk[rows, :] += dot(grad_raw, keys_win, 1, 0)
        acc_qk[cols, :] += dot(grad_raw, all_ref[rows, 256:384], 0, 0)
        acc_v[cols, :] += dot(weight.astype(BF), upstream, 0, 0)
        return carry

    lax.fori_loop(0, total // QUERY_BLOCK, step_fn, 0)

    def turn(index, carry):
        first = pl.multiple_of(index * QUERY_BLOCK, QUERY_BLOCK)
        rows = pl.ds(first, QUERY_BLOCK)
        both = acc_qk[rows, :]
        low = lanes_of(both) % HD < HD // 2
        swapped = jnp.where(low, pltpu.roll(both, 96, 1), -pltpu.roll(both, 32, 1))
        turned = (both * cos_ref[rows, :] + swapped * sin_ref[rows, :]).astype(BF)
        made = jnp.concatenate([turned, acc_v[rows, :].astype(BF)], 1)
        for j in range(blocks):
            block = spots[index * blocks + j]
            first = pl.multiple_of(block * block_len, block_len)
            piece = made[j * block_len : (j + 1) * block_len]
            keep = first // where[3] == where[1]
            own_ref[pl.ds(first, block_len), :] = jnp.where(keep, piece, jnp.zeros_like(piece))
        return carry

    lax.fori_loop(0, total // QUERY_BLOCK, turn, 0, unroll=total // QUERY_BLOCK <= 8)


def attend_backward(heads_all, upstream, logs, tables, ids, spots, firsts, where, count, band):
    total = heads_all.shape[0]
    work = total * (band + QUERY_BLOCK)
    return pl.pallas_call(
        functools.partial(attend_kernel, count // 2, band),
        out_shape=jax.ShapeDtypeStruct((total, 256), BF),
        grid_spec=pltpu.PrefetchScalarGridSpec(
            num_scalar_prefetch=4,
            grid=(1,),
            in_specs=[
                fixed((total, 512)), fixed((HD, total)), fixed((total, 1)), fixed((total, 128)),
                fixed((total, 128)),
            ],
            out_specs=fixed((total, 256)),
            scratch_shapes=[
                pltpu.VMEM((total, 128), BF),
                pltpu.VMEM((total, 128), F32),
                pltpu.VMEM((total, 128), F32),
            ],
        ),
        compiler_params=params(60),
        cost_estimate=cost(10 * work * 128, 2 * total * 1024, work),
        name="attend_backward",
    )(ids, spots, firsts, where, heads_all, upstream, logs, *tables)


def pull_kernel(
    last, order, every, g_ref, h_ref, w_ref, gain_ref, x_ref, y_ref, gm_ref, hm_ref, w_in_ref, n_in_ref,
    out_ref, w_out_ref, n_out_ref, acc_w,
):
    step = pl.program_id(0)

    @pl.when(step == 0)
    def _():
        acc_w[...] = w_in_ref[...]
        n_out_ref[...] = n_in_ref[...]

    grads = jnp.concatenate([g_ref[...], h_ref[...]], 0)
    grad_mid = jnp.concatenate([gm_ref[...], hm_ref[...]], 0).astype(F32)
    grad_normed = dot(grads, w_ref[...], 1, 1)
    x_f = jnp.concatenate([x_ref[...], y_ref[...]], 0).astype(F32)
    factor = lax.rsqrt(jnp.mean(x_f * x_f, axis=1, keepdims=True) + EPSILON)
    scaled = x_f * factor
    normed = (scaled * gain_ref[...]).astype(BF)
    acc_w[...] += dot(normed, grads, 0, 0)
    n_out_ref[...] += jnp.broadcast_to(
        jnp.sum(grad_normed * scaled, axis=0, keepdims=True), n_out_ref.shape
    )
    inner = grad_normed * gain_ref[...]
    grad_x = factor * (inner - scaled * jnp.mean(inner * scaled, axis=1, keepdims=True))
    out_ref[...] = (grad_x + grad_mid).astype(BF)

    @pl.when(step == pl.num_programs(0) - 1)
    def _():
        if last:
            tail = acc_w[:, 128:]
            acc_w[:, 128:] = jnp.where(lanes_of(tail) == HD, column_of(n_out_ref), tail)
            places = every.shape[0]
            size = acc_w.shape[0] // places
            for j in range(places):
                first = pl.multiple_of(every[j] * size, size)
                w_out_ref[j * size : (j + 1) * size, :] = acc_w[pl.ds(first, size), :].astype(BF)
        else:
            w_out_ref[...] = acc_w[...]


def pull_heads(
    own_grads, w_head, gain, hidden, grad_mid, w_in, n_in, order, every, count, last
):
    total = hidden.shape[0] // 2

    def at(width, j):
        return pl.BlockSpec((count, width), lambda i, order, _: (order[2 * i + j], 0))

    block = pl.BlockSpec((2 * count, D), lambda i, *_: (i, 0))
    return pl.pallas_call(
        functools.partial(pull_kernel, last),
        out_shape=(
            jax.ShapeDtypeStruct((total, D), BF),
            jax.ShapeDtypeStruct((D, 256), BF if last else F32),
            jax.ShapeDtypeStruct((8, D), F32),
        ),
        grid_spec=pltpu.PrefetchScalarGridSpec(
            num_scalar_prefetch=2,
            grid=(total // count // 2,),
            in_specs=[
                at(256, 0), at(256, 1), fixed((D, 256)), fixed((1, D)), at(D, 0), at(D, 1), at(D, 0),
                at(D, 1),
                fixed((D, 256)), fixed((8, D)),
            ],
            out_specs=(block, fixed((D, 256)), fixed((8, D))),
            scratch_shapes=[pltpu.VMEM((D, 256), F32)],
        ),
        compiler_params=params(),
        cost_estimate=cost(4 * total * D * 256, 6 * total * D, weight=1),
        name="pull_last" if last else "pull_first",
    )(
        order, every, own_grads, own_grads, w_head, gain, hidden, hidden, grad_mid, grad_mid, w_in, n_in
    )


def finish_kernel(places, *refs):
    q_ref, k_ref, v_ref, gain_ref, scr = refs[4:]
    for j in range(16):
        scr[places[j]] = refs[j // 4][j % 4].astype(F32)
    total = jnp.zeros_like(scr[0])
    for quad in range(H // 4):
        heads = [scr[4 * quad + j] for j in range(4)]
        for j in range(2):
            first = (4 * quad + 2 * j) * HD
            q_ref[:, first : first + 128] = jnp.concatenate(
                [heads[2 * j][:, :HD], heads[2 * j + 1][:, :HD]], 1
            )
        pairs = [heads[0] + heads[1], heads[2] + heads[3]]
        total = total + pairs[0] + pairs[1]
        for ref, low in ((k_ref, HD), (v_ref, 2 * HD)):
            ref[:, quad * 128 : (quad + 1) * 128] = jnp.concatenate(
                [pair[:, low : low + HD] for pair in pairs], 1
            )
    gain_ref[...] = total[:, 128:]


def finish_heads(places, pieces):
    rows = pieces[0].shape[1]
    shapes = ((rows, D), (rows, D // 2), (rows, D // 2), (rows, 128))
    return pl.pallas_call(
        finish_kernel,
        out_shape=tuple(jax.ShapeDtypeStruct(shape, F32) for shape in shapes),
        grid_spec=pltpu.PrefetchScalarGridSpec(
            num_scalar_prefetch=1,
            grid=(1,),
            in_specs=[fixed(piece.shape) for piece in pieces],
            out_specs=tuple(fixed(shape) for shape in shapes),
            scratch_shapes=[pltpu.VMEM((16, rows, 256), F32)],
        ),
        compiler_params=params(),
        cost_estimate=cost(1, 2**20),
        name="finish_heads",
    )(places, *pieces)


def finish_kernel_experts(in_ref, up_ref, down_ref, tail_ref):
    many = in_ref.shape[0]
    wide, narrow = up_ref.shape[1] // many, down_ref.shape[1] // many
    for j in range(many):
        up_ref[:, j * wide : (j + 1) * wide] = in_ref[j, :, :wide].astype(F32)
        down_ref[:, j * narrow : (j + 1) * narrow] = in_ref[j, :, wide + 128 :].astype(F32)

    @pl.when(pl.program_id(0) == 0)
    def _():
        tail_ref[...] = jnp.zeros_like(tail_ref)

    for j in range(many):
        tail_ref[...] += in_ref[j, :, wide : wide + 128].astype(F32)


def finish_experts(arrived):
    places, rows, width = arrived.shape
    part = (width - 128) // 3
    return pl.pallas_call(
        finish_kernel_experts,
        out_shape=(
            jax.ShapeDtypeStruct((rows, places * 2 * part), F32),
            jax.ShapeDtypeStruct((rows, places * part), F32),
            jax.ShapeDtypeStruct((rows, 128), F32),
        ),
        grid=(places // 4,),
        in_specs=[pl.BlockSpec((4, rows, width), lambda i: (i, 0, 0))],
        out_specs=(
            pl.BlockSpec((rows, 8 * part), lambda i: (0, i)),
            pl.BlockSpec((rows, 4 * part), lambda i: (0, i)),
            fixed((rows, 128)),
        ),
        compiler_params=params(),
        cost_estimate=cost(1, 5 * 2**20),
        name="finish_experts",
    )(arrived)


def per_device(
    hidden_in,
    out_grad,
    doc_lengths,
    block_order,
    routes,
    attn_norm,
    w_query,
    w_key,
    w_value,
    w_output,
    ffn_norm,
    w_router,
    w_gate_up,
    w_down,
):
    ctx_count = lax.axis_size("ctx")
    ctx_place = lax.axis_index("ctx")
    fsdp_place = lax.axis_index("fsdp")
    copies = ctx_count // E
    own_expert, own_copy = ctx_place // copies, ctx_place % copies
    tok_count = hidden_in.shape[1]
    seq_len = tok_count * ctx_count
    block_len = tok_count // 2
    band = seq_len // 4
    rows = attn_norm.shape[0]
    part = F // copies
    groups = H // KVH
    share = seq_len // copies
    swap_y = [(0, 1), (1, 0)]
    alone = copies == 1

    def swap_fsdp(mine):
        return lax.ppermute(mine, "fsdp", swap_y)

    def both_rows(mine):
        theirs = swap_fsdp(mine)
        stacked = jnp.where(
            fsdp_place == 0, jnp.stack([mine, theirs], 1), jnp.stack([theirs, mine], 1)
        )
        return stacked.reshape(-1, mine.shape[-1])

    def exchange(split):
        return lax.all_to_all(split, "ctx", 0, 0, tiled=True)

    ids = block_order[0]
    block_ids = jnp.arange(ids.shape[0], dtype=jnp.int32)
    spots = jnp.sum(jnp.where(ids[None, :] == block_ids[:, None], block_ids[None, :], 0), axis=1)
    lengths = doc_lengths[0]
    doc_ids = jnp.arange(lengths.shape[0], dtype=jnp.int32)
    firsts = jnp.sum(
        jnp.where(doc_ids[None, :] < doc_ids[:, None], lengths[None, :], 0), axis=1
    )
    tables = tables_of(seq_len)
    order, heads = block_order_of(ctx_count), block_order_of(E)
    where = jnp.stack([own_expert, own_copy, ctx_place, jnp.int32(share)]).astype(jnp.int32)

    def by_expert(weight, pieces):
        split = weight.reshape(rows, E, pieces, copies, part)
        return split.transpose(1, 3, 0, 2, 4).reshape(ctx_count, rows, pieces * part)

    chosen_mask = jnp.any(
        routes[0][:, :, None] == jnp.arange(E, dtype=jnp.int32)[None, None, :], axis=1
    ).astype(BF)
    grads_own = jnp.concatenate(
        [out_grad[0], chosen_mask, jnp.zeros((tok_count, 128 - E), BF)], axis=1
    )
    experts = jnp.concatenate([by_expert(w_gate_up, 2), by_expert(w_down, 1)], axis=2)
    norms = jnp.stack([attn_norm, ffn_norm], 1)
    if alone:
        small_here = exchange(pack_small(copies, w_query, w_key, w_value, w_router, norms))
        w_ext, w_head, router_full, gain_one, gain_two = split_small(both_rows(small_here))
        near = Gather(hidden_in[0])
        near.cross()
        near.last(small_here)
        experts_here = exchange(after(experts, near.two))
        hidden_all = near.join(order, "join_hidden", w_ext).reshape(seq_len, D)
    else:
        small_here = exchange(pack_small(copies, w_query, w_key, w_value, w_router, norms))
        w_ext, w_head, router_full, gain_one, gain_two = split_small(both_rows(small_here))
        hidden_all = lax.all_gather(hidden_in[0], "ctx", axis=0, tiled=True)
        experts_here = exchange(experts)
    out_all = lax.all_gather(w_output, BOTH, axis=0, tiled=True).reshape(ctx_count, 2 * rows, D)
    top_all = lax.all_gather(grads_own[None], "ctx", axis=0, tiled=True)

    heads_all, logs, attended = head_forward(
        hidden_all, w_ext, gain_one, tables, ids, spots, firsts, tok_count, band
    )
    def half_rows(mine, theirs):
        stacked = jnp.where(
            fsdp_place == 0, jnp.stack([mine, theirs], 1), jnp.stack([theirs, mine], 1)
        )
        return stacked.reshape(D, mine.shape[-1])

    if alone:
        att = Gather(attended)
        experts_here = after(experts_here, att.one, att.three)
    gu_here, dn_here = experts_here[:, :, : 2 * part], experts_here[:, :, 2 * part :]
    gu_there, dn_there = swap_fsdp(gu_here), swap_fsdp(dn_here)
    w_gu, w_dn = half_rows(gu_here, gu_there), half_rows(dn_here, dn_there)
    if alone:
        att.cross()
        att.last(experts_here)
        att_all = att.join(heads, "join_heads", w_gu)
    else:
        sent = lax.dynamic_slice_in_dim(attended, own_copy * share, share, 1)
        att_all = lax.all_gather(sent, "ctx", axis=0, tiled=True)
        att_all = att_all.reshape(H, copies, HD, share).transpose(0, 2, 1, 3)
        att_all = att_all.reshape(H, HD, seq_len)

    act, grad_mid, pull_a, pull_b, grads_expert, middle = expert_main(
        att_all, hidden_all, top_all, out_all, w_gu, w_dn, router_full, gain_two, heads, where,
        tok_count,
    )

    def given_rows(grads):
        by_owner = grads.reshape(ctx_count, 2, rows, grads.shape[1])
        return by_owner, lax.dynamic_index_in_dim(by_owner, 1 - fsdp_place, 1, keepdims=False)

    def to_owner(by_owner, theirs):
        kept = lax.dynamic_index_in_dim(by_owner, fsdp_place, 1, keepdims=False)
        return (kept.astype(F32) + theirs.astype(F32)).astype(BF)

    owner, given = given_rows(grads_expert)
    theirs = swap_fsdp(given)
    mid_late = grad_mid
    if alone:
        ring = RingSum(pull_a, permute(pull_b, SWAP_CORE))
        mid_late = after(grad_mid, ring.cross_out)
    moe = moe_out(act, w_dn, tok_count, rows)
    out_both = output_weights(
        att_all, mid_late, top_all, moe, where, tok_count, rows
    )
    if alone:
        ring.cross()
        out_both = after(out_both, *ring.sends)
    if alone:
        upstream = ring.end(theirs)
    else:
        joined = jnp.concatenate([pull_a, pull_b], 0)
        pulled = lax.psum_scatter(joined, "ctx", scatter_dimension=0, tiled=True)
        rings = [[i * copies + j for j in range(copies)] for i in range(E)]
        pulled = lax.all_gather(pulled, "ctx", axis=0, tiled=True, axis_index_groups=rings)
        own_out = lax.dynamic_slice_in_dim(out_all.reshape(D, D), own_expert * HD, HD, 0)
        top_rows = top_all[:, :, :D].reshape(seq_len, D)
        upstream = pulled.astype(F32) + RESIDUAL_SCALE * dot(own_out, top_rows, 1, 1)
    if alone:
        theirs = after(theirs, upstream)
    grads_all_expert = to_owner(owner, theirs)

    own_grads = attend_backward(
        heads_all, upstream, logs, tables, ids, spots, firsts, where, tok_count, band
    )
    experts_in = exchange(grads_all_expert)
    grad_b, head_sum, norm_head = pull_heads(
        own_grads, w_head, gain_one, hidden_all, grad_mid, jnp.zeros((D, 256), F32),
        jnp.zeros((8, D), F32), order[ctx_count // 2 :], order, tok_count, False,
    )
    grad_a, grad_heads, ignored = pull_heads(
        own_grads, w_head, gain_one, hidden_all, grad_mid, head_sum, norm_head,
        order[: ctx_count // 2], order, tok_count, True,
    )
    if alone:
        by_owner = grad_heads.reshape(ctx_count, 2, rows, 256)
        kept = lax.dynamic_index_in_dim(by_owner, fsdp_place, 1, keepdims=False)
        given = lax.dynamic_index_in_dim(by_owner, 1 - fsdp_place, 1, keepdims=False)
        theirs = swap_fsdp(given)
        ring = RingSum(grad_a, permute(grad_b, SWAP_CORE))
        ring.cross()
        theirs = after(theirs, *ring.sends)
        tail_sum = (kept.astype(F32) + theirs.astype(F32)).astype(BF)
        experts_in = after(experts_in, *ring.sends)
    else:
        joined = jnp.concatenate([grad_a, grad_b], 0)
        grad_own = lax.psum_scatter(joined, "ctx", scatter_dimension=0, tiled=True).astype(F32)
    def from_experts(block, pieces):
        block = block[:, :, : pieces * part].astype(F32)
        block = block.reshape(E, copies, rows, pieces, part).transpose(2, 0, 3, 1, 4)
        return block.reshape(rows, E * pieces * F)

    if alone:
        share_gate_up, share_down, tail = finish_experts(experts_in)
    else:
        gu_in = experts_in[:, :, : 2 * part + 128]
        dn_in = experts_in[:, :, 2 * part + 128 :]
        share_gate_up = from_experts(gu_in, 2)
        share_down = from_experts(dn_in, 1)
        tail = jnp.sum(gu_in[:, :, 2 * part :].astype(F32), axis=0)
    share_router = tail[:, :E]
    share_gain_two = tail[:, E]
    out_own = lax.psum_scatter(out_both, "ctx", scatter_dimension=0, tiled=False).astype(F32)
    hidden_out = (middle + out_own[:tok_count]).astype(BF)
    out_rows = out_own[tok_count:].reshape(2, rows, D)
    mine = lax.dynamic_index_in_dim(out_rows, fsdp_place, 0, keepdims=False)
    theirs = lax.dynamic_index_in_dim(out_rows, 1 - fsdp_place, 0, keepdims=False)
    share_output = mine + swap_fsdp(theirs)

    if alone:
        grad_own = ring.end(share_output, hidden_out, share_gate_up)
    grad_in = out_grad[0].astype(F32) + grad_own
    if alone:
        pieces = spread_ctx(tail_sum)
        share_query, share_key, share_value, gain_sum = finish_heads(sender_order_of(), pieces)
        share_gain_one = gain_sum[:, HD]
    else:
        tail_in = lax.all_to_all(
            grad_heads.reshape(2 * ctx_count, rows, 256), BOTH, 0, 0, tiled=True
        )
        tail_in = tail_in.astype(F32).reshape(H, copies * 2, rows, 256)
        heads_in = jnp.sum(tail_in[..., : 3 * HD], axis=1)
        share_query = heads_in[:, :, :HD].transpose(1, 0, 2).reshape(rows, H * HD)
        pairs_in = heads_in[:, :, HD:].reshape(KVH, groups, rows, 2, HD).sum(1)
        share_key = pairs_in[:, :, 0].transpose(1, 0, 2).reshape(rows, KVH * HD)
        share_value = pairs_in[:, :, 1].transpose(1, 0, 2).reshape(rows, KVH * HD)
        share_gain_one = jnp.sum(tail_in[..., 3 * HD], axis=(0, 1))
    return (
        hidden_out[None],
        grad_in[None],
        share_gain_one,
        share_query,
        share_key,
        share_value,
        share_output,
        share_gain_two,
        share_router,
        share_gate_up,
        share_down,
    )


def solution(mesh):
    return jax.shard_map(
        per_device,
        mesh=mesh,
        in_specs=(
            P("fsdp", "ctx", None),
            P("fsdp", "ctx", None),
            P("fsdp", None),
            P("fsdp", None),
            P("fsdp", "ctx", None),
            P(BOTH),
            P(BOTH, None),
            P(BOTH, None),
            P(BOTH, None),
            P(BOTH, None),
            P(BOTH),
            P(BOTH, None),
            P(BOTH, None),
            P(BOTH, None),
        ),
        out_specs=(
            P("fsdp", "ctx", None),
            P("fsdp", "ctx", None),
            P(BOTH),
            P(BOTH, None),
            P(BOTH, None),
            P(BOTH, None),
            P(BOTH, None),
            P(BOTH),
            P(BOTH, None),
            P(BOTH, None),
            P(BOTH, None),
        ),
        check_vma=False,
    )
```
